128 devices in a mesh: rep: 16 (over y, z), tp: 8 (over x, core).
Axes of the slice: x: 4, y: 4, z: 4, core: 2. Of those that a mesh axis runs over, the one named last changes fastest.
Arguments:
- grads: bfloat16 [16, 12, 768, 2048], P('rep', None, None, 'tp'), may hold values from -6 to 6
- error: float32 [16, 12, 768, 2048], P('rep', None, None, 'tp'), may hold values from -2 to 2
- query: float32 [12, 32, 2048], P(None, None, 'tp'), may hold values from -6 to 6
- momentum: float32 [9216, 2048], P(('rep', 'tp')), may hold values from -0.8 to 0.8
- master: float32 [9216, 2048], P(('rep', 'tp')), may hold values from -0.8 to 0.8
Outputs:
- new_error: float32 [16, 12, 768, 2048], P('rep', None, None, 'tp')
- new_query: float32 [12, 32, 2048], P(None, None, 'tp')
- new_momentum: float32 [9216, 2048], P(('rep', 'tp'))
- new_master: float32 [9216, 2048], P(('rep', 'tp'))
- weights: bfloat16 [12, 768, 2048], P(None, None, 'tp')
The draws below stay inside these ranges and needn't reach their ends.
All inputs are finite; a program needn't handle non-finite values.
Results may differ from the reference program's by a relative error of at most 0.0004.
Values may be sent and summed in bfloat16 or wider, within the bound.
A program may use at most 128 MiB of HBM per device.

```python
import jax
import jax.numpy as jnp
from jax import lax

D = 768
FF = 2048
RANK = 32
ROUNDS = 2
NS_STEPS = 5
MATS = 12
REPLICAS = 16
N_REP = 16


def block_levels(rng, dims, shards, low, top_value):
    factor_of, own = 1.0, jax.random.fold_in(rng, 6)
    for dim, blocks in shards:
        heights = jnp.exp(jax.random.uniform(jax.random.fold_in(own, dim), (blocks,), jnp.float32, low / len(shards), top_value / len(shards)))
        factor_of = factor_of * jnp.repeat(heights, dims[dim] // blocks).reshape([-1 if axis == dim else 1 for axis in range(len(dims))])
    return factor_of


def noise(stream_key, shape, deviation, reach, pieces=(), dtype=jnp.bfloat16):
    values = deviation * jax.random.normal(stream_key, shape, jnp.float32)
    if pieces:
        values = values * block_levels(stream_key, shape, pieces, -0.22, 0.18)
    return jnp.clip(values, -reach, reach).astype(dtype)


def setup_inputs(seed: int = 0) -> dict:
    streams_of = jax.random.split(jax.random.key(seed), 6)
    return {
        "grads": noise(streams_of[0], (REPLICAS, MATS, D, FF), 1.0, 6.0, ((0, 16), (3, 8))),
        "error": noise(streams_of[1], (REPLICAS, MATS, D, FF), 0.3, 2.0, ((0, 16), (3, 8)), jnp.float32),
        "query": noise(streams_of[2], (MATS, RANK, FF), 1.0, 6.0, ((2, 8),), jnp.float32),
        "momentum": noise(streams_of[3], (MATS * D, FF), 0.2, 0.8, ((0, 128),), jnp.float32),
        "master": noise(streams_of[4], (MATS * D, FF), 0.2, 0.8, ((0, 128),), jnp.float32),
    }


NORM_EPSILON = 1e-06
MOMENTUM_DECAY = 0.9
LEARNING_RATE = 0.5

def gram_matrix(factor):
    return jnp.einsum('krd,ksd->krs', factor, factor, precision=lax.Precision.HIGHEST)

def orthonormal(factor):
    gram_now = gram_matrix(factor)
    sum_squares = jnp.trace(gram_now, axis1=1, axis2=2)[:, None, None]
    factor_scale = lax.rsqrt(sum_squares + NORM_EPSILON)
    ortho_basis = factor * factor_scale
    gram_now = gram_now * (factor_scale * factor_scale)
    for iteration in range(NS_STEPS):
        if iteration > 0:
            gram_now = gram_matrix(ortho_basis)
        ortho_basis = 1.5 * ortho_basis - 0.5 * jnp.einsum('krs,ksd->krd', gram_now, ortho_basis, precision=lax.Precision.HIGHEST)
    return ortho_basis

def reference(grads, error, query, momentum, master):
    corrected = grads.astype(jnp.float32) + error
    current = query
    for power_pass in range(ROUNDS):
        summed = jnp.einsum('nkdf,krf->krd', corrected, current, precision=lax.Precision.HIGHEST)
        ortho_basis = orthonormal(summed)
        current = jnp.einsum('nkdf,krd->krf', corrected, ortho_basis, precision=lax.Precision.HIGHEST) / N_REP
    approx = jnp.einsum('krd,krf->kdf', ortho_basis, current, precision=lax.Precision.HIGHEST)
    new_error = corrected - approx[None]
    flat_approx = approx.reshape(MATS * D, FF)
    new_momentum = MOMENTUM_DECAY * momentum + flat_approx
    new_master = master - LEARNING_RATE * new_momentum
    weights = new_master.astype(jnp.bfloat16).reshape(MATS, D, FF)
    return (new_error, current, new_momentum, new_master, weights)
```

```python
import functools

import jax
import jax.numpy as jnp
from jax import lax
from jax.experimental import pallas as pl
from jax.experimental.pallas import tpu as pltpu
from jax.sharding import PartitionSpec as P

ROUNDS = 2
NS_STEPS = 5


NORM_EPSILON = 1e-06
MOMENTUM_DECAY = 0.9
LEARNING_RATE = 0.5

MESH_AXES = ("rep", "tp")
LANES = 128


def _peer(name, index):
    return tuple(index if axis == name else lax.axis_index(axis) for axis in MESH_AXES)


def _allreduce_kernel(levels, x_ref, o_ref, *scratch):
    n_lev = len(levels)
    it = iter(scratch)
    recv = [next(it) for _ in range(n_lev)]
    sums = [next(it) for _ in range(n_lev - 1)]
    gath = [next(it) for _ in range(n_lev - 1)] + [None]
    rs_send = [next(it) for _ in range(n_lev)]
    rs_recv = [next(it) for _ in range(n_lev)]
    ag_send = [next(it) for _ in range(n_lev)]
    ag_recv = [next(it) for _ in range(n_lev)]
    local_sem = next(it)

    me = [lax.axis_index(name) for name, _ in levels]

    barrier = pltpu.get_barrier_semaphore()
    total_peers = 0
    for lev, (name, n) in enumerate(levels):
        for off in range(1, n):
            j = lax.rem(me[lev] + off, n)
            pl.semaphore_signal(barrier, inc=1, device_id=_peer(name, j),
                                device_id_type=pl.DeviceIdType.MESH)
        total_peers += n - 1
    pl.semaphore_wait(barrier, total_peers)

    gath_bufs = [o_ref] + gath[: n_lev - 1]

    src = x_ref
    for lev, (name, n) in enumerate(levels):
        m = me[lev]
        copies = []
        for off in range(1, n):
            j = lax.rem(m + off, n)
            cp = pltpu.make_async_remote_copy(
                src_ref=src.at[j], dst_ref=recv[lev].at[m],
                send_sem=rs_send[lev].at[off], recv_sem=rs_recv[lev].at[m],
                device_id=_peer(name, j), device_id_type=pl.DeviceIdType.MESH)
            cp.start()
            copies.append((j, off, cp))
        own = pltpu.make_async_copy(src.at[m], recv[lev].at[m], local_sem.at[0])
        own.start()
        own.wait()
        for j, off, cp in copies:
            pltpu.make_async_remote_copy(
                src_ref=src.at[j], dst_ref=recv[lev].at[j],
                send_sem=rs_send[lev].at[off], recv_sem=rs_recv[lev].at[j],
                device_id=_peer(name, j), device_id_type=pl.DeviceIdType.MESH).wait_recv()
        for j, off, cp in copies:
            cp.wait_send()
        r = recv[lev]
        if lev < n_lev - 1:
            dst = sums[lev]
        else:
            dst = gath_bufs[lev].at[m]
        if len(r.shape) > 3:
            def body(i, carry, r=r, dst=dst, n=n):
                acc = r[0, i]
                for j in range(1, n):
                    acc = acc + r[j, i]
                dst[i] = acc
                return carry
            lax.fori_loop(0, r.shape[1], body, 0)
        else:
            acc = r[0]
            for j in range(1, n):
                acc = acc + r[j]
            dst[...] = acc
        if lev < n_lev - 1:
            src = sums[lev]

    for lev in reversed(range(n_lev)):
        name, n = levels[lev]
        m = me[lev]
        buf = gath_bufs[lev]
        if lev == n_lev - 1:
            piece = buf.at[m]
        else:
            piece = gath_bufs[lev + 1]
            own = pltpu.make_async_copy(piece, buf.at[m], local_sem.at[0])
            own.start()
            own.wait()
        copies = []
        for off in range(1, n):
            j = lax.rem(m + off, n)
            cp = pltpu.make_async_remote_copy(
                src_ref=piece, dst_ref=buf.at[m],
                send_sem=ag_send[lev].at[off], recv_sem=ag_recv[lev].at[m],
                device_id=_peer(name, j), device_id_type=pl.DeviceIdType.MESH)
            cp.start()
            copies.append((j, off, cp))
        for j, off, cp in copies:
            pltpu.make_async_remote_copy(
                src_ref=piece, dst_ref=buf.at[j],
                send_sem=ag_send[lev].at[off], recv_sem=ag_recv[lev].at[j],
                device_id=_peer(name, j), device_id_type=pl.DeviceIdType.MESH).wait_recv()
        for j, off, cp in copies:
            cp.wait_send()


def allreduce(x, levels, collective_id):
    shape = x.shape
    total = x.size
    counts = [n for _, n in levels]
    per = total
    for n in counts:
        per //= n
    rows = per // LANES
    full = tuple(counts) + (rows, LANES)
    xr = x.reshape(full)
    scratch = []
    for lev in range(len(levels)):
        scratch.append(pltpu.VMEM(full[lev:], jnp.float32))
    for lev in range(len(levels) - 1):
        scratch.append(pltpu.VMEM(full[lev + 1:], jnp.float32))
    for lev in range(len(levels) - 1):
        scratch.append(pltpu.VMEM(full[lev + 1:], jnp.float32))
    for _ in range(4):
        for _, n in levels:
            scratch.append(pltpu.SemaphoreType.DMA((n,)))
    scratch.append(pltpu.SemaphoreType.DMA((1,)))
    out = pl.pallas_call(
        functools.partial(_allreduce_kernel, tuple(levels)),
        out_shape=jax.ShapeDtypeStruct(full, jnp.float32),
        in_specs=[pl.BlockSpec(memory_space=pltpu.VMEM)],
        out_specs=pl.BlockSpec(memory_space=pltpu.VMEM),
        scratch_shapes=scratch,
        compiler_params=pltpu.CompilerParams(collective_id=collective_id, has_side_effects=True),
        cost_estimate=pl.CostEstimate(flops=total * 2, bytes_accessed=total * 4 * 4, transcendentals=0),
    )(xr)
    return out.reshape(shape)


def local_gram(factor):
    return jnp.einsum("krd,ksd->krs", factor, factor, precision=lax.Precision.HIGHEST)


def orthonormal(factor, gram_of):
    gram_now = gram_of(factor)
    sum_squares = jnp.trace(gram_now, axis1=1, axis2=2)[:, None, None]
    factor_scale = lax.rsqrt(sum_squares + NORM_EPSILON)
    ortho_basis = factor * factor_scale
    gram_now = gram_now * (factor_scale * factor_scale)
    for iteration in range(NS_STEPS):
        if iteration > 0:
            gram_now = gram_of(ortho_basis)
        ortho_basis = 1.5 * ortho_basis - 0.5 * jnp.einsum(
            "krs,ksd->krd", gram_now, ortho_basis, precision=lax.Precision.HIGHEST
        )
    return ortho_basis


def local(grads, error, query, momentum, master):
    corrected = grads[0].astype(jnp.float32) + error[0]
    current = query
    replicas = lax.axis_size("rep")
    both = (("tp", lax.axis_size("tp")), ("rep", replicas))
    rep_only = (("rep", replicas),)
    for power_pass in range(ROUNDS):
        partial_factor = jnp.einsum(
            "kdf,krf->krd", corrected, current, precision=lax.Precision.HIGHEST
        )
        summed = allreduce(partial_factor, both, 0)
        ortho_basis = orthonormal(summed, local_gram)
        partial_query = jnp.einsum(
            "kdf,krd->krf", corrected, ortho_basis, precision=lax.Precision.HIGHEST
        )
        current = allreduce(partial_query, rep_only, 1) / replicas
    approx = jnp.einsum("krd,krf->kdf", ortho_basis, current, precision=lax.Precision.HIGHEST)
    new_error = (corrected - approx)[None]
    matrices, model_width, shard_cols = approx.shape
    block_rows = matrices * model_width // replicas
    approx_rows = approx.reshape(matrices * model_width, shard_cols)
    own_block = lax.dynamic_slice_in_dim(
        approx_rows, lax.axis_index("rep") * block_rows, block_rows, 0
    )
    flat_approx = lax.all_to_all(own_block, "tp", split_axis=0, concat_axis=1, tiled=True)
    new_momentum = MOMENTUM_DECAY * momentum + flat_approx
    new_master = master - LEARNING_RATE * new_momentum
    working = new_master.astype(jnp.bfloat16)
    by_columns = lax.all_to_all(working, "tp", split_axis=1, concat_axis=0, tiled=True)
    weight_rows = lax.all_gather(by_columns, "rep", axis=0, tiled=True)
    weights = weight_rows.reshape(matrices, model_width, shard_cols)
    return (new_error, current, new_momentum, new_master, weights)


def solution(mesh):
    placed = (
        P("rep", None, None, "tp"),
        P("rep", None, None, "tp"),
        P(None, None, "tp"),
        P(("rep", "tp"), None),
        P(("rep", "tp"), None),
    )
    return jax.shard_map(
        local,
        mesh=mesh,
        in_specs=placed,
        out_specs=(
            P("rep", None, None, "tp"),
            P(None, None, "tp"),
            P(("rep", "tp"), None),
            P(("rep", "tp"), None),
            P(None, None, "tp"),
        ),
        check_vma=False,
    )
```

```python
import functools

import jax
import jax.numpy as jnp
from jax import lax
from jax.experimental import pallas as pl
from jax.experimental.pallas import tpu as pltpu
from jax.sharding import PartitionSpec as P

ROUNDS = 2
NS_STEPS = 5


NORM_EPSILON = 1e-06
MOMENTUM_DECAY = 0.9
LEARNING_RATE = 0.5

MESH_AXES = ("rep", "tp")
LANES = 128


def _coord(level):
    name, n, stride = level
    return lax.rem(lax.div(lax.axis_index(name), stride), n)


def _peer(level, j):
    name, n, stride = level
    base = lax.axis_index(name) + (j - _coord(level)) * stride
    return tuple(base if axis == name else lax.axis_index(axis) for axis in MESH_AXES)


def _allreduce_kernel(levels, x_ref, o_ref, *scratch):
    n_lev = len(levels)
    it = iter(scratch)
    recv = [next(it) for _ in range(n_lev)]
    sums = [next(it) for _ in range(n_lev - 1)]
    gath = [next(it) for _ in range(n_lev - 1)] + [None]
    rs_send = [next(it) for _ in range(n_lev)]
    rs_recv = [next(it) for _ in range(n_lev)]
    ag_send = [next(it) for _ in range(n_lev)]
    ag_recv = [next(it) for _ in range(n_lev)]
    local_sem = next(it)

    me = [_coord(level) for level in levels]

    barrier = pltpu.get_barrier_semaphore()
    total_peers = 0
    for lev, (name, n, _) in enumerate(levels):
        for off in range(1, n):
            j = lax.rem(me[lev] + off, n)
            pl.semaphore_signal(barrier, inc=1, device_id=_peer(levels[lev], j),
                                device_id_type=pl.DeviceIdType.MESH)
        total_peers += n - 1
    pl.semaphore_wait(barrier, total_peers)

    gath_bufs = [o_ref] + gath[: n_lev - 1]

    src = x_ref
    for lev, (name, n, _) in enumerate(levels):
        m = me[lev]
        copies = []
        for off in range(1, n):
            j = lax.rem(m + off, n)
            cp = pltpu.make_async_remote_copy(
                src_ref=src.at[j], dst_ref=recv[lev].at[m],
                send_sem=rs_send[lev].at[off], recv_sem=rs_recv[lev].at[m],
                device_id=_peer(levels[lev], j), device_id_type=pl.DeviceIdType.MESH)
            cp.start()
            copies.append((j, off, cp))
        own = pltpu.make_async_copy(src.at[m], recv[lev].at[m], local_sem.at[0])
        own.start()
        own.wait()
        for j, off, cp in copies:
            pltpu.make_async_remote_copy(
                src_ref=src.at[j], dst_ref=recv[lev].at[j],
                send_sem=rs_send[lev].at[off], recv_sem=rs_recv[lev].at[j],
                device_id=_peer(levels[lev], j), device_id_type=pl.DeviceIdType.MESH).wait_recv()
        for j, off, cp in copies:
            cp.wait_send()
        r = recv[lev]
        if lev < n_lev - 1:
            dst = sums[lev]
        else:
            dst = gath_bufs[lev].at[m]
        if len(r.shape) > 3:
            lead = r.shape[1:-2]
            count = 1
            for d in lead:
                count *= d

            def body(i, carry, r=r, dst=dst, n=n, lead=lead):
                idx = []
                rest = i
                for d in reversed(lead):
                    idx.append(lax.rem(rest, d))
                    rest = lax.div(rest, d)
                idx = tuple(reversed(idx))
                acc = r[(0,) + idx]
                for j in range(1, n):
                    acc = acc + r[(j,) + idx]
                dst[idx] = acc
                return carry
            lax.fori_loop(0, count, body, 0)
        else:
            acc = r[0]
            for j in range(1, n):
                acc = acc + r[j]
            dst[...] = acc
        if lev < n_lev - 1:
            src = sums[lev]

    for lev in reversed(range(n_lev)):
        name, n, _ = levels[lev]
        m = me[lev]
        buf = gath_bufs[lev]
        if lev == n_lev - 1:
            piece = buf.at[m]
        else:
            piece = gath_bufs[lev + 1]
            own = pltpu.make_async_copy(piece, buf.at[m], local_sem.at[0])
            own.start()
            own.wait()
        copies = []
        for off in range(1, n):
            j = lax.rem(m + off, n)
            cp = pltpu.make_async_remote_copy(
                src_ref=piece, dst_ref=buf.at[m],
                send_sem=ag_send[lev].at[off], recv_sem=ag_recv[lev].at[m],
                device_id=_peer(levels[lev], j), device_id_type=pl.DeviceIdType.MESH)
            cp.start()
            copies.append((j, off, cp))
        for j, off, cp in copies:
            pltpu.make_async_remote_copy(
                src_ref=piece, dst_ref=buf.at[j],
                send_sem=ag_send[lev].at[off], recv_sem=ag_recv[lev].at[j],
                device_id=_peer(levels[lev], j), device_id_type=pl.DeviceIdType.MESH).wait_recv()
        for j, off, cp in copies:
            cp.wait_send()


def allreduce(x, levels, collective_id):
    shape = x.shape
    total = x.size
    counts = [n for _, n, _ in levels]
    per = total
    for n in counts:
        per //= n
    rows = per // LANES
    full = tuple(counts) + (rows, LANES)
    xr = x.reshape(full)
    scratch = []
    for lev in range(len(levels)):
        scratch.append(pltpu.VMEM(full[lev:], jnp.float32))
    for lev in range(len(levels) - 1):
        scratch.append(pltpu.VMEM(full[lev + 1:], jnp.float32))
    for lev in range(len(levels) - 1):
        scratch.append(pltpu.VMEM(full[lev + 1:], jnp.float32))
    for _ in range(4):
        for _, n, _ in levels:
            scratch.append(pltpu.SemaphoreType.DMA((n,)))
    scratch.append(pltpu.SemaphoreType.DMA((1,)))
    out = pl.pallas_call(
        functools.partial(_allreduce_kernel, tuple(levels)),
        out_shape=jax.ShapeDtypeStruct(full, jnp.float32),
        in_specs=[pl.BlockSpec(memory_space=pltpu.VMEM)],
        out_specs=pl.BlockSpec(memory_space=pltpu.VMEM),
        scratch_shapes=scratch,
        compiler_params=pltpu.CompilerParams(collective_id=collective_id, has_side_effects=True),
        cost_estimate=pl.CostEstimate(flops=total * 2, bytes_accessed=total * 4 * 4, transcendentals=0),
    )(xr)
    return out.reshape(shape)


def split_levels(name, size, inner):
    if size % inner or size == inner:
        return ((name, size, 1),)
    if inner == 2:
        return ((name, inner, 1), (name, size // inner, inner))
    return ((name, size // inner, inner), (name, inner, 1))


def local_gram(factor):
    return jnp.einsum("krd,ksd->krs", factor, factor, precision=lax.Precision.HIGHEST)


def orthonormal(factor, gram_of):
    gram_now = gram_of(factor)
    sum_squares = jnp.trace(gram_now, axis1=1, axis2=2)[:, None, None]
    factor_scale = lax.rsqrt(sum_squares + NORM_EPSILON)
    ortho_basis = factor * factor_scale
    gram_now = gram_now * (factor_scale * factor_scale)
    for iteration in range(NS_STEPS):
        if iteration > 0:
            gram_now = gram_of(ortho_basis)
        ortho_basis = 1.5 * ortho_basis - 0.5 * jnp.einsum(
            "krs,ksd->krd", gram_now, ortho_basis, precision=lax.Precision.HIGHEST
        )
    return ortho_basis


def local(grads, error, query, momentum, master):
    corrected = grads[0].astype(jnp.float32) + error[0]
    current = query
    replicas = lax.axis_size("rep")
    rep_only = split_levels("rep", replicas, 4)
    both = split_levels("tp", lax.axis_size("tp"), 2) + rep_only
    for power_pass in range(ROUNDS):
        partial_factor = jnp.einsum(
            "kdf,krf->krd", corrected, current, precision=lax.Precision.HIGHEST
        )
        summed = allreduce(partial_factor, both, 0)
        ortho_basis = orthonormal(summed, local_gram)
        partial_query = jnp.einsum(
            "kdf,krd->krf", corrected, ortho_basis, precision=lax.Precision.HIGHEST
        )
        current = allreduce(partial_query, rep_only, 1) / replicas
    approx = jnp.einsum("krd,krf->kdf", ortho_basis, current, precision=lax.Precision.HIGHEST)
    new_error = (corrected - approx)[None]
    matrices, model_width, shard_cols = approx.shape
    block_rows = matrices * model_width // replicas
    approx_rows = approx.reshape(matrices * model_width, shard_cols)
    own_block = lax.dynamic_slice_in_dim(
        approx_rows, lax.axis_index("rep") * block_rows, block_rows, 0
    )
    flat_approx = lax.all_to_all(own_block, "tp", split_axis=0, concat_axis=1, tiled=True)
    new_momentum = MOMENTUM_DECAY * momentum + flat_approx
    new_master = master - LEARNING_RATE * new_momentum
    working = new_master.astype(jnp.bfloat16)
    by_columns = lax.all_to_all(working, "tp", split_axis=1, concat_axis=0, tiled=True)
    weight_rows = lax.all_gather(by_columns, "rep", axis=0, tiled=True)
    weights = weight_rows.reshape(matrices, model_width, shard_cols)
    return (new_error, current, new_momentum, new_master, weights)


def solution(mesh):
    placed = (
        P("rep", None, None, "tp"),
        P("rep", None, None, "tp"),
        P(None, None, "tp"),
        P(("rep", "tp"), None),
        P(("rep", "tp"), None),
    )
    return jax.shard_map(
        local,
        mesh=mesh,
        in_specs=placed,
        out_specs=(
            P("rep", None, None, "tp"),
            P(None, None, "tp"),
            P(("rep", "tp"), None),
            P(("rep", "tp"), None),
            P(None, None, "tp"),
        ),
        check_vma=False,
    )
```

```python
import functools

import jax
import jax.numpy as jnp
from jax import lax
from jax.experimental import pallas as pl
from jax.experimental.pallas import tpu as pltpu
from jax.sharding import PartitionSpec as P

ROUNDS = 2
NS_STEPS = 5


NORM_EPSILON = 1e-06
MOMENTUM_DECAY = 0.9
LEARNING_RATE = 0.5

MESH_AXES = ("rep", "tp")
LANES = 128


def _coord(level):
    name, n, stride = level
    return lax.rem(lax.div(lax.axis_index(name), stride), n)


def _peer(level, j):
    name, n, stride = level
    base = lax.axis_index(name) + (j - _coord(level)) * stride
    return tuple(base if axis == name else lax.axis_index(axis) for axis in MESH_AXES)


def _allreduce_kernel(levels, x_ref, o_ref, *scratch):
    n_lev = len(levels)
    it = iter(scratch)
    recv = [next(it) for _ in range(n_lev)]
    sums = [next(it) for _ in range(n_lev - 1)]
    gath = [next(it) for _ in range(n_lev - 1)] + [None]
    rs_send = [next(it) for _ in range(n_lev)]
    rs_recv = [next(it) for _ in range(n_lev)]
    ag_send = [next(it) for _ in range(n_lev)]
    ag_recv = [next(it) for _ in range(n_lev)]
    local_sem = next(it)

    me = [_coord(level) for level in levels]

    barrier = pltpu.get_barrier_semaphore()
    total_peers = 0
    for lev, (name, n, _) in enumerate(levels):
        for off in range(1, n):
            j = lax.rem(me[lev] + off, n)
            pl.semaphore_signal(barrier, inc=1, device_id=_peer(levels[lev], j),
                                device_id_type=pl.DeviceIdType.MESH)
        total_peers += n - 1
    pl.semaphore_wait(barrier, total_peers)

    gath_bufs = [o_ref] + gath[: n_lev - 1]

    src = x_ref
    for lev, (name, n, _) in enumerate(levels):
        m = me[lev]
        copies = []
        for off in range(1, n):
            j = lax.rem(m + off, n)
            cp = pltpu.make_async_remote_copy(
                src_ref=src.at[j], dst_ref=recv[lev].at[m],
                send_sem=rs_send[lev].at[off], recv_sem=rs_recv[lev].at[m],
                device_id=_peer(levels[lev], j), device_id_type=pl.DeviceIdType.MESH)
            cp.start()
            copies.append((j, off, cp))
        own = pltpu.make_async_copy(src.at[m], recv[lev].at[m], local_sem.at[0])
        own.start()
        own.wait()
        for j, off, cp in copies:
            pltpu.make_async_remote_copy(
                src_ref=src.at[j], dst_ref=recv[lev].at[j],
                send_sem=rs_send[lev].at[off], recv_sem=rs_recv[lev].at[j],
                device_id=_peer(levels[lev], j), device_id_type=pl.DeviceIdType.MESH).wait_recv()
        for j, off, cp in copies:
            cp.wait_send()
        r = recv[lev]
        if lev < n_lev - 1:
            dst = sums[lev]
        else:
            dst = gath_bufs[lev].at[m]
        if len(r.shape) > 3:
            lead = r.shape[1:-2]
            count = 1
            for d in lead:
                count *= d

            def body(i, carry, r=r, dst=dst, n=n, lead=lead):
                idx = []
                rest = i
                for d in reversed(lead):
                    idx.append(lax.rem(rest, d))
                    rest = lax.div(rest, d)
                idx = tuple(reversed(idx))
                acc = r[(0,) + idx]
                for j in range(1, n):
                    acc = acc + r[(j,) + idx]
                dst[idx] = acc
                return carry
            lax.fori_loop(0, count, body, 0)
        else:
            acc = r[0]
            for j in range(1, n):
                acc = acc + r[j]
            dst[...] = acc
        if lev < n_lev - 1:
            src = sums[lev]

    for lev in reversed(range(n_lev)):
        name, n, _ = levels[lev]
        m = me[lev]
        buf = gath_bufs[lev]
        if lev == n_lev - 1:
            piece = buf.at[m]
        else:
            piece = gath_bufs[lev + 1]
            own = pltpu.make_async_copy(piece, buf.at[m], local_sem.at[0])
            own.start()
            own.wait()
        copies = []
        for off in range(1, n):
            j = lax.rem(m + off, n)
            cp = pltpu.make_async_remote_copy(
                src_ref=piece, dst_ref=buf.at[m],
                send_sem=ag_send[lev].at[off], recv_sem=ag_recv[lev].at[m],
                device_id=_peer(levels[lev], j), device_id_type=pl.DeviceIdType.MESH)
            cp.start()
            copies.append((j, off, cp))
        for j, off, cp in copies:
            pltpu.make_async_remote_copy(
                src_ref=piece, dst_ref=buf.at[j],
                send_sem=ag_send[lev].at[off], recv_sem=ag_recv[lev].at[j],
                device_id=_peer(levels[lev], j), device_id_type=pl.DeviceIdType.MESH).wait_recv()
        for j, off, cp in copies:
            cp.wait_send()


def allreduce(x, levels, collective_id):
    shape = x.shape
    total = x.size
    counts = [n for _, n, _ in levels]
    per = total
    for n in counts:
        per //= n
    rows = per // LANES
    full = tuple(counts) + (rows, LANES)
    xr = x.reshape(full)
    scratch = []
    for lev in range(len(levels)):
        scratch.append(pltpu.VMEM(full[lev:], jnp.float32))
    for lev in range(len(levels) - 1):
        scratch.append(pltpu.VMEM(full[lev + 1:], jnp.float32))
    for lev in range(len(levels) - 1):
        scratch.append(pltpu.VMEM(full[lev + 1:], jnp.float32))
    for _ in range(4):
        for _, n, _ in levels:
            scratch.append(pltpu.SemaphoreType.DMA((n,)))
    scratch.append(pltpu.SemaphoreType.DMA((1,)))
    out = pl.pallas_call(
        functools.partial(_allreduce_kernel, tuple(levels)),
        out_shape=jax.ShapeDtypeStruct(full, jnp.float32),
        in_specs=[pl.BlockSpec(memory_space=pltpu.VMEM)],
        out_specs=pl.BlockSpec(memory_space=pltpu.VMEM),
        scratch_shapes=scratch,
        compiler_params=pltpu.CompilerParams(collective_id=collective_id, has_side_effects=True),
        cost_estimate=pl.CostEstimate(flops=total * 2, bytes_accessed=total * 4 * 4, transcendentals=0),
    )(xr)
    return out.reshape(shape)


def split_levels(name, size, inner):
    if size % inner or size == inner:
        return ((name, size, 1),)
    if inner == 2:
        return ((name, inner, 1), (name, size // inner, inner))
    return ((name, size // inner, inner), (name, inner, 1))


def local_gram(factor):
    return jnp.einsum("krd,ksd->krs", factor, factor, precision=lax.Precision.HIGHEST)


def orthonormal(factor, gram_of):
    gram_now = gram_of(factor)
    sum_squares = jnp.trace(gram_now, axis1=1, axis2=2)[:, None, None]
    factor_scale = lax.rsqrt(sum_squares + NORM_EPSILON)
    ortho_basis = factor * factor_scale
    gram_now = gram_now * (factor_scale * factor_scale)
    for iteration in range(NS_STEPS):
        if iteration > 0:
            gram_now = gram_of(ortho_basis)
        ortho_basis = 1.5 * ortho_basis - 0.5 * jnp.einsum(
            "krs,ksd->krd", gram_now, ortho_basis, precision=lax.Precision.HIGHEST
        )
    return ortho_basis


def local(grads, error, query, momentum, master):
    corrected = grads[0].astype(jnp.float32) + error[0]
    current = query
    replicas = lax.axis_size("rep")
    rep_only = (("rep", replicas, 1),)
    both = split_levels("tp", lax.axis_size("tp"), 2) + split_levels("rep", replicas, 4)
    for power_pass in range(ROUNDS):
        partial_factor = jnp.einsum(
            "kdf,krf->krd", corrected, current, precision=lax.Precision.HIGHEST
        )
        summed = allreduce(partial_factor, both, 0)
        ortho_basis = orthonormal(summed, local_gram)
        partial_query = jnp.einsum(
            "kdf,krd->krf", corrected, ortho_basis, precision=lax.Precision.HIGHEST
        )
        current = allreduce(partial_query, rep_only, 1) / replicas
    approx = jnp.einsum("krd,krf->kdf", ortho_basis, current, precision=lax.Precision.HIGHEST)
    new_error = (corrected - approx)[None]
    matrices, model_width, shard_cols = approx.shape
    block_rows = matrices * model_width // replicas
    assert block_rows <= model_width and matrices >= 2
    first_row = lax.axis_index("rep") * block_rows
    first_mat = jnp.minimum(first_row // model_width, matrices - 2)
    pair = jnp.einsum(
        "krd,krf->kdf",
        lax.dynamic_slice_in_dim(ortho_basis, first_mat, 2, 0),
        lax.dynamic_slice_in_dim(current, first_mat, 2, 0),
        precision=lax.Precision.HIGHEST,
    ).reshape(2 * model_width, shard_cols)
    own_block = lax.dynamic_slice_in_dim(
        pair, first_row - first_mat * model_width, block_rows, 0
    )
    flat_approx = lax.all_to_all(own_block, "tp", split_axis=0, concat_axis=1, tiled=True)
    new_momentum = MOMENTUM_DECAY * momentum + flat_approx
    new_master = master - LEARNING_RATE * new_momentum
    working = new_master.astype(jnp.bfloat16)
    by_columns = lax.all_to_all(working, "tp", split_axis=1, concat_axis=0, tiled=True)
    weight_rows = lax.all_gather(by_columns, "rep", axis=0, tiled=True)
    weights = weight_rows.reshape(matrices, model_width, shard_cols)
    return (new_error, current, new_momentum, new_master, weights)


def solution(mesh):
    placed = (
        P("rep", None, None, "tp"),
        P("rep", None, None, "tp"),
        P(None, None, "tp"),
        P(("rep", "tp"), None),
        P(("rep", "tp"), None),
    )
    return jax.shard_map(
        local,
        mesh=mesh,
        in_specs=placed,
        out_specs=(
            P("rep", None, None, "tp"),
            P(None, None, "tp"),
            P(("rep", "tp"), None),
            P(("rep", "tp"), None),
            P(None, None, "tp"),
        ),
        check_vma=False,
    )
```

```python
import functools

import jax
import jax.numpy as jnp
from jax import lax
from jax.experimental import pallas as pl
from jax.experimental.pallas import tpu as pltpu
from jax.sharding import PartitionSpec as P

ROUNDS = 2
NS_STEPS = 5


NORM_EPSILON = 1e-06
MOMENTUM_DECAY = 0.9
LEARNING_RATE = 0.5

MESH_AXES = ("rep", "tp")
LANES = 128


def _coord(level):
    name, n, stride = level
    return lax.rem(lax.div(lax.axis_index(name), stride), n)


def _peer(level, j):
    name, n, stride = level
    base = lax.axis_index(name) + (j - _coord(level)) * stride
    return tuple(base if axis == name else lax.axis_index(axis) for axis in MESH_AXES)


def _allreduce_kernel(levels, x_ref, o_ref, *scratch):
    n_lev = len(levels)
    it = iter(scratch)
    recv = [next(it) for _ in range(n_lev)]
    sums = [next(it) for _ in range(n_lev - 1)]
    gath = [next(it) for _ in range(n_lev - 1)] + [None]
    rs_send = [next(it) for _ in range(n_lev)]
    rs_recv = [next(it) for _ in range(n_lev)]
    ag_send = [next(it) for _ in range(n_lev)]
    ag_recv = [next(it) for _ in range(n_lev)]
    local_sem = next(it)

    me = [_coord(level) for level in levels]

    barrier = pltpu.get_barrier_semaphore()
    total_peers = 0
    for lev, (name, n, _) in enumerate(levels):
        for off in range(1, n):
            j = lax.rem(me[lev] + off, n)
            pl.semaphore_signal(barrier, inc=1, device_id=_peer(levels[lev], j),
                                device_id_type=pl.DeviceIdType.MESH)
        total_peers += n - 1
    pl.semaphore_wait(barrier, total_peers)

    gath_bufs = [o_ref] + gath[: n_lev - 1]

    src = x_ref
    for lev, (name, n, _) in enumerate(levels):
        m = me[lev]
        copies = []
        for off in range(1, n):
            j = lax.rem(m + off, n)
            cp = pltpu.make_async_remote_copy(
                src_ref=src.at[j], dst_ref=recv[lev].at[m],
                send_sem=rs_send[lev].at[off], recv_sem=rs_recv[lev].at[m],
                device_id=_peer(levels[lev], j), device_id_type=pl.DeviceIdType.MESH)
            cp.start()
            copies.append((j, off, cp))
        own = pltpu.make_async_copy(src.at[m], recv[lev].at[m], local_sem.at[0])
        own.start()
        own.wait()
        for j, off, cp in copies:
            pltpu.make_async_remote_copy(
                src_ref=src.at[j], dst_ref=recv[lev].at[j],
                send_sem=rs_send[lev].at[off], recv_sem=rs_recv[lev].at[j],
                device_id=_peer(levels[lev], j), device_id_type=pl.DeviceIdType.MESH).wait_recv()
        for j, off, cp in copies:
            cp.wait_send()
        r = recv[lev]
        if lev < n_lev - 1:
            dst = sums[lev]
        else:
            dst = gath_bufs[lev].at[m]
        if len(r.shape) > 3:
            lead = r.shape[1:-2]
            count = 1
            for d in lead:
                count *= d

            def body(i, carry, r=r, dst=dst, n=n, lead=lead):
                idx = []
                rest = i
                for d in reversed(lead):
                    idx.append(lax.rem(rest, d))
                    rest = lax.div(rest, d)
                idx = tuple(reversed(idx))
                acc = r[(0,) + idx]
                for j in range(1, n):
                    acc = acc + r[(j,) + idx]
                dst[idx] = acc
                return carry
            lax.fori_loop(0, count, body, 0)
        else:
            acc = r[0]
            for j in range(1, n):
                acc = acc + r[j]
            dst[...] = acc
        if lev < n_lev - 1:
            src = sums[lev]

    for lev in reversed(range(n_lev)):
        name, n, _ = levels[lev]
        m = me[lev]
        buf = gath_bufs[lev]
        if lev == n_lev - 1:
            piece = buf.at[m]
        else:
            piece = gath_bufs[lev + 1]
            own = pltpu.make_async_copy(piece, buf.at[m], local_sem.at[0])
            own.start()
            own.wait()
        copies = []
        for off in range(1, n):
            j = lax.rem(m + off, n)
            cp = pltpu.make_async_remote_copy(
                src_ref=piece, dst_ref=buf.at[m],
                send_sem=ag_send[lev].at[off], recv_sem=ag_recv[lev].at[m],
                device_id=_peer(levels[lev], j), device_id_type=pl.DeviceIdType.MESH)
            cp.start()
            copies.append((j, off, cp))
        for j, off, cp in copies:
            pltpu.make_async_remote_copy(
                src_ref=piece, dst_ref=buf.at[j],
                send_sem=ag_send[lev].at[off], recv_sem=ag_recv[lev].at[j],
                device_id=_peer(levels[lev], j), device_id_type=pl.DeviceIdType.MESH).wait_recv()
        for j, off, cp in copies:
            cp.wait_send()


def allreduce(x, levels, collective_id):
    shape = x.shape
    total = x.size
    counts = [n for _, n, _ in levels]
    per = total
    for n in counts:
        per //= n
    rows = per // LANES
    full = tuple(counts) + (rows, LANES)
    xr = x.reshape(full)
    scratch = []
    for lev in range(len(levels)):
        scratch.append(pltpu.VMEM(full[lev:], jnp.float32))
    for lev in range(len(levels) - 1):
        scratch.append(pltpu.VMEM(full[lev + 1:], jnp.float32))
    for lev in range(len(levels) - 1):
        scratch.append(pltpu.VMEM(full[lev + 1:], jnp.float32))
    for _ in range(4):
        for _, n, _ in levels:
            scratch.append(pltpu.SemaphoreType.DMA((n,)))
    scratch.append(pltpu.SemaphoreType.DMA((1,)))
    out = pl.pallas_call(
        functools.partial(_allreduce_kernel, tuple(levels)),
        out_shape=jax.ShapeDtypeStruct(full, jnp.float32),
        in_specs=[pl.BlockSpec(memory_space=pltpu.VMEM)],
        out_specs=pl.BlockSpec(memory_space=pltpu.VMEM),
        scratch_shapes=scratch,
        compiler_params=pltpu.CompilerParams(collective_id=collective_id, has_side_effects=True),
        cost_estimate=pl.CostEstimate(flops=total * 2, bytes_accessed=total * 4 * 4, transcendentals=0),
    )(xr)
    return out.reshape(shape)


def _update_kernel(x_ref, mom_ref, master_ref, mom_out, master_out, cols_out,
                   rows_buf, work_buf, send1, recv1, send2, recv2, local_sem):
    n, rows, cols = x_ref.shape
    me = lax.axis_index("tp")
    barrier = pltpu.get_barrier_semaphore()
    for off in range(1, n):
        j = lax.rem(me + off, n)
        pl.semaphore_signal(barrier, inc=1, device_id=_peer(("tp", n, 1), j),
                            device_id_type=pl.DeviceIdType.MESH)
    pl.semaphore_wait(barrier, n - 1)

    def to_rows(j, src):
        return pltpu.make_async_remote_copy(
            src_ref=src, dst_ref=rows_buf.at[:, pl.ds(pl.multiple_of(me * cols, cols), cols)],
            send_sem=send1.at[j], recv_sem=recv1.at[me],
            device_id=_peer(("tp", n, 1), j), device_id_type=pl.DeviceIdType.MESH)

    copies = []
    for off in range(1, n):
        j = lax.rem(me + off, n)
        cp = to_rows(j, x_ref.at[j])
        cp.start()
        copies.append((j, cp))
    own = pltpu.make_async_copy(
        x_ref.at[me], rows_buf.at[:, pl.ds(pl.multiple_of(me * cols, cols), cols)], local_sem.at[0])
    own.start()
    own.wait()
    for j, cp in copies:
        pltpu.make_async_remote_copy(
            src_ref=x_ref.at[j], dst_ref=rows_buf.at[:, pl.ds(pl.multiple_of(j * cols, cols), cols)],
            send_sem=send1.at[j], recv_sem=recv1.at[j],
            device_id=_peer(("tp", n, 1), j), device_id_type=pl.DeviceIdType.MESH).wait_recv()
    for j, cp in copies:
        cp.wait_send()

    new_mom = MOMENTUM_DECAY * mom_ref[...] + rows_buf[...]
    new_master = master_ref[...] - LEARNING_RATE * new_mom
    mom_out[...] = new_mom
    master_out[...] = new_master
    work_buf[...] = new_master.astype(work_buf.dtype)

    copies = []
    for off in range(1, n):
        j = lax.rem(me + off, n)
        cp = pltpu.make_async_remote_copy(
            src_ref=work_buf.at[:, pl.ds(pl.multiple_of(j * cols, cols), cols)], dst_ref=cols_out.at[me],
            send_sem=send2.at[j], recv_sem=recv2.at[me],
            device_id=_peer(("tp", n, 1), j), device_id_type=pl.DeviceIdType.MESH)
        cp.start()
        copies.append((j, cp))
    own = pltpu.make_async_copy(
        work_buf.at[:, pl.ds(pl.multiple_of(me * cols, cols), cols)], cols_out.at[me], local_sem.at[0])
    own.start()
    own.wait()
    for j, cp in copies:
        pltpu.make_async_remote_copy(
            src_ref=work_buf.at[:, pl.ds(pl.multiple_of(j * cols, cols), cols)], dst_ref=cols_out.at[j],
            send_sem=send2.at[j], recv_sem=recv2.at[j],
            device_id=_peer(("tp", n, 1), j), device_id_type=pl.DeviceIdType.MESH).wait_recv()
    for j, cp in copies:
        cp.wait_send()


def flat_update(own_block, momentum, master, n, collective_id):
    block_rows, cols = own_block.shape
    rows = block_rows // n
    x = own_block.reshape(n, rows, cols)
    f32 = jnp.float32
    vmem = pl.BlockSpec(memory_space=pltpu.VMEM)
    return pl.pallas_call(
        _update_kernel,
        out_shape=(
            jax.ShapeDtypeStruct(momentum.shape, f32),
            jax.ShapeDtypeStruct(master.shape, f32),
            jax.ShapeDtypeStruct((n, rows, cols), jnp.bfloat16),
        ),
        in_specs=[vmem, vmem, vmem],
        out_specs=(vmem, vmem, vmem),
        scratch_shapes=[
            pltpu.VMEM((rows, n * cols), f32),
            pltpu.VMEM((rows, n * cols), jnp.bfloat16),
            pltpu.SemaphoreType.DMA((n,)),
            pltpu.SemaphoreType.DMA((n,)),
            pltpu.SemaphoreType.DMA((n,)),
            pltpu.SemaphoreType.DMA((n,)),
            pltpu.SemaphoreType.DMA((1,)),
        ],
        compiler_params=pltpu.CompilerParams(collective_id=collective_id, has_side_effects=True),
        cost_estimate=pl.CostEstimate(flops=4 * momentum.size, bytes_accessed=5 * 4 * momentum.size,
                                      transcendentals=0),
    )(x, momentum, master)


def split_levels(name, size, inner):
    if size % inner or size == inner:
        return ((name, size, 1),)
    if inner == 2:
        return ((name, inner, 1), (name, size // inner, inner))
    return ((name, size // inner, inner), (name, inner, 1))


def local_gram(factor):
    return jnp.einsum("krd,ksd->krs", factor, factor, precision=lax.Precision.HIGHEST)


def orthonormal(factor, gram_of):
    gram_now = gram_of(factor)
    sum_squares = jnp.trace(gram_now, axis1=1, axis2=2)[:, None, None]
    factor_scale = lax.rsqrt(sum_squares + NORM_EPSILON)
    ortho_basis = factor * factor_scale
    gram_now = gram_now * (factor_scale * factor_scale)
    for iteration in range(NS_STEPS):
        if iteration > 0:
            gram_now = gram_of(ortho_basis)
        ortho_basis = 1.5 * ortho_basis - 0.5 * jnp.einsum(
            "krs,ksd->krd", gram_now, ortho_basis, precision=lax.Precision.HIGHEST
        )
    return ortho_basis


def local(grads, error, query, momentum, master):
    corrected = grads[0].astype(jnp.float32) + error[0]
    current = query
    replicas = lax.axis_size("rep")
    rep_only = (("rep", replicas, 1),)
    both = split_levels("tp", lax.axis_size("tp"), 2) + split_levels("rep", replicas, 4)
    for power_pass in range(ROUNDS):
        partial_factor = jnp.einsum(
            "kdf,krf->krd", corrected, current, precision=lax.Precision.HIGHEST
        )
        summed = allreduce(partial_factor, both, 0)
        ortho_basis = orthonormal(summed, local_gram)
        partial_query = jnp.einsum(
            "kdf,krd->krf", corrected, ortho_basis, precision=lax.Precision.HIGHEST
        )
        current = allreduce(partial_query, rep_only, 1) / replicas
    approx = jnp.einsum("krd,krf->kdf", ortho_basis, current, precision=lax.Precision.HIGHEST)
    new_error = (corrected - approx)[None]
    matrices, model_width, shard_cols = approx.shape
    block_rows = matrices * model_width // replicas
    span = min(matrices, -(-block_rows // model_width) + 1)
    first_row = lax.axis_index("rep") * block_rows
    first_mat = jnp.minimum(first_row // model_width, matrices - span)
    pair = jnp.einsum(
        "krd,krf->kdf",
        lax.dynamic_slice_in_dim(ortho_basis, first_mat, span, 0),
        lax.dynamic_slice_in_dim(current, first_mat, span, 0),
        precision=lax.Precision.HIGHEST,
    ).reshape(span * model_width, shard_cols)
    own_block = lax.dynamic_slice_in_dim(
        pair, first_row - first_mat * model_width, block_rows, 0
    )
    new_momentum, new_master, by_columns = flat_update(
        own_block, momentum, master, lax.axis_size("tp"), 2)
    by_columns = by_columns.reshape(block_rows, shard_cols)
    weight_rows = lax.all_gather(by_columns, "rep", axis=0, tiled=True)
    weights = weight_rows.reshape(matrices, model_width, shard_cols)
    return (new_error, current, new_momentum, new_master, weights)


def solution(mesh):
    placed = (
        P("rep", None, None, "tp"),
        P("rep", None, None, "tp"),
        P(None, None, "tp"),
        P(("rep", "tp"), None),
        P(("rep", "tp"), None),
    )
    return jax.shard_map(
        local,
        mesh=mesh,
        in_specs=placed,
        out_specs=(
            P("rep", None, None, "tp"),
            P(None, None, "tp"),
            P(("rep", "tp"), None),
            P(("rep", "tp"), None),
            P(None, None, "tp"),
        ),
        check_vma=False,
    )
```

```python
import functools

import jax
import jax.numpy as jnp
from jax import lax
from jax.experimental import pallas as pl
from jax.experimental.pallas import tpu as pltpu
from jax.sharding import PartitionSpec as P

ROUNDS = 2
NS_STEPS = 5


NORM_EPSILON = 1e-06
MOMENTUM_DECAY = 0.9
LEARNING_RATE = 0.5

MESH_AXES = ("rep", "tp")
LANES = 128


def _coord(level):
    name, n, stride = level
    return lax.rem(lax.div(lax.axis_index(name), stride), n)


def _peer(level, j):
    name, n, stride = level
    base = lax.axis_index(name) + (j - _coord(level)) * stride
    return tuple(base if axis == name else lax.axis_index(axis) for axis in MESH_AXES)


def _allreduce_kernel(levels, x_ref, o_ref, *scratch):
    n_lev = len(levels)
    it = iter(scratch)
    recv = [next(it) for _ in range(n_lev)]
    sums = [next(it) for _ in range(n_lev - 1)]
    gath = [next(it) for _ in range(n_lev - 1)] + [None]
    rs_send = [next(it) for _ in range(n_lev)]
    rs_recv = [next(it) for _ in range(n_lev)]
    ag_send = [next(it) for _ in range(n_lev)]
    ag_recv = [next(it) for _ in range(n_lev)]
    local_sem = next(it)

    me = [_coord(level) for level in levels]

    barrier = pltpu.get_barrier_semaphore()
    total_peers = 0
    for lev, (name, n, _) in enumerate(levels):
        for off in range(1, n):
            j = lax.rem(me[lev] + off, n)
            pl.semaphore_signal(barrier, inc=1, device_id=_peer(levels[lev], j),
                                device_id_type=pl.DeviceIdType.MESH)
        total_peers += n - 1
    pl.semaphore_wait(barrier, total_peers)

    gath_bufs = [o_ref] + gath[: n_lev - 1]

    src = x_ref
    for lev, (name, n, _) in enumerate(levels):
        m = me[lev]
        copies = []
        for off in range(1, n):
            j = lax.rem(m + off, n)
            cp = pltpu.make_async_remote_copy(
                src_ref=src.at[j], dst_ref=recv[lev].at[m],
                send_sem=rs_send[lev].at[off], recv_sem=rs_recv[lev].at[m],
                device_id=_peer(levels[lev], j), device_id_type=pl.DeviceIdType.MESH)
            cp.start()
            copies.append((j, off, cp))
        own = pltpu.make_async_copy(src.at[m], recv[lev].at[m], local_sem.at[0])
        own.start()
        own.wait()
        for j, off, cp in copies:
            pltpu.make_async_remote_copy(
                src_ref=src.at[j], dst_ref=recv[lev].at[j],
                send_sem=rs_send[lev].at[off], recv_sem=rs_recv[lev].at[j],
                device_id=_peer(levels[lev], j), device_id_type=pl.DeviceIdType.MESH).wait_recv()
        for j, off, cp in copies:
            cp.wait_send()
        r = recv[lev]
        if lev < n_lev - 1:
            dst = sums[lev]
        else:
            dst = gath_bufs[lev].at[m]
        if len(r.shape) > 3:
            lead = r.shape[1:-2]
            count = 1
            for d in lead:
                count *= d

            def body(i, carry, r=r, dst=dst, n=n, lead=lead):
                idx = []
                rest = i
                for d in reversed(lead):
                    idx.append(lax.rem(rest, d))
                    rest = lax.div(rest, d)
                idx = tuple(reversed(idx))
                acc = r[(0,) + idx]
                for j in range(1, n):
                    acc = acc + r[(j,) + idx]
                dst[idx] = acc
                return carry
            lax.fori_loop(0, count, body, 0)
        else:
            acc = r[0]
            for j in range(1, n):
                acc = acc + r[j]
            dst[...] = acc
        if lev < n_lev - 1:
            src = sums[lev]

    for lev in reversed(range(n_lev)):
        name, n, _ = levels[lev]
        m = me[lev]
        buf = gath_bufs[lev]
        if lev == n_lev - 1:
            piece = buf.at[m]
        else:
            piece = gath_bufs[lev + 1]
            own = pltpu.make_async_copy(piece, buf.at[m], local_sem.at[0])
            own.start()
            own.wait()
        copies = []
        for off in range(1, n):
            j = lax.rem(m + off, n)
            cp = pltpu.make_async_remote_copy(
                src_ref=piece, dst_ref=buf.at[m],
                send_sem=ag_send[lev].at[off], recv_sem=ag_recv[lev].at[m],
                device_id=_peer(levels[lev], j), device_id_type=pl.DeviceIdType.MESH)
            cp.start()
            copies.append((j, off, cp))
        for j, off, cp in copies:
            pltpu.make_async_remote_copy(
                src_ref=piece, dst_ref=buf.at[j],
                send_sem=ag_send[lev].at[off], recv_sem=ag_recv[lev].at[j],
                device_id=_peer(levels[lev], j), device_id_type=pl.DeviceIdType.MESH).wait_recv()
        for j, off, cp in copies:
            cp.wait_send()


def allreduce(x, levels, collective_id):
    shape = x.shape
    total = x.size
    counts = [n for _, n, _ in levels]
    per = total
    for n in counts:
        per //= n
    rows = per // LANES
    full = tuple(counts) + (rows, LANES)
    xr = x.reshape(full)
    scratch = []
    for lev in range(len(levels)):
        scratch.append(pltpu.VMEM(full[lev:], jnp.float32))
    for lev in range(len(levels) - 1):
        scratch.append(pltpu.VMEM(full[lev + 1:], jnp.float32))
    for lev in range(len(levels) - 1):
        scratch.append(pltpu.VMEM(full[lev + 1:], jnp.float32))
    for _ in range(4):
        for _, n, _ in levels:
            scratch.append(pltpu.SemaphoreType.DMA((n,)))
    scratch.append(pltpu.SemaphoreType.DMA((1,)))
    out = pl.pallas_call(
        functools.partial(_allreduce_kernel, tuple(levels)),
        out_shape=jax.ShapeDtypeStruct(full, jnp.float32),
        in_specs=[pl.BlockSpec(memory_space=pltpu.VMEM)],
        out_specs=pl.BlockSpec(memory_space=pltpu.VMEM),
        scratch_shapes=scratch,
        compiler_params=pltpu.CompilerParams(collective_id=collective_id, has_side_effects=True),
        cost_estimate=pl.CostEstimate(flops=total * 2, bytes_accessed=total * 4 * 4, transcendentals=0),
    )(xr)
    return out.reshape(shape)


def _update_kernel(x_ref, mom_ref, master_ref, mom_out, master_out, cols_out,
                   rows_buf, work_buf, send1, recv1, send2, recv2, local_sem):
    n, rows, cols = x_ref.shape
    me = lax.axis_index("tp")
    barrier = pltpu.get_barrier_semaphore()
    for off in range(1, n):
        j = lax.rem(me + off, n)
        pl.semaphore_signal(barrier, inc=1, device_id=_peer(("tp", n, 1), j),
                            device_id_type=pl.DeviceIdType.MESH)
    pl.semaphore_wait(barrier, n - 1)

    def to_rows(j, src):
        return pltpu.make_async_remote_copy(
            src_ref=src, dst_ref=rows_buf.at[:, pl.ds(pl.multiple_of(me * cols, cols), cols)],
            send_sem=send1.at[j], recv_sem=recv1.at[me],
            device_id=_peer(("tp", n, 1), j), device_id_type=pl.DeviceIdType.MESH)

    copies = []
    for off in range(1, n):
        j = lax.rem(me + off, n)
        cp = to_rows(j, x_ref.at[j])
        cp.start()
        copies.append((j, cp))
    own = pltpu.make_async_copy(
        x_ref.at[me], rows_buf.at[:, pl.ds(pl.multiple_of(me * cols, cols), cols)], local_sem.at[0])
    own.start()
    own.wait()
    for j, cp in copies:
        pltpu.make_async_remote_copy(
            src_ref=x_ref.at[j], dst_ref=rows_buf.at[:, pl.ds(pl.multiple_of(j * cols, cols), cols)],
            send_sem=send1.at[j], recv_sem=recv1.at[j],
            device_id=_peer(("tp", n, 1), j), device_id_type=pl.DeviceIdType.MESH).wait_recv()
    for j, cp in copies:
        cp.wait_send()

    new_mom = MOMENTUM_DECAY * mom_ref[...] + rows_buf[...]
    new_master = master_ref[...] - LEARNING_RATE * new_mom
    mom_out[...] = new_mom
    master_out[...] = new_master
    work_buf[...] = new_master.astype(work_buf.dtype)

    copies = []
    for off in range(1, n):
        j = lax.rem(me + off, n)
        cp = pltpu.make_async_remote_copy(
            src_ref=work_buf.at[:, pl.ds(pl.multiple_of(j * cols, cols), cols)], dst_ref=cols_out.at[me],
            send_sem=send2.at[j], recv_sem=recv2.at[me],
            device_id=_peer(("tp", n, 1), j), device_id_type=pl.DeviceIdType.MESH)
        cp.start()
        copies.append((j, cp))
    own = pltpu.make_async_copy(
        work_buf.at[:, pl.ds(pl.multiple_of(me * cols, cols), cols)], cols_out.at[me], local_sem.at[0])
    own.start()
    own.wait()
    for j, cp in copies:
        pltpu.make_async_remote_copy(
            src_ref=work_buf.at[:, pl.ds(pl.multiple_of(j * cols, cols), cols)], dst_ref=cols_out.at[j],
            send_sem=send2.at[j], recv_sem=recv2.at[j],
            device_id=_peer(("tp", n, 1), j), device_id_type=pl.DeviceIdType.MESH).wait_recv()
    for j, cp in copies:
        cp.wait_send()


def flat_update(own_block, momentum, master, n, collective_id):
    block_rows, cols = own_block.shape
    rows = block_rows // n
    x = own_block.reshape(n, rows, cols)
    f32 = jnp.float32
    vmem = pl.BlockSpec(memory_space=pltpu.VMEM)
    return pl.pallas_call(
        _update_kernel,
        out_shape=(
            jax.ShapeDtypeStruct(momentum.shape, f32),
            jax.ShapeDtypeStruct(master.shape, f32),
            jax.ShapeDtypeStruct((n, rows, cols), jnp.bfloat16),
        ),
        in_specs=[vmem, vmem, vmem],
        out_specs=(vmem, vmem, vmem),
        scratch_shapes=[
            pltpu.VMEM((rows, n * cols), f32),
            pltpu.VMEM((rows, n * cols), jnp.bfloat16),
            pltpu.SemaphoreType.DMA((n,)),
            pltpu.SemaphoreType.DMA((n,)),
            pltpu.SemaphoreType.DMA((n,)),
            pltpu.SemaphoreType.DMA((n,)),
            pltpu.SemaphoreType.DMA((1,)),
        ],
        compiler_params=pltpu.CompilerParams(collective_id=collective_id, has_side_effects=True),
        cost_estimate=pl.CostEstimate(flops=4 * momentum.size, bytes_accessed=5 * 4 * momentum.size,
                                      transcendentals=0),
    )(x, momentum, master)


def _orthonormal_kernel(l_ref, o_ref):
    rank = l_ref.shape[1]
    hi = lax.Precision.HIGHEST
    eye = lax.broadcasted_iota(jnp.int32, (rank, rank), 0) == lax.broadcasted_iota(
        jnp.int32, (rank, rank), 1)

    def gram(x):
        return lax.dot_general(x, x, (((1,), (1,)), ((), ())), precision=hi,
                               preferred_element_type=jnp.float32)

    def body(k, carry):
        x = l_ref[k]
        g = gram(x)
        sum_squares = jnp.sum(jnp.where(eye, g, 0.0), keepdims=True)
        scale = lax.rsqrt(sum_squares + NORM_EPSILON)
        x = x * scale
        g = g * (scale * scale)
        for iteration in range(NS_STEPS):
            if iteration > 0:
                g = gram(x)
            x = 1.5 * x - 0.5 * jnp.dot(g, x, precision=hi, preferred_element_type=jnp.float32)
        o_ref[k] = x
        return carry

    lax.fori_loop(0, l_ref.shape[0], body, 0)


def orthonormal_kernel(factor):
    mats, rank, width = factor.shape
    vmem = pl.BlockSpec(memory_space=pltpu.VMEM)
    return pl.pallas_call(
        _orthonormal_kernel,
        out_shape=jax.ShapeDtypeStruct(factor.shape, jnp.float32),
        in_specs=[vmem],
        out_specs=vmem,
        cost_estimate=pl.CostEstimate(flops=mats * NS_STEPS * 4 * rank * rank * width * 6,
                                      bytes_accessed=2 * 4 * factor.size, transcendentals=mats),
    )(factor)


def split_levels(name, size, inner):
    if size % inner or size == inner:
        return ((name, size, 1),)
    if inner == 2:
        return ((name, inner, 1), (name, size // inner, inner))
    return ((name, size // inner, inner), (name, inner, 1))


def local_gram(factor):
    return jnp.einsum("krd,ksd->krs", factor, factor, precision=lax.Precision.HIGHEST)


def orthonormal(factor, gram_of):
    gram_now = gram_of(factor)
    sum_squares = jnp.trace(gram_now, axis1=1, axis2=2)[:, None, None]
    factor_scale = lax.rsqrt(sum_squares + NORM_EPSILON)
    ortho_basis = factor * factor_scale
    gram_now = gram_now * (factor_scale * factor_scale)
    for iteration in range(NS_STEPS):
        if iteration > 0:
            gram_now = gram_of(ortho_basis)
        ortho_basis = 1.5 * ortho_basis - 0.5 * jnp.einsum(
            "krs,ksd->krd", gram_now, ortho_basis, precision=lax.Precision.HIGHEST
        )
    return ortho_basis


def local(grads, error, query, momentum, master):
    corrected = grads[0].astype(jnp.float32) + error[0]
    current = query
    replicas = lax.axis_size("rep")
    rep_only = (("rep", replicas, 1),)
    both = split_levels("tp", lax.axis_size("tp"), 2) + split_levels("rep", replicas, 4)
    for power_pass in range(ROUNDS):
        partial_factor = jnp.einsum(
            "kdf,krf->krd", corrected, current, precision=lax.Precision.HIGHEST
        )
        summed = allreduce(partial_factor, both, 0)
        ortho_basis = orthonormal_kernel(summed)
        partial_query = jnp.einsum(
            "kdf,krd->krf", corrected, ortho_basis, precision=lax.Precision.HIGHEST
        )
        current = allreduce(partial_query, rep_only, 1) / replicas
    approx = jnp.einsum("krd,krf->kdf", ortho_basis, current, precision=lax.Precision.HIGHEST)
    new_error = (corrected - approx)[None]
    matrices, model_width, shard_cols = approx.shape
    block_rows = matrices * model_width // replicas
    span = min(matrices, -(-block_rows // model_width) + 1)
    first_row = lax.axis_index("rep") * block_rows
    first_mat = jnp.minimum(first_row // model_width, matrices - span)
    pair = jnp.einsum(
        "krd,krf->kdf",
        lax.dynamic_slice_in_dim(ortho_basis, first_mat, span, 0),
        lax.dynamic_slice_in_dim(current, first_mat, span, 0),
        precision=lax.Precision.HIGHEST,
    ).reshape(span * model_width, shard_cols)
    own_block = lax.dynamic_slice_in_dim(
        pair, first_row - first_mat * model_width, block_rows, 0
    )
    new_momentum, new_master, by_columns = flat_update(
        own_block, momentum, master, lax.axis_size("tp"), 2)
    by_columns = by_columns.reshape(block_rows, shard_cols)
    weight_rows = lax.all_gather(by_columns, "rep", axis=0, tiled=True)
    weights = weight_rows.reshape(matrices, model_width, shard_cols)
    return (new_error, current, new_momentum, new_master, weights)


def solution(mesh):
    placed = (
        P("rep", None, None, "tp"),
        P("rep", None, None, "tp"),
        P(None, None, "tp"),
        P(("rep", "tp"), None),
        P(("rep", "tp"), None),
    )
    return jax.shard_map(
        local,
        mesh=mesh,
        in_specs=placed,
        out_specs=(
            P("rep", None, None, "tp"),
            P(None, None, "tp"),
            P(("rep", "tp"), None),
            P(("rep", "tp"), None),
            P(None, None, "tp"),
        ),
        check_vma=False,
    )
```

```python
import functools

import jax
import jax.numpy as jnp
from jax import lax
from jax.experimental import pallas as pl
from jax.experimental.pallas import tpu as pltpu
from jax.sharding import PartitionSpec as P

ROUNDS = 2
NS_STEPS = 5


NORM_EPSILON = 1e-06
MOMENTUM_DECAY = 0.9
LEARNING_RATE = 0.5

MESH_AXES = ("rep", "tp")
LANES = 128


def _coord(level):
    name, n, stride = level
    return lax.rem(lax.div(lax.axis_index(name), stride), n)


def _peer(level, j):
    name, n, stride = level
    base = lax.axis_index(name) + (j - _coord(level)) * stride
    return tuple(base if axis == name else lax.axis_index(axis) for axis in MESH_AXES)


def _allreduce_kernel(levels, x_ref, o_ref, *scratch):
    n_lev = len(levels)
    it = iter(scratch)
    recv = [next(it) for _ in range(n_lev)]
    sums = [next(it) for _ in range(n_lev - 1)]
    gath = [next(it) for _ in range(n_lev - 1)] + [None]
    rs_send = [next(it) for _ in range(n_lev)]
    rs_recv = [next(it) for _ in range(n_lev)]
    ag_send = [next(it) for _ in range(n_lev)]
    ag_recv = [next(it) for _ in range(n_lev)]
    local_sem = next(it)

    me = [_coord(level) for level in levels]

    barrier = pltpu.get_barrier_semaphore()
    total_peers = 0
    for lev, (name, n, _) in enumerate(levels):
        for off in range(1, n):
            j = lax.rem(me[lev] + off, n)
            pl.semaphore_signal(barrier, inc=1, device_id=_peer(levels[lev], j),
                                device_id_type=pl.DeviceIdType.MESH)
        total_peers += n - 1
    pl.semaphore_wait(barrier, total_peers)

    gath_bufs = [o_ref] + gath[: n_lev - 1]

    src = x_ref
    for lev, (name, n, _) in enumerate(levels):
        m = me[lev]
        copies = []
        for off in range(1, n):
            j = lax.rem(m + off, n)
            cp = pltpu.make_async_remote_copy(
                src_ref=src.at[j], dst_ref=recv[lev].at[m],
                send_sem=rs_send[lev].at[off], recv_sem=rs_recv[lev].at[m],
                device_id=_peer(levels[lev], j), device_id_type=pl.DeviceIdType.MESH)
            cp.start()
            copies.append((j, off, cp))
        own = pltpu.make_async_copy(src.at[m], recv[lev].at[m], local_sem.at[0])
        own.start()
        own.wait()
        for j, off, cp in copies:
            pltpu.make_async_remote_copy(
                src_ref=src.at[j], dst_ref=recv[lev].at[j],
                send_sem=rs_send[lev].at[off], recv_sem=rs_recv[lev].at[j],
                device_id=_peer(levels[lev], j), device_id_type=pl.DeviceIdType.MESH).wait_recv()
        for j, off, cp in copies:
            cp.wait_send()
        r = recv[lev]
        if lev < n_lev - 1:
            dst = sums[lev]
        else:
            dst = gath_bufs[lev].at[m]
        if len(r.shape) > 3:
            lead = r.shape[1:-2]
            count = 1
            for d in lead:
                count *= d

            def body(i, carry, r=r, dst=dst, n=n, lead=lead):
                idx = []
                rest = i
                for d in reversed(lead):
                    idx.append(lax.rem(rest, d))
                    rest = lax.div(rest, d)
                idx = tuple(reversed(idx))
                acc = r[(0,) + idx]
                for j in range(1, n):
                    acc = acc + r[(j,) + idx]
                dst[idx] = acc
                return carry
            lax.fori_loop(0, count, body, 0)
        else:
            acc = r[0]
            for j in range(1, n):
                acc = acc + r[j]
            dst[...] = acc
        if lev < n_lev - 1:
            src = sums[lev]

    for lev in reversed(range(n_lev)):
        name, n, _ = levels[lev]
        m = me[lev]
        buf = gath_bufs[lev]
        if lev == n_lev - 1:
            piece = buf.at[m]
        else:
            piece = gath_bufs[lev + 1]
            own = pltpu.make_async_copy(piece, buf.at[m], local_sem.at[0])
            own.start()
            own.wait()
        copies = []
        for off in range(1, n):
            j = lax.rem(m + off, n)
            cp = pltpu.make_async_remote_copy(
                src_ref=piece, dst_ref=buf.at[m],
                send_sem=ag_send[lev].at[off], recv_sem=ag_recv[lev].at[m],
                device_id=_peer(levels[lev], j), device_id_type=pl.DeviceIdType.MESH)
            cp.start()
            copies.append((j, off, cp))
        for j, off, cp in copies:
            pltpu.make_async_remote_copy(
                src_ref=piece, dst_ref=buf.at[j],
                send_sem=ag_send[lev].at[off], recv_sem=ag_recv[lev].at[j],
                device_id=_peer(levels[lev], j), device_id_type=pl.DeviceIdType.MESH).wait_recv()
        for j, off, cp in copies:
            cp.wait_send()


def allreduce(x, levels, collective_id):
    shape = x.shape
    total = x.size
    counts = [n for _, n, _ in levels]
    per = total
    for n in counts:
        per //= n
    rows = per // LANES
    full = tuple(counts) + (rows, LANES)
    xr = x.reshape(full)
    scratch = []
    for lev in range(len(levels)):
        scratch.append(pltpu.VMEM(full[lev:], jnp.float32))
    for lev in range(len(levels) - 1):
        scratch.append(pltpu.VMEM(full[lev + 1:], jnp.float32))
    for lev in range(len(levels) - 1):
        scratch.append(pltpu.VMEM(full[lev + 1:], jnp.float32))
    for _ in range(4):
        for _, n, _ in levels:
            scratch.append(pltpu.SemaphoreType.DMA((n,)))
    scratch.append(pltpu.SemaphoreType.DMA((1,)))
    out = pl.pallas_call(
        functools.partial(_allreduce_kernel, tuple(levels)),
        out_shape=jax.ShapeDtypeStruct(full, jnp.float32),
        in_specs=[pl.BlockSpec(memory_space=pltpu.VMEM)],
        out_specs=pl.BlockSpec(memory_space=pltpu.VMEM),
        scratch_shapes=scratch,
        compiler_params=pltpu.CompilerParams(collective_id=collective_id, has_side_effects=True),
        cost_estimate=pl.CostEstimate(flops=total * 2, bytes_accessed=total * 4 * 4, transcendentals=0),
    )(xr)
    return out.reshape(shape)


def _update_kernel(x_ref, mom_ref, master_ref, mom_out, master_out,
                   rows_buf, send1, recv1, local_sem):
    n, rows, cols = x_ref.shape
    me = lax.axis_index("tp")
    barrier = pltpu.get_barrier_semaphore()
    for off in range(1, n):
        j = lax.rem(me + off, n)
        pl.semaphore_signal(barrier, inc=1, device_id=_peer(("tp", n, 1), j),
                            device_id_type=pl.DeviceIdType.MESH)
    pl.semaphore_wait(barrier, n - 1)

    def to_rows(j, src):
        return pltpu.make_async_remote_copy(
            src_ref=src, dst_ref=rows_buf.at[:, pl.ds(pl.multiple_of(me * cols, cols), cols)],
            send_sem=send1.at[j], recv_sem=recv1.at[me],
            device_id=_peer(("tp", n, 1), j), device_id_type=pl.DeviceIdType.MESH)

    copies = []
    for off in range(1, n):
        j = lax.rem(me + off, n)
        cp = to_rows(j, x_ref.at[j])
        cp.start()
        copies.append((j, cp))
    own = pltpu.make_async_copy(
        x_ref.at[me], rows_buf.at[:, pl.ds(pl.multiple_of(me * cols, cols), cols)], local_sem.at[0])
    own.start()
    own.wait()
    for j, cp in copies:
        pltpu.make_async_remote_copy(
            src_ref=x_ref.at[j], dst_ref=rows_buf.at[:, pl.ds(pl.multiple_of(j * cols, cols), cols)],
            send_sem=send1.at[j], recv_sem=recv1.at[j],
            device_id=_peer(("tp", n, 1), j), device_id_type=pl.DeviceIdType.MESH).wait_recv()
    for j, cp in copies:
        cp.wait_send()

    new_mom = MOMENTUM_DECAY * mom_ref[...] + rows_buf[...]
    new_master = master_ref[...] - LEARNING_RATE * new_mom
    mom_out[...] = new_mom
    master_out[...] = new_master


def _columns_kernel(x_ref, cols_out, send, recv, local_sem):
    n, rows, cols = cols_out.shape
    me = lax.axis_index("tp")
    barrier = pltpu.get_barrier_semaphore()
    for off in range(1, n):
        j = lax.rem(me + off, n)
        pl.semaphore_signal(barrier, inc=1, device_id=_peer(("tp", n, 1), j),
                            device_id_type=pl.DeviceIdType.MESH)
    pl.semaphore_wait(barrier, n - 1)

    def block(j):
        return x_ref.at[:, pl.ds(pl.multiple_of(j * cols, cols), cols)]

    copies = []
    for off in range(1, n):
        j = lax.rem(me + off, n)
        cp = pltpu.make_async_remote_copy(
            src_ref=block(j), dst_ref=cols_out.at[me],
            send_sem=send.at[j], recv_sem=recv.at[me],
            device_id=_peer(("tp", n, 1), j), device_id_type=pl.DeviceIdType.MESH)
        cp.start()
        copies.append((j, cp))
    own = pltpu.make_async_copy(block(me), cols_out.at[me], local_sem.at[0])
    own.start()
    own.wait()
    for j, cp in copies:
        pltpu.make_async_remote_copy(
            src_ref=block(j), dst_ref=cols_out.at[j],
            send_sem=send.at[j], recv_sem=recv.at[j],
            device_id=_peer(("tp", n, 1), j), device_id_type=pl.DeviceIdType.MESH).wait_recv()
    for j, cp in copies:
        cp.wait_send()


def by_columns(x, n, collective_id):
    rows, width = x.shape
    cols = width // n
    vmem = pl.BlockSpec(memory_space=pltpu.VMEM)
    return pl.pallas_call(
        _columns_kernel,
        out_shape=jax.ShapeDtypeStruct((n, rows, cols), x.dtype),
        in_specs=[vmem],
        out_specs=vmem,
        scratch_shapes=[
            pltpu.SemaphoreType.DMA((n,)),
            pltpu.SemaphoreType.DMA((n,)),
            pltpu.SemaphoreType.DMA((1,)),
        ],
        compiler_params=pltpu.CompilerParams(collective_id=collective_id, has_side_effects=True),
        cost_estimate=pl.CostEstimate(flops=0, bytes_accessed=2 * x.size * x.dtype.itemsize,
                                      transcendentals=0),
    )(x)


def flat_update(own_block, momentum, master, n, collective_id):
    block_rows, cols = own_block.shape
    rows = block_rows // n
    x = own_block.reshape(n, rows, cols)
    f32 = jnp.float32
    vmem = pl.BlockSpec(memory_space=pltpu.VMEM)
    return pl.pallas_call(
        _update_kernel,
        out_shape=(
            jax.ShapeDtypeStruct(momentum.shape, f32),
            jax.ShapeDtypeStruct(master.shape, f32),
        ),
        in_specs=[vmem, vmem, vmem],
        out_specs=(vmem, vmem),
        scratch_shapes=[
            pltpu.VMEM((rows, n * cols), f32),
            pltpu.SemaphoreType.DMA((n,)),
            pltpu.SemaphoreType.DMA((n,)),
            pltpu.SemaphoreType.DMA((1,)),
        ],
        compiler_params=pltpu.CompilerParams(collective_id=collective_id, has_side_effects=True),
        cost_estimate=pl.CostEstimate(flops=4 * momentum.size, bytes_accessed=5 * 4 * momentum.size,
                                      transcendentals=0),
    )(x, momentum, master)


def split_levels(name, size, inner):
    if size % inner or size == inner:
        return ((name, size, 1),)
    if inner == 2:
        return ((name, inner, 1), (name, size // inner, inner))
    return ((name, size // inner, inner), (name, inner, 1))


def local_gram(factor):
    return jnp.einsum("krd,ksd->krs", factor, factor, precision=lax.Precision.HIGHEST)


def orthonormal(factor, gram_of):
    gram_now = gram_of(factor)
    sum_squares = jnp.trace(gram_now, axis1=1, axis2=2)[:, None, None]
    factor_scale = lax.rsqrt(sum_squares + NORM_EPSILON)
    ortho_basis = factor * factor_scale
    gram_now = gram_now * (factor_scale * factor_scale)
    for iteration in range(NS_STEPS):
        if iteration > 0:
            gram_now = gram_of(ortho_basis)
        ortho_basis = 1.5 * ortho_basis - 0.5 * jnp.einsum(
            "krs,ksd->krd", gram_now, ortho_basis, precision=lax.Precision.HIGHEST
        )
    return ortho_basis


def local(grads, error, query, momentum, master):
    corrected = grads[0].astype(jnp.float32) + error[0]
    current = query
    replicas = lax.axis_size("rep")
    tensor = lax.axis_size("tp")
    kept = master - LEARNING_RATE * (MOMENTUM_DECAY * momentum)
    kept_cols = by_columns(kept, tensor, 3)
    kept_cols = kept_cols.reshape(-1, kept_cols.shape[-1])
    kept_all = lax.all_gather(kept_cols, "rep", axis=0, tiled=True)
    rep_only = (("rep", replicas, 1),)
    both = split_levels("tp", lax.axis_size("tp"), 2) + split_levels("rep", replicas, 4)
    for power_pass in range(ROUNDS):
        partial_factor = jnp.einsum(
            "kdf,krf->krd", corrected, current, precision=lax.Precision.HIGHEST
        )
        summed = allreduce(partial_factor, both, 0)
        ortho_basis = orthonormal(summed, local_gram)
        partial_query = jnp.einsum(
            "kdf,krd->krf", corrected, ortho_basis, precision=lax.Precision.HIGHEST
        )
        current = allreduce(partial_query, rep_only, 1) / replicas
    approx = jnp.einsum("krd,krf->kdf", ortho_basis, current, precision=lax.Precision.HIGHEST)
    new_error = (corrected - approx)[None]
    matrices, model_width, shard_cols = approx.shape
    weights = (kept_all.reshape(approx.shape) - LEARNING_RATE * approx).astype(jnp.bfloat16)
    block_rows = matrices * model_width // replicas
    span = min(matrices, -(-block_rows // model_width) + 1)
    first_row = lax.axis_index("rep") * block_rows
    first_mat = jnp.minimum(first_row // model_width, matrices - span)
    pair = jnp.einsum(
        "krd,krf->kdf",
        lax.dynamic_slice_in_dim(ortho_basis, first_mat, span, 0),
        lax.dynamic_slice_in_dim(current, first_mat, span, 0),
        precision=lax.Precision.HIGHEST,
    ).reshape(span * model_width, shard_cols)
    own_block = lax.dynamic_slice_in_dim(
        pair, first_row - first_mat * model_width, block_rows, 0
    )
    new_momentum, new_master = flat_update(own_block, momentum, master, tensor, 2)
    return (new_error, current, new_momentum, new_master, weights)


def solution(mesh):
    placed = (
        P("rep", None, None, "tp"),
        P("rep", None, None, "tp"),
        P(None, None, "tp"),
        P(("rep", "tp"), None),
        P(("rep", "tp"), None),
    )
    return jax.shard_map(
        local,
        mesh=mesh,
        in_specs=placed,
        out_specs=(
            P("rep", None, None, "tp"),
            P(None, None, "tp"),
            P(("rep", "tp"), None),
            P(("rep", "tp"), None),
            P(None, None, "tp"),
        ),
        check_vma=False,
    )
```

```python
import functools

import jax
import jax.numpy as jnp
from jax import lax
from jax.experimental import pallas as pl
from jax.experimental.pallas import tpu as pltpu
from jax.sharding import PartitionSpec as P

ROUNDS = 2
NS_STEPS = 5


NORM_EPSILON = 1e-06
MOMENTUM_DECAY = 0.9
LEARNING_RATE = 0.5

MESH_AXES = ("rep", "tp")
LANES = 128


def _coord(level):
    name, n, stride = level
    return lax.rem(lax.div(lax.axis_index(name), stride), n)


def _peer(level, j):
    name, n, stride = level
    base = lax.axis_index(name) + (j - _coord(level)) * stride
    return tuple(base if axis == name else lax.axis_index(axis) for axis in MESH_AXES)


def _allreduce_kernel(levels, x_ref, o_ref, *scratch):
    n_lev = len(levels)
    it = iter(scratch)
    recv = [next(it) for _ in range(n_lev)]
    sums = [next(it) for _ in range(n_lev - 1)]
    gath = [next(it) for _ in range(n_lev - 1)] + [None]
    rs_send = [next(it) for _ in range(n_lev)]
    rs_recv = [next(it) for _ in range(n_lev)]
    ag_send = [next(it) for _ in range(n_lev)]
    ag_recv = [next(it) for _ in range(n_lev)]
    local_sem = next(it)

    me = [_coord(level) for level in levels]

    barrier = pltpu.get_barrier_semaphore()
    total_peers = 0
    for lev, (name, n, _) in enumerate(levels):
        for off in range(1, n):
            j = lax.rem(me[lev] + off, n)
            pl.semaphore_signal(barrier, inc=1, device_id=_peer(levels[lev], j),
                                device_id_type=pl.DeviceIdType.MESH)
        total_peers += n - 1
    pl.semaphore_wait(barrier, total_peers)

    gath_bufs = [o_ref] + gath[: n_lev - 1]

    src = x_ref
    for lev, (name, n, _) in enumerate(levels):
        m = me[lev]
        copies = []
        for off in range(1, n):
            j = lax.rem(m + off, n)
            cp = pltpu.make_async_remote_copy(
                src_ref=src.at[j], dst_ref=recv[lev].at[m],
                send_sem=rs_send[lev].at[off], recv_sem=rs_recv[lev].at[m],
                device_id=_peer(levels[lev], j), device_id_type=pl.DeviceIdType.MESH)
            cp.start()
            copies.append((j, off, cp))
        own = pltpu.make_async_copy(src.at[m], recv[lev].at[m], local_sem.at[0])
        own.start()
        own.wait()
        for j, off, cp in copies:
            pltpu.make_async_remote_copy(
                src_ref=src.at[j], dst_ref=recv[lev].at[j],
                send_sem=rs_send[lev].at[off], recv_sem=rs_recv[lev].at[j],
                device_id=_peer(levels[lev], j), device_id_type=pl.DeviceIdType.MESH).wait_recv()
        for j, off, cp in copies:
            cp.wait_send()
        r = recv[lev]
        if lev < n_lev - 1:
            dst = sums[lev]
        else:
            dst = gath_bufs[lev].at[m]
        if len(r.shape) > 3:
            lead = r.shape[1:-2]
            count = 1
            for d in lead:
                count *= d

            def body(i, carry, r=r, dst=dst, n=n, lead=lead):
                idx = []
                rest = i
                for d in reversed(lead):
                    idx.append(lax.rem(rest, d))
                    rest = lax.div(rest, d)
                idx = tuple(reversed(idx))
                acc = r[(0,) + idx]
                for j in range(1, n):
                    acc = acc + r[(j,) + idx]
                dst[idx] = acc
                return carry
            lax.fori_loop(0, count, body, 0)
        else:
            acc = r[0]
            for j in range(1, n):
                acc = acc + r[j]
            dst[...] = acc
        if lev < n_lev - 1:
            src = sums[lev]

    for lev in reversed(range(n_lev)):
        name, n, _ = levels[lev]
        m = me[lev]
        buf = gath_bufs[lev]
        if lev == n_lev - 1:
            piece = buf.at[m]
        else:
            piece = gath_bufs[lev + 1]
            own = pltpu.make_async_copy(piece, buf.at[m], local_sem.at[0])
            own.start()
            own.wait()
        copies = []
        for off in range(1, n):
            j = lax.rem(m + off, n)
            cp = pltpu.make_async_remote_copy(
                src_ref=piece, dst_ref=buf.at[m],
                send_sem=ag_send[lev].at[off], recv_sem=ag_recv[lev].at[m],
                device_id=_peer(levels[lev], j), device_id_type=pl.DeviceIdType.MESH)
            cp.start()
            copies.append((j, off, cp))
        for j, off, cp in copies:
            pltpu.make_async_remote_copy(
                src_ref=piece, dst_ref=buf.at[j],
                send_sem=ag_send[lev].at[off], recv_sem=ag_recv[lev].at[j],
                device_id=_peer(levels[lev], j), device_id_type=pl.DeviceIdType.MESH).wait_recv()
        for j, off, cp in copies:
            cp.wait_send()


def allreduce(x, levels, collective_id):
    shape = x.shape
    total = x.size
    counts = [n for _, n, _ in levels]
    per = total
    for n in counts:
        per //= n
    rows = per // LANES
    full = tuple(counts) + (rows, LANES)
    xr = x.reshape(full)
    scratch = []
    for lev in range(len(levels)):
        scratch.append(pltpu.VMEM(full[lev:], jnp.float32))
    for lev in range(len(levels) - 1):
        scratch.append(pltpu.VMEM(full[lev + 1:], jnp.float32))
    for lev in range(len(levels) - 1):
        scratch.append(pltpu.VMEM(full[lev + 1:], jnp.float32))
    for _ in range(4):
        for _, n, _ in levels:
            scratch.append(pltpu.SemaphoreType.DMA((n,)))
    scratch.append(pltpu.SemaphoreType.DMA((1,)))
    out = pl.pallas_call(
        functools.partial(_allreduce_kernel, tuple(levels)),
        out_shape=jax.ShapeDtypeStruct(full, jnp.float32),
        in_specs=[pl.BlockSpec(memory_space=pltpu.VMEM)],
        out_specs=pl.BlockSpec(memory_space=pltpu.VMEM),
        scratch_shapes=scratch,
        compiler_params=pltpu.CompilerParams(collective_id=collective_id, has_side_effects=True),
        cost_estimate=pl.CostEstimate(flops=total * 2, bytes_accessed=total * 4 * 4, transcendentals=0),
    )(xr)
    return out.reshape(shape)


def _update_kernel(x_ref, mom_ref, master_ref, mom_out, master_out,
                   rows_buf, send1, recv1, local_sem):
    n, rows, cols = x_ref.shape
    me = lax.axis_index("tp")
    barrier = pltpu.get_barrier_semaphore()
    for off in range(1, n):
        j = lax.rem(me + off, n)
        pl.semaphore_signal(barrier, inc=1, device_id=_peer(("tp", n, 1), j),
                            device_id_type=pl.DeviceIdType.MESH)
    pl.semaphore_wait(barrier, n - 1)

    def to_rows(j, src):
        return pltpu.make_async_remote_copy(
            src_ref=src, dst_ref=rows_buf.at[:, pl.ds(pl.multiple_of(me * cols, cols), cols)],
            send_sem=send1.at[j], recv_sem=recv1.at[me],
            device_id=_peer(("tp", n, 1), j), device_id_type=pl.DeviceIdType.MESH)

    copies = []
    for off in range(1, n):
        j = lax.rem(me + off, n)
        cp = to_rows(j, x_ref.at[j])
        cp.start()
        copies.append((j, cp))
    own = pltpu.make_async_copy(
        x_ref.at[me], rows_buf.at[:, pl.ds(pl.multiple_of(me * cols, cols), cols)], local_sem.at[0])
    own.start()
    own.wait()
    for j, cp in copies:
        pltpu.make_async_remote_copy(
            src_ref=x_ref.at[j], dst_ref=rows_buf.at[:, pl.ds(pl.multiple_of(j * cols, cols), cols)],
            send_sem=send1.at[j], recv_sem=recv1.at[j],
            device_id=_peer(("tp", n, 1), j), device_id_type=pl.DeviceIdType.MESH).wait_recv()
    for j, cp in copies:
        cp.wait_send()

    new_mom = MOMENTUM_DECAY * mom_ref[...] + rows_buf[...]
    new_master = master_ref[...] - LEARNING_RATE * new_mom
    mom_out[...] = new_mom
    master_out[...] = new_master


def _columns_kernel(x_ref, cols_out, send, recv, local_sem):
    n, rows, cols = cols_out.shape
    me = lax.axis_index("tp")
    barrier = pltpu.get_barrier_semaphore()
    for off in range(1, n):
        j = lax.rem(me + off, n)
        pl.semaphore_signal(barrier, inc=1, device_id=_peer(("tp", n, 1), j),
                            device_id_type=pl.DeviceIdType.MESH)
    pl.semaphore_wait(barrier, n - 1)

    def block(j):
        return x_ref.at[:, pl.ds(pl.multiple_of(j * cols, cols), cols)]

    copies = []
    for off in range(1, n):
        j = lax.rem(me + off, n)
        cp = pltpu.make_async_remote_copy(
            src_ref=block(j), dst_ref=cols_out.at[me],
            send_sem=send.at[j], recv_sem=recv.at[me],
            device_id=_peer(("tp", n, 1), j), device_id_type=pl.DeviceIdType.MESH)
        cp.start()
        copies.append((j, cp))
    own = pltpu.make_async_copy(block(me), cols_out.at[me], local_sem.at[0])
    own.start()
    own.wait()
    for j, cp in copies:
        pltpu.make_async_remote_copy(
            src_ref=block(j), dst_ref=cols_out.at[j],
            send_sem=send.at[j], recv_sem=recv.at[j],
            device_id=_peer(("tp", n, 1), j), device_id_type=pl.DeviceIdType.MESH).wait_recv()
    for j, cp in copies:
        cp.wait_send()


def by_columns(x, n, collective_id):
    rows, width = x.shape
    cols = width // n
    vmem = pl.BlockSpec(memory_space=pltpu.VMEM)
    return pl.pallas_call(
        _columns_kernel,
        out_shape=jax.ShapeDtypeStruct((n, rows, cols), x.dtype),
        in_specs=[vmem],
        out_specs=vmem,
        scratch_shapes=[
            pltpu.SemaphoreType.DMA((n,)),
            pltpu.SemaphoreType.DMA((n,)),
            pltpu.SemaphoreType.DMA((1,)),
        ],
        compiler_params=pltpu.CompilerParams(collective_id=collective_id, has_side_effects=True),
        cost_estimate=pl.CostEstimate(flops=0, bytes_accessed=2 * x.size * x.dtype.itemsize,
                                      transcendentals=0),
    )(x)


def flat_update(own_block, momentum, master, n, collective_id):
    block_rows, cols = own_block.shape
    rows = block_rows // n
    x = own_block.reshape(n, rows, cols)
    f32 = jnp.float32
    vmem = pl.BlockSpec(memory_space=pltpu.VMEM)
    return pl.pallas_call(
        _update_kernel,
        out_shape=(
            jax.ShapeDtypeStruct(momentum.shape, f32),
            jax.ShapeDtypeStruct(master.shape, f32),
        ),
        in_specs=[vmem, vmem, vmem],
        out_specs=(vmem, vmem),
        scratch_shapes=[
            pltpu.VMEM((rows, n * cols), f32),
            pltpu.SemaphoreType.DMA((n,)),
            pltpu.SemaphoreType.DMA((n,)),
            pltpu.SemaphoreType.DMA((1,)),
        ],
        compiler_params=pltpu.CompilerParams(collective_id=collective_id, has_side_effects=True),
        cost_estimate=pl.CostEstimate(flops=4 * momentum.size, bytes_accessed=5 * 4 * momentum.size,
                                      transcendentals=0),
    )(x, momentum, master)


def split_levels(name, size, inner):
    if size % inner or size == inner:
        return ((name, size, 1),)
    if inner == 2:
        return ((name, inner, 1), (name, size // inner, inner))
    return ((name, size // inner, inner), (name, inner, 1))


def orthonormal_by_gram(factor):
    hi = lax.Precision.HIGHEST
    gram_now = local_gram(factor)
    rank = factor.shape[1]
    eye = jnp.eye(rank, dtype=factor.dtype)
    sum_squares = jnp.trace(gram_now, axis1=1, axis2=2)[:, None, None]
    factor_scale = lax.rsqrt(sum_squares + NORM_EPSILON)
    gram_now = gram_now * (factor_scale * factor_scale)
    mixing = None
    for iteration in range(NS_STEPS):
        step = 1.5 * eye - 0.5 * gram_now
        mixing = step if mixing is None else jnp.einsum("krs,kst->krt", step, mixing, precision=hi)
        if iteration < NS_STEPS - 1:
            gram_now = jnp.einsum(
                "krs,kst,kut->kru", step, gram_now, step, precision=hi)
    return jnp.einsum("krs,ksd->krd", mixing * factor_scale, factor, precision=hi)


def local_gram(factor):
    return jnp.einsum("krd,ksd->krs", factor, factor, precision=lax.Precision.HIGHEST)


def orthonormal(factor, gram_of):
    gram_now = gram_of(factor)
    sum_squares = jnp.trace(gram_now, axis1=1, axis2=2)[:, None, None]
    factor_scale = lax.rsqrt(sum_squares + NORM_EPSILON)
    ortho_basis = factor * factor_scale
    gram_now = gram_now * (factor_scale * factor_scale)
    for iteration in range(NS_STEPS):
        if iteration > 0:
            gram_now = gram_of(ortho_basis)
        ortho_basis = 1.5 * ortho_basis - 0.5 * jnp.einsum(
            "krs,ksd->krd", gram_now, ortho_basis, precision=lax.Precision.HIGHEST
        )
    return ortho_basis


def local(grads, error, query, momentum, master):
    corrected = grads[0].astype(jnp.float32) + error[0]
    current = query
    replicas = lax.axis_size("rep")
    tensor = lax.axis_size("tp")
    kept = master - LEARNING_RATE * (MOMENTUM_DECAY * momentum)
    kept_cols = by_columns(kept, tensor, 3)
    kept_cols = kept_cols.reshape(-1, kept_cols.shape[-1])
    kept_all = lax.all_gather(kept_cols, "rep", axis=0, tiled=True)
    rep_only = (("rep", replicas, 1),)
    both = split_levels("tp", lax.axis_size("tp"), 2) + split_levels("rep", replicas, 4)
    for power_pass in range(ROUNDS):
        partial_factor = jnp.einsum(
            "kdf,krf->krd", corrected, current, precision=lax.Precision.HIGHEST
        )
        summed = allreduce(partial_factor, both, 0)
        ortho_basis = orthonormal_by_gram(summed)
        partial_query = jnp.einsum(
            "kdf,krd->krf", corrected, ortho_basis, precision=lax.Precision.HIGHEST
        )
        current = allreduce(partial_query, rep_only, 1) / replicas
    approx = jnp.einsum("krd,krf->kdf", ortho_basis, current, precision=lax.Precision.HIGHEST)
    new_error = (corrected - approx)[None]
    matrices, model_width, shard_cols = approx.shape
    weights = (kept_all.reshape(approx.shape) - LEARNING_RATE * approx).astype(jnp.bfloat16)
    block_rows = matrices * model_width // replicas
    span = min(matrices, -(-block_rows // model_width) + 1)
    first_row = lax.axis_index("rep") * block_rows
    first_mat = jnp.minimum(first_row // model_width, matrices - span)
    pair = jnp.einsum(
        "krd,krf->kdf",
        lax.dynamic_slice_in_dim(ortho_basis, first_mat, span, 0),
        lax.dynamic_slice_in_dim(current, first_mat, span, 0),
        precision=lax.Precision.HIGHEST,
    ).reshape(span * model_width, shard_cols)
    own_block = lax.dynamic_slice_in_dim(
        pair, first_row - first_mat * model_width, block_rows, 0
    )
    new_momentum, new_master = flat_update(own_block, momentum, master, tensor, 2)
    return (new_error, current, new_momentum, new_master, weights)


def solution(mesh):
    placed = (
        P("rep", None, None, "tp"),
        P("rep", None, None, "tp"),
        P(None, None, "tp"),
        P(("rep", "tp"), None),
        P(("rep", "tp"), None),
    )
    return jax.shard_map(
        local,
        mesh=mesh,
        in_specs=placed,
        out_specs=(
            P("rep", None, None, "tp"),
            P(None, None, "tp"),
            P(("rep", "tp"), None),
            P(("rep", "tp"), None),
            P(None, None, "tp"),
        ),
        check_vma=False,
    )
```

```python
import functools

import jax
import jax.numpy as jnp
from jax import lax
from jax.experimental import pallas as pl
from jax.experimental.pallas import tpu as pltpu
from jax.sharding import PartitionSpec as P

ROUNDS = 2
NS_STEPS = 5


NORM_EPSILON = 1e-06
MOMENTUM_DECAY = 0.9
LEARNING_RATE = 0.5

MESH_AXES = ("rep", "tp")
LANES = 128


def _coord(level):
    name, n, stride = level
    return lax.rem(lax.div(lax.axis_index(name), stride), n)


def _peer(level, j):
    name, n, stride = level
    base = lax.axis_index(name) + (j - _coord(level)) * stride
    return tuple(base if axis == name else lax.axis_index(axis) for axis in MESH_AXES)


def _chunk(region, splits, j):
    new = list(region)
    rest = j
    for dim, parts in reversed(splits):
        if isinstance(rest, int):
            q, rest = rest % parts, rest // parts
        else:
            q, rest = lax.rem(rest, parts), lax.div(rest, parts)
        start, size = new[dim]
        new[dim] = (start + q * (size // parts), size // parts)
    return tuple(new)


def _at(ref, region):
    index = []
    for start, size in region:
        if not isinstance(start, int) and size % LANES == 0:
            start = pl.multiple_of(start, LANES)
        index.append(pl.ds(start, size))
    return ref.at[tuple(index)]


def _whole(shape):
    return tuple((0, size) for size in shape)


def _sum_into(dst, recv, n):
    def body(i, carry):
        acc = recv[0, i]
        for j in range(1, n):
            acc = acc + recv[j, i]
        dst[i] = acc
        return carry
    lax.fori_loop(0, recv.shape[1], body, 0)


def _allreduce_kernel(levels, direct, x_ref, o_ref, *scratch):
    n_lev = len(levels)
    it = iter(scratch)
    recv = [next(it) for _ in range(n_lev)]
    sums = [next(it) for _ in range(n_lev - 1)]
    rs_send = [next(it) for _ in range(n_lev)]
    rs_recv = [next(it) for _ in range(n_lev)]
    ag_send = [next(it) for _ in range(n_lev)]
    ag_recv = [next(it) for _ in range(n_lev)]
    local_sem = next(it)

    me = [_coord(level[:3]) for level in levels]
    mesh_id = pl.DeviceIdType.MESH

    barrier = pltpu.get_barrier_semaphore()
    total_peers = 0
    for lev, level in enumerate(levels):
        n = level[1]
        for off in range(1, n):
            j = lax.rem(me[lev] + off, n)
            pl.semaphore_signal(barrier, inc=1, device_id=_peer(level[:3], j), device_id_type=mesh_id)
        total_peers += n - 1
    pl.semaphore_wait(barrier, total_peers)

    src = x_ref
    regions = [_whole(x_ref.shape)]
    for lev, level in enumerate(levels):
        n, splits = level[1], level[3]
        m = me[lev]
        last_direct = direct and lev == n_lev - 1

        def piece(j):
            return src if last_direct else _at(src, _chunk(_whole(src.shape), splits, j))

        copies = []
        for off in range(1, n):
            j = lax.rem(m + off, n)
            cp = pltpu.make_async_remote_copy(
                src_ref=piece(j), dst_ref=recv[lev].at[m],
                send_sem=rs_send[lev].at[off], recv_sem=rs_recv[lev].at[m],
                device_id=_peer(level[:3], j), device_id_type=mesh_id)
            cp.start()
            copies.append((j, off, cp))
        own = pltpu.make_async_copy(piece(m), recv[lev].at[m], local_sem.at[0])
        own.start()
        own.wait()
        for j, off, cp in copies:
            pltpu.make_async_remote_copy(
                src_ref=piece(j), dst_ref=recv[lev].at[j],
                send_sem=rs_send[lev].at[off], recv_sem=rs_recv[lev].at[j],
                device_id=_peer(level[:3], j), device_id_type=mesh_id).wait_recv()
        for j, off, cp in copies:
            cp.wait_send()
        if not last_direct:
            regions.append(_chunk(regions[-1], splits, m))
        if lev < n_lev - 1:
            dst = sums[lev]
        else:
            dst = _at(o_ref, regions[-1])
        _sum_into(dst, recv[lev], n)
        src = dst

    gather_levels = n_lev - 1 if direct else n_lev
    for lev in reversed(range(gather_levels)):
        level = levels[lev]
        n, splits = level[1], level[3]
        m = me[lev]
        mine = _at(o_ref, regions[lev + 1])
        copies = []
        for off in range(1, n):
            j = lax.rem(m + off, n)
            cp = pltpu.make_async_remote_copy(
                src_ref=mine, dst_ref=mine,
                send_sem=ag_send[lev].at[off], recv_sem=ag_recv[lev].at[m],
                device_id=_peer(level[:3], j), device_id_type=mesh_id)
            cp.start()
            copies.append((j, off, cp))
        for j, off, cp in copies:
            theirs = _at(o_ref, _chunk(regions[lev], splits, j))
            pltpu.make_async_remote_copy(
                src_ref=mine, dst_ref=theirs,
                send_sem=ag_send[lev].at[off], recv_sem=ag_recv[lev].at[j],
                device_id=_peer(level[:3], j), device_id_type=mesh_id).wait_recv()
        for j, off, cp in copies:
            cp.wait_send()


def allreduce(x, levels, direct, collective_id):
    shapes = [x.shape]
    for lev, (_, n, _, splits) in enumerate(levels):
        if direct and lev == len(levels) - 1:
            break
        shape = list(shapes[-1])
        for dim, parts in splits:
            assert shape[dim] % parts == 0
            shape[dim] //= parts
        shapes.append(tuple(shape))
    scratch = []
    for lev, (_, n, _, _) in enumerate(levels):
        scratch.append(pltpu.VMEM((n,) + shapes[min(lev + 1, len(shapes) - 1)], jnp.float32))
    for lev in range(len(levels) - 1):
        scratch.append(pltpu.VMEM(shapes[lev + 1], jnp.float32))
    for _ in range(4):
        for _, n, _, _ in levels:
            scratch.append(pltpu.SemaphoreType.DMA((n,)))
    scratch.append(pltpu.SemaphoreType.DMA((1,)))
    total = x.size
    return pl.pallas_call(
        functools.partial(_allreduce_kernel, tuple(levels), direct),
        out_shape=jax.ShapeDtypeStruct(x.shape, jnp.float32),
        in_specs=[pl.BlockSpec(memory_space=pltpu.VMEM)],
        out_specs=pl.BlockSpec(memory_space=pltpu.VMEM),
        scratch_shapes=scratch,
        compiler_params=pltpu.CompilerParams(collective_id=collective_id, has_side_effects=True),
        cost_estimate=pl.CostEstimate(flops=total * 2, bytes_accessed=total * 4 * 4, transcendentals=0),
    )(x)

def _update_kernel(x_ref, mom_ref, master_ref, mom_out, master_out,
                   rows_buf, send1, recv1, local_sem):
    n, rows, cols = x_ref.shape
    me = lax.axis_index("tp")
    barrier = pltpu.get_barrier_semaphore()
    for off in range(1, n):
        j = lax.rem(me + off, n)
        pl.semaphore_signal(barrier, inc=1, device_id=_peer(("tp", n, 1), j),
                            device_id_type=pl.DeviceIdType.MESH)
    pl.semaphore_wait(barrier, n - 1)

    def to_rows(j, src):
        return pltpu.make_async_remote_copy(
            src_ref=src, dst_ref=rows_buf.at[:, pl.ds(pl.multiple_of(me * cols, cols), cols)],
            send_sem=send1.at[j], recv_sem=recv1.at[me],
            device_id=_peer(("tp", n, 1), j), device_id_type=pl.DeviceIdType.MESH)

    copies = []
    for off in range(1, n):
        j = lax.rem(me + off, n)
        cp = to_rows(j, x_ref.at[j])
        cp.start()
        copies.append((j, cp))
    own = pltpu.make_async_copy(
        x_ref.at[me], rows_buf.at[:, pl.ds(pl.multiple_of(me * cols, cols), cols)], local_sem.at[0])
    own.start()
    own.wait()
    for j, cp in copies:
        pltpu.make_async_remote_copy(
            src_ref=x_ref.at[j], dst_ref=rows_buf.at[:, pl.ds(pl.multiple_of(j * cols, cols), cols)],
            send_sem=send1.at[j], recv_sem=recv1.at[j],
            device_id=_peer(("tp", n, 1), j), device_id_type=pl.DeviceIdType.MESH).wait_recv()
    for j, cp in copies:
        cp.wait_send()

    new_mom = MOMENTUM_DECAY * mom_ref[...] + rows_buf[...]
    new_master = master_ref[...] - LEARNING_RATE * new_mom
    mom_out[...] = new_mom
    master_out[...] = new_master


def _columns_kernel(x_ref, cols_out, send, recv, local_sem):
    n, rows, cols = cols_out.shape
    me = lax.axis_index("tp")
    barrier = pltpu.get_barrier_semaphore()
    for off in range(1, n):
        j = lax.rem(me + off, n)
        pl.semaphore_signal(barrier, inc=1, device_id=_peer(("tp", n, 1), j),
                            device_id_type=pl.DeviceIdType.MESH)
    pl.semaphore_wait(barrier, n - 1)

    def block(j):
        return x_ref.at[:, pl.ds(pl.multiple_of(j * cols, cols), cols)]

    copies = []
    for off in range(1, n):
        j = lax.rem(me + off, n)
        cp = pltpu.make_async_remote_copy(
            src_ref=block(j), dst_ref=cols_out.at[me],
            send_sem=send.at[j], recv_sem=recv.at[me],
            device_id=_peer(("tp", n, 1), j), device_id_type=pl.DeviceIdType.MESH)
        cp.start()
        copies.append((j, cp))
    own = pltpu.make_async_copy(block(me), cols_out.at[me], local_sem.at[0])
    own.start()
    own.wait()
    for j, cp in copies:
        pltpu.make_async_remote_copy(
            src_ref=block(j), dst_ref=cols_out.at[j],
            send_sem=send.at[j], recv_sem=recv.at[j],
            device_id=_peer(("tp", n, 1), j), device_id_type=pl.DeviceIdType.MESH).wait_recv()
    for j, cp in copies:
        cp.wait_send()


def by_columns(x, n, collective_id):
    rows, width = x.shape
    cols = width // n
    vmem = pl.BlockSpec(memory_space=pltpu.VMEM)
    return pl.pallas_call(
        _columns_kernel,
        out_shape=jax.ShapeDtypeStruct((n, rows, cols), x.dtype),
        in_specs=[vmem],
        out_specs=vmem,
        scratch_shapes=[
            pltpu.SemaphoreType.DMA((n,)),
            pltpu.SemaphoreType.DMA((n,)),
            pltpu.SemaphoreType.DMA((1,)),
        ],
        compiler_params=pltpu.CompilerParams(collective_id=collective_id, has_side_effects=True),
        cost_estimate=pl.CostEstimate(flops=0, bytes_accessed=2 * x.size * x.dtype.itemsize,
                                      transcendentals=0),
    )(x)


def flat_update(own_block, momentum, master, n, collective_id):
    block_rows, cols = own_block.shape
    rows = block_rows // n
    x = own_block.reshape(n, rows, cols)
    f32 = jnp.float32
    vmem = pl.BlockSpec(memory_space=pltpu.VMEM)
    return pl.pallas_call(
        _update_kernel,
        out_shape=(
            jax.ShapeDtypeStruct(momentum.shape, f32),
            jax.ShapeDtypeStruct(master.shape, f32),
        ),
        in_specs=[vmem, vmem, vmem],
        out_specs=(vmem, vmem),
        scratch_shapes=[
            pltpu.VMEM((rows, n * cols), f32),
            pltpu.SemaphoreType.DMA((n,)),
            pltpu.SemaphoreType.DMA((n,)),
            pltpu.SemaphoreType.DMA((1,)),
        ],
        compiler_params=pltpu.CompilerParams(collective_id=collective_id, has_side_effects=True),
        cost_estimate=pl.CostEstimate(flops=4 * momentum.size, bytes_accessed=5 * 4 * momentum.size,
                                      transcendentals=0),
    )(x, momentum, master)


def left_plan(query_shape, tensor, replicas):
    mats, rank = query_shape[0], query_shape[1]
    if tensor % 2 or replicas % 4 or mats % (replicas // 4) or rank % (8 * (tensor // 2)):
        return ((("tp", tensor, 1, ((1, tensor),)), ("rep", replicas, 1, ((0, 1),))), True)
    return ((
        ("tp", 2, 1, ((2, 2),)),
        ("tp", tensor // 2, 2, ((1, tensor // 2),)),
        ("rep", replicas // 4, 4, ((0, replicas // 4),)),
        ("rep", 4, 1, ()),
    ), True)


def right_splits(query_shape, replicas):
    mats, rank = query_shape[0], query_shape[1]
    for k_parts in range(1, replicas + 1):
        r_parts = replicas // k_parts
        if replicas % k_parts == 0 and mats % k_parts == 0 and rank % (8 * r_parts) == 0:
            return ((0, k_parts), (1, r_parts))
    return ((0, 1),)


def split_levels(name, size, inner):
    if size % inner or size == inner:
        return ((name, size, 1),)
    if inner == 2:
        return ((name, inner, 1), (name, size // inner, inner))
    return ((name, size // inner, inner), (name, inner, 1))


def orthonormal_by_gram(factor):
    hi = lax.Precision.HIGHEST
    gram_now = local_gram(factor)
    rank = factor.shape[1]
    eye = jnp.eye(rank, dtype=factor.dtype)
    sum_squares = jnp.trace(gram_now, axis1=1, axis2=2)[:, None, None]
    factor_scale = lax.rsqrt(sum_squares + NORM_EPSILON)
    gram_now = gram_now * (factor_scale * factor_scale)
    mixing = None
    for iteration in range(NS_STEPS):
        step = 1.5 * eye - 0.5 * gram_now
        mixing = step if mixing is None else jnp.einsum("krs,kst->krt", step, mixing, precision=hi)
        if iteration < NS_STEPS - 1:
            gram_now = jnp.einsum(
                "krs,kst,kut->kru", step, gram_now, step, precision=hi)
    return jnp.einsum("krs,ksd->krd", mixing * factor_scale, factor, precision=hi)


def local_gram(factor):
    return jnp.einsum("krd,ksd->krs", factor, factor, precision=lax.Precision.HIGHEST)


def orthonormal(factor, gram_of):
    gram_now = gram_of(factor)
    sum_squares = jnp.trace(gram_now, axis1=1, axis2=2)[:, None, None]
    factor_scale = lax.rsqrt(sum_squares + NORM_EPSILON)
    ortho_basis = factor * factor_scale
    gram_now = gram_now * (factor_scale * factor_scale)
    for iteration in range(NS_STEPS):
        if iteration > 0:
            gram_now = gram_of(ortho_basis)
        ortho_basis = 1.5 * ortho_basis - 0.5 * jnp.einsum(
            "krs,ksd->krd", gram_now, ortho_basis, precision=lax.Precision.HIGHEST
        )
    return ortho_basis


def local(grads, error, query, momentum, master):
    corrected = grads[0].astype(jnp.float32) + error[0]
    current = query
    replicas = lax.axis_size("rep")
    tensor = lax.axis_size("tp")
    kept = master - LEARNING_RATE * (MOMENTUM_DECAY * momentum)
    kept_cols = by_columns(kept, tensor, 3)
    kept_cols = kept_cols.reshape(-1, kept_cols.shape[-1])
    kept_all = lax.all_gather(kept_cols, "rep", axis=0, tiled=True)
    left_levels, left_direct = left_plan(query.shape, tensor, replicas)
    right_levels = (("rep", replicas, 1, right_splits(query.shape, replicas)),)
    for power_pass in range(ROUNDS):
        partial_factor = jnp.einsum(
            "kdf,krf->krd", corrected, current, precision=lax.Precision.HIGHEST
        )
        summed = allreduce(partial_factor, left_levels, left_direct, 0)
        ortho_basis = orthonormal_by_gram(summed)
        partial_query = jnp.einsum(
            "kdf,krd->krf", corrected, ortho_basis, precision=lax.Precision.HIGHEST
        )
        current = allreduce(partial_query, right_levels, False, 1) / replicas
    approx = jnp.einsum("krd,krf->kdf", ortho_basis, current, precision=lax.Precision.HIGHEST)
    new_error = (corrected - approx)[None]
    matrices, model_width, shard_cols = approx.shape
    weights = (kept_all.reshape(approx.shape) - LEARNING_RATE * approx).astype(jnp.bfloat16)
    block_rows = matrices * model_width // replicas
    span = min(matrices, -(-block_rows // model_width) + 1)
    first_row = lax.axis_index("rep") * block_rows
    first_mat = jnp.minimum(first_row // model_width, matrices - span)
    pair = jnp.einsum(
        "krd,krf->kdf",
        lax.dynamic_slice_in_dim(ortho_basis, first_mat, span, 0),
        lax.dynamic_slice_in_dim(current, first_mat, span, 0),
        precision=lax.Precision.HIGHEST,
    ).reshape(span * model_width, shard_cols)
    own_block = lax.dynamic_slice_in_dim(
        pair, first_row - first_mat * model_width, block_rows, 0
    )
    new_momentum, new_master = flat_update(own_block, momentum, master, tensor, 2)
    return (new_error, current, new_momentum, new_master, weights)


def solution(mesh):
    placed = (
        P("rep", None, None, "tp"),
        P("rep", None, None, "tp"),
        P(None, None, "tp"),
        P(("rep", "tp"), None),
        P(("rep", "tp"), None),
    )
    return jax.shard_map(
        local,
        mesh=mesh,
        in_specs=placed,
        out_specs=(
            P("rep", None, None, "tp"),
            P(None, None, "tp"),
            P(("rep", "tp"), None),
            P(("rep", "tp"), None),
            P(None, None, "tp"),
        ),
        check_vma=False,
    )
```

```python
import functools

import jax
import jax.numpy as jnp
from jax import lax
from jax.experimental import pallas as pl
from jax.experimental.pallas import tpu as pltpu
from jax.sharding import PartitionSpec as P

ROUNDS = 2
NS_STEPS = 5


NORM_EPSILON = 1e-06
MOMENTUM_DECAY = 0.9
LEARNING_RATE = 0.5

MESH_AXES = ("rep", "tp")
LANES = 128


def _coord(level):
    name, n, stride = level
    return lax.rem(lax.div(lax.axis_index(name), stride), n)


def _peer(level, j):
    name, n, stride = level
    base = lax.axis_index(name) + (j - _coord(level)) * stride
    return tuple(base if axis == name else lax.axis_index(axis) for axis in MESH_AXES)


def _allreduce_kernel(levels, x_ref, o_ref, *scratch):
    n_lev = len(levels)
    it = iter(scratch)
    recv = [next(it) for _ in range(n_lev)]
    sums = [next(it) for _ in range(n_lev - 1)]
    gath = [next(it) for _ in range(n_lev - 1)] + [None]
    rs_send = [next(it) for _ in range(n_lev)]
    rs_recv = [next(it) for _ in range(n_lev)]
    ag_send = [next(it) for _ in range(n_lev)]
    ag_recv = [next(it) for _ in range(n_lev)]
    local_sem = next(it)

    me = [_coord(level) for level in levels]

    barrier = pltpu.get_barrier_semaphore()
    total_peers = 0
    for lev, (name, n, _) in enumerate(levels):
        for off in range(1, n):
            j = lax.rem(me[lev] + off, n)
            pl.semaphore_signal(barrier, inc=1, device_id=_peer(levels[lev], j),
                                device_id_type=pl.DeviceIdType.MESH)
        total_peers += n - 1
    pl.semaphore_wait(barrier, total_peers)

    gath_bufs = [o_ref] + gath[: n_lev - 1]

    src = x_ref
    for lev, (name, n, _) in enumerate(levels):
        m = me[lev]
        copies = []
        for off in range(1, n):
            j = lax.rem(m + off, n)
            cp = pltpu.make_async_remote_copy(
                src_ref=src.at[j], dst_ref=recv[lev].at[m],
                send_sem=rs_send[lev].at[off], recv_sem=rs_recv[lev].at[m],
                device_id=_peer(levels[lev], j), device_id_type=pl.DeviceIdType.MESH)
            cp.start()
            copies.append((j, off, cp))
        own = pltpu.make_async_copy(src.at[m], recv[lev].at[m], local_sem.at[0])
        own.start()
        own.wait()
        for j, off, cp in copies:
            pltpu.make_async_remote_copy(
                src_ref=src.at[j], dst_ref=recv[lev].at[j],
                send_sem=rs_send[lev].at[off], recv_sem=rs_recv[lev].at[j],
                device_id=_peer(levels[lev], j), device_id_type=pl.DeviceIdType.MESH).wait_recv()
        for j, off, cp in copies:
            cp.wait_send()
        r = recv[lev]
        if lev < n_lev - 1:
            dst = sums[lev]
        else:
            dst = gath_bufs[lev].at[m]
        if len(r.shape) > 3:
            lead = r.shape[1:-2]
            count = 1
            for d in lead:
                count *= d

            def body(i, carry, r=r, dst=dst, n=n, lead=lead):
                idx = []
                rest = i
                for d in reversed(lead):
                    idx.append(lax.rem(rest, d))
                    rest = lax.div(rest, d)
                idx = tuple(reversed(idx))
                acc = r[(0,) + idx]
                for j in range(1, n):
                    acc = acc + r[(j,) + idx]
                dst[idx] = acc
                return carry
            lax.fori_loop(0, count, body, 0)
        else:
            acc = r[0]
            for j in range(1, n):
                acc = acc + r[j]
            dst[...] = acc
        if lev < n_lev - 1:
            src = sums[lev]

    for lev in reversed(range(n_lev)):
        name, n, _ = levels[lev]
        m = me[lev]
        buf = gath_bufs[lev]
        if lev == n_lev - 1:
            piece = buf.at[m]
        else:
            piece = gath_bufs[lev + 1]
            own = pltpu.make_async_copy(piece, buf.at[m], local_sem.at[0])
            own.start()
            own.wait()
        copies = []
        for off in range(1, n):
            j = lax.rem(m + off, n)
            cp = pltpu.make_async_remote_copy(
                src_ref=piece, dst_ref=buf.at[m],
                send_sem=ag_send[lev].at[off], recv_sem=ag_recv[lev].at[m],
                device_id=_peer(levels[lev], j), device_id_type=pl.DeviceIdType.MESH)
            cp.start()
            copies.append((j, off, cp))
        for j, off, cp in copies:
            pltpu.make_async_remote_copy(
                src_ref=piece, dst_ref=buf.at[j],
                send_sem=ag_send[lev].at[off], recv_sem=ag_recv[lev].at[j],
                device_id=_peer(levels[lev], j), device_id_type=pl.DeviceIdType.MESH).wait_recv()
        for j, off, cp in copies:
            cp.wait_send()


def allreduce(x, levels, collective_id):
    shape = x.shape
    total = x.size
    counts = [n for _, n, _ in levels]
    per = total
    for n in counts:
        per //= n
    rows = per // LANES
    full = tuple(counts) + (rows, LANES)
    xr = x.reshape(full)
    scratch = []
    for lev in range(len(levels)):
        scratch.append(pltpu.VMEM(full[lev:], jnp.float32))
    for lev in range(len(levels) - 1):
        scratch.append(pltpu.VMEM(full[lev + 1:], jnp.float32))
    for lev in range(len(levels) - 1):
        scratch.append(pltpu.VMEM(full[lev + 1:], jnp.float32))
    for _ in range(4):
        for _, n, _ in levels:
            scratch.append(pltpu.SemaphoreType.DMA((n,)))
    scratch.append(pltpu.SemaphoreType.DMA((1,)))
    out = pl.pallas_call(
        functools.partial(_allreduce_kernel, tuple(levels)),
        out_shape=jax.ShapeDtypeStruct(full, jnp.float32),
        in_specs=[pl.BlockSpec(memory_space=pltpu.VMEM)],
        out_specs=pl.BlockSpec(memory_space=pltpu.VMEM),
        scratch_shapes=scratch,
        compiler_params=pltpu.CompilerParams(collective_id=collective_id, has_side_effects=True),
        cost_estimate=pl.CostEstimate(flops=total * 2, bytes_accessed=total * 4 * 4, transcendentals=0),
    )(xr)
    return out.reshape(shape)


def _update_kernel(x_ref, mom_ref, master_ref, mom_out, master_out,
                   rows_buf, send1, recv1, local_sem):
    n, rows, cols = x_ref.shape
    me = lax.axis_index("tp")
    barrier = pltpu.get_barrier_semaphore()
    for off in range(1, n):
        j = lax.rem(me + off, n)
        pl.semaphore_signal(barrier, inc=1, device_id=_peer(("tp", n, 1), j),
                            device_id_type=pl.DeviceIdType.MESH)
    pl.semaphore_wait(barrier, n - 1)

    def to_rows(j, src):
        return pltpu.make_async_remote_copy(
            src_ref=src, dst_ref=rows_buf.at[:, pl.ds(pl.multiple_of(me * cols, cols), cols)],
            send_sem=send1.at[j], recv_sem=recv1.at[me],
            device_id=_peer(("tp", n, 1), j), device_id_type=pl.DeviceIdType.MESH)

    copies = []
    for off in range(1, n):
        j = lax.rem(me + off, n)
        cp = to_rows(j, x_ref.at[j])
        cp.start()
        copies.append((j, cp))
    own = pltpu.make_async_copy(
        x_ref.at[me], rows_buf.at[:, pl.ds(pl.multiple_of(me * cols, cols), cols)], local_sem.at[0])
    own.start()
    own.wait()
    for j, cp in copies:
        pltpu.make_async_remote_copy(
            src_ref=x_ref.at[j], dst_ref=rows_buf.at[:, pl.ds(pl.multiple_of(j * cols, cols), cols)],
            send_sem=send1.at[j], recv_sem=recv1.at[j],
            device_id=_peer(("tp", n, 1), j), device_id_type=pl.DeviceIdType.MESH).wait_recv()
    for j, cp in copies:
        cp.wait_send()

    new_mom = MOMENTUM_DECAY * mom_ref[...] + rows_buf[...]
    new_master = master_ref[...] - LEARNING_RATE * new_mom
    mom_out[...] = new_mom
    master_out[...] = new_master


def _columns_kernel(x_ref, cols_out, send, recv, local_sem):
    n, rows, cols = cols_out.shape
    me = lax.axis_index("tp")
    barrier = pltpu.get_barrier_semaphore()
    for off in range(1, n):
        j = lax.rem(me + off, n)
        pl.semaphore_signal(barrier, inc=1, device_id=_peer(("tp", n, 1), j),
                            device_id_type=pl.DeviceIdType.MESH)
    pl.semaphore_wait(barrier, n - 1)

    def block(j):
        return x_ref.at[j]

    copies = []
    for off in range(1, n):
        j = lax.rem(me + off, n)
        cp = pltpu.make_async_remote_copy(
            src_ref=block(j), dst_ref=cols_out.at[me],
            send_sem=send.at[j], recv_sem=recv.at[me],
            device_id=_peer(("tp", n, 1), j), device_id_type=pl.DeviceIdType.MESH)
        cp.start()
        copies.append((j, cp))
    own = pltpu.make_async_copy(block(me), cols_out.at[me], local_sem.at[0])
    own.start()
    own.wait()
    for j, cp in copies:
        pltpu.make_async_remote_copy(
            src_ref=block(j), dst_ref=cols_out.at[j],
            send_sem=send.at[j], recv_sem=recv.at[j],
            device_id=_peer(("tp", n, 1), j), device_id_type=pl.DeviceIdType.MESH).wait_recv()
    for j, cp in copies:
        cp.wait_send()


def by_columns(x, n, collective_id):
    rows, width = x.shape
    cols = width // n
    x = x.reshape(rows, n, cols).transpose(1, 0, 2)
    vmem = pl.BlockSpec(memory_space=pltpu.VMEM)
    return pl.pallas_call(
        _columns_kernel,
        out_shape=jax.ShapeDtypeStruct((n, rows, cols), x.dtype),
        in_specs=[vmem],
        out_specs=vmem,
        scratch_shapes=[
            pltpu.SemaphoreType.DMA((n,)),
            pltpu.SemaphoreType.DMA((n,)),
            pltpu.SemaphoreType.DMA((1,)),
        ],
        compiler_params=pltpu.CompilerParams(collective_id=collective_id, has_side_effects=True),
        cost_estimate=pl.CostEstimate(flops=0, bytes_accessed=2 * x.size * x.dtype.itemsize,
                                      transcendentals=0),
    )(x)


def flat_update(own_block, momentum, master, n, collective_id):
    block_rows, cols = own_block.shape
    rows = block_rows // n
    x = own_block.reshape(n, rows, cols)
    f32 = jnp.float32
    vmem = pl.BlockSpec(memory_space=pltpu.VMEM)
    return pl.pallas_call(
        _update_kernel,
        out_shape=(
            jax.ShapeDtypeStruct(momentum.shape, f32),
            jax.ShapeDtypeStruct(master.shape, f32),
        ),
        in_specs=[vmem, vmem, vmem],
        out_specs=(vmem, vmem),
        scratch_shapes=[
            pltpu.VMEM((rows, n * cols), f32),
            pltpu.SemaphoreType.DMA((n,)),
            pltpu.SemaphoreType.DMA((n,)),
            pltpu.SemaphoreType.DMA((1,)),
        ],
        compiler_params=pltpu.CompilerParams(collective_id=collective_id, has_side_effects=True),
        cost_estimate=pl.CostEstimate(flops=4 * momentum.size, bytes_accessed=5 * 4 * momentum.size,
                                      transcendentals=0),
    )(x, momentum, master)


def split_levels(name, size, inner):
    if size % inner or size == inner:
        return ((name, size, 1),)
    if inner == 2:
        return ((name, inner, 1), (name, size // inner, inner))
    return ((name, size // inner, inner), (name, inner, 1))


def orthonormal_by_gram(factor):
    hi = lax.Precision.HIGHEST
    gram_now = local_gram(factor)
    rank = factor.shape[1]
    eye = jnp.eye(rank, dtype=factor.dtype)
    sum_squares = jnp.trace(gram_now, axis1=1, axis2=2)[:, None, None]
    factor_scale = lax.rsqrt(sum_squares + NORM_EPSILON)
    gram_now = gram_now * (factor_scale * factor_scale)
    mixing = None
    for iteration in range(NS_STEPS):
        step = 1.5 * eye - 0.5 * gram_now
        mixing = step if mixing is None else jnp.einsum("krs,kst->krt", step, mixing, precision=hi)
        if iteration < NS_STEPS - 1:
            gram_now = jnp.einsum(
                "krs,kst,kut->kru", step, gram_now, step, precision=hi)
    return jnp.einsum("krs,ksd->krd", mixing * factor_scale, factor, precision=hi)


def local_gram(factor):
    return jnp.einsum("krd,ksd->krs", factor, factor, precision=lax.Precision.HIGHEST)


def orthonormal(factor, gram_of):
    gram_now = gram_of(factor)
    sum_squares = jnp.trace(gram_now, axis1=1, axis2=2)[:, None, None]
    factor_scale = lax.rsqrt(sum_squares + NORM_EPSILON)
    ortho_basis = factor * factor_scale
    gram_now = gram_now * (factor_scale * factor_scale)
    for iteration in range(NS_STEPS):
        if iteration > 0:
            gram_now = gram_of(ortho_basis)
        ortho_basis = 1.5 * ortho_basis - 0.5 * jnp.einsum(
            "krs,ksd->krd", gram_now, ortho_basis, precision=lax.Precision.HIGHEST
        )
    return ortho_basis


def local(grads, error, query, momentum, master):
    corrected = grads[0].astype(jnp.float32) + error[0]
    current = query
    replicas = lax.axis_size("rep")
    tensor = lax.axis_size("tp")
    kept = master - LEARNING_RATE * (MOMENTUM_DECAY * momentum)
    kept_cols = by_columns(kept, tensor, 3)
    kept_cols = kept_cols.reshape(-1, kept_cols.shape[-1])
    kept_all = lax.all_gather(kept_cols, "rep", axis=0, tiled=True)
    rep_only = (("rep", replicas, 1),)
    both = split_levels("tp", lax.axis_size("tp"), 2) + split_levels("rep", replicas, 4)
    for power_pass in range(ROUNDS):
        partial_factor = jnp.einsum(
            "kdf,krf->krd", corrected, current, precision=lax.Precision.HIGHEST
        )
        summed = allreduce(partial_factor, both, 0)
        ortho_basis = orthonormal_by_gram(summed)
        partial_query = jnp.einsum(
            "kdf,krd->krf", corrected, ortho_basis, precision=lax.Precision.HIGHEST
        )
        current = allreduce(partial_query, rep_only, 1) / replicas
    approx = jnp.einsum("krd,krf->kdf", ortho_basis, current, precision=lax.Precision.HIGHEST)
    new_error = (corrected - approx)[None]
    matrices, model_width, shard_cols = approx.shape
    weights = (kept_all.reshape(approx.shape) - LEARNING_RATE * approx).astype(jnp.bfloat16)
    block_rows = matrices * model_width // replicas
    span = min(matrices, -(-block_rows // model_width) + 1)
    first_row = lax.axis_index("rep") * block_rows
    first_mat = jnp.minimum(first_row // model_width, matrices - span)
    pair = jnp.einsum(
        "krd,krf->kdf",
        lax.dynamic_slice_in_dim(ortho_basis, first_mat, span, 0),
        lax.dynamic_slice_in_dim(current, first_mat, span, 0),
        precision=lax.Precision.HIGHEST,
    ).reshape(span * model_width, shard_cols)
    own_block = lax.dynamic_slice_in_dim(
        pair, first_row - first_mat * model_width, block_rows, 0
    )
    new_momentum, new_master = flat_update(own_block, momentum, master, tensor, 2)
    return (new_error, current, new_momentum, new_master, weights)


def solution(mesh):
    placed = (
        P("rep", None, None, "tp"),
        P("rep", None, None, "tp"),
        P(None, None, "tp"),
        P(("rep", "tp"), None),
        P(("rep", "tp"), None),
    )
    return jax.shard_map(
        local,
        mesh=mesh,
        in_specs=placed,
        out_specs=(
            P("rep", None, None, "tp"),
            P(None, None, "tp"),
            P(("rep", "tp"), None),
            P(("rep", "tp"), None),
            P(None, None, "tp"),
        ),
        check_vma=False,
    )
```

```python
import functools

import jax
import jax.numpy as jnp
from jax import lax
from jax.experimental import pallas as pl
from jax.experimental.pallas import tpu as pltpu
from jax.sharding import PartitionSpec as P

ROUNDS = 2
NS_STEPS = 5


NORM_EPSILON = 1e-06
MOMENTUM_DECAY = 0.9
LEARNING_RATE = 0.5

MESH_AXES = ("rep", "tp")
LANES = 128


def _coord(level):
    name, n, stride = level
    return lax.rem(lax.div(lax.axis_index(name), stride), n)


def _peer(level, j):
    name, n, stride = level
    base = lax.axis_index(name) + (j - _coord(level)) * stride
    return tuple(base if axis == name else lax.axis_index(axis) for axis in MESH_AXES)


def _allreduce_kernel(levels, direct, x_ref, o_ref, *scratch):
    n_lev = len(levels)
    it = iter(scratch)
    recv = [next(it) for _ in range(n_lev)]
    sums = [next(it) for _ in range(n_lev - 1)]
    gath = [next(it) for _ in range(n_lev - 1)] + [None]
    rs_send = [next(it) for _ in range(n_lev)]
    rs_recv = [next(it) for _ in range(n_lev)]
    ag_send = [next(it) for _ in range(n_lev)]
    ag_recv = [next(it) for _ in range(n_lev)]
    local_sem = next(it)

    me = [_coord(level) for level in levels]

    barrier = pltpu.get_barrier_semaphore()
    total_peers = 0
    for lev, (name, n, _) in enumerate(levels):
        for off in range(1, n):
            j = lax.rem(me[lev] + off, n)
            pl.semaphore_signal(barrier, inc=1, device_id=_peer(levels[lev], j),
                                device_id_type=pl.DeviceIdType.MESH)
        total_peers += n - 1
    pl.semaphore_wait(barrier, total_peers)

    gath_bufs = [o_ref] + gath[: n_lev - 1]

    src = x_ref
    for lev, (name, n, _) in enumerate(levels):
        m = me[lev]
        last_direct = direct and lev == n_lev - 1

        def piece(j, src=src, last_direct=last_direct):
            return src if last_direct else src.at[j]

        copies = []
        for off in range(1, n):
            j = lax.rem(m + off, n)
            cp = pltpu.make_async_remote_copy(
                src_ref=piece(j), dst_ref=recv[lev].at[m],
                send_sem=rs_send[lev].at[off], recv_sem=rs_recv[lev].at[m],
                device_id=_peer(levels[lev], j), device_id_type=pl.DeviceIdType.MESH)
            cp.start()
            copies.append((j, off, cp))
        own = pltpu.make_async_copy(piece(m), recv[lev].at[m], local_sem.at[0])
        own.start()
        own.wait()
        for j, off, cp in copies:
            pltpu.make_async_remote_copy(
                src_ref=piece(j), dst_ref=recv[lev].at[j],
                send_sem=rs_send[lev].at[off], recv_sem=rs_recv[lev].at[j],
                device_id=_peer(levels[lev], j), device_id_type=pl.DeviceIdType.MESH).wait_recv()
        for j, off, cp in copies:
            cp.wait_send()
        r = recv[lev]
        if lev < n_lev - 1:
            dst = sums[lev]
        elif last_direct:
            dst = gath_bufs[lev]
        else:
            dst = gath_bufs[lev].at[m]
        if len(r.shape) > 3:
            lead = r.shape[1:-2]
            count = 1
            for d in lead:
                count *= d

            def body(i, carry, r=r, dst=dst, n=n, lead=lead):
                idx = []
                rest = i
                for d in reversed(lead):
                    idx.append(lax.rem(rest, d))
                    rest = lax.div(rest, d)
                idx = tuple(reversed(idx))
                acc = r[(0,) + idx]
                for j in range(1, n):
                    acc = acc + r[(j,) + idx]
                dst[idx] = acc
                return carry
            lax.fori_loop(0, count, body, 0)
        else:
            acc = r[0]
            for j in range(1, n):
                acc = acc + r[j]
            dst[...] = acc
        if lev < n_lev - 1:
            src = sums[lev]

    for lev in reversed(range(n_lev - 1 if direct else n_lev)):
        name, n, _ = levels[lev]
        m = me[lev]
        buf = gath_bufs[lev]
        if lev == n_lev - 1:
            piece = buf.at[m]
        else:
            piece = gath_bufs[lev + 1]
            own = pltpu.make_async_copy(piece, buf.at[m], local_sem.at[0])
            own.start()
            own.wait()
        copies = []
        for off in range(1, n):
            j = lax.rem(m + off, n)
            cp = pltpu.make_async_remote_copy(
                src_ref=piece, dst_ref=buf.at[m],
                send_sem=ag_send[lev].at[off], recv_sem=ag_recv[lev].at[m],
                device_id=_peer(levels[lev], j), device_id_type=pl.DeviceIdType.MESH)
            cp.start()
            copies.append((j, off, cp))
        for j, off, cp in copies:
            pltpu.make_async_remote_copy(
                src_ref=piece, dst_ref=buf.at[j],
                send_sem=ag_send[lev].at[off], recv_sem=ag_recv[lev].at[j],
                device_id=_peer(levels[lev], j), device_id_type=pl.DeviceIdType.MESH).wait_recv()
        for j, off, cp in copies:
            cp.wait_send()


def allreduce(x, levels, collective_id, direct=False):
    shape = x.shape
    total = x.size
    counts = [n for _, n, _ in levels]
    per = total
    for n in counts:
        per //= n
    rows = per // LANES
    full = tuple(counts) + (rows, LANES)
    xr = x.reshape(full)
    scratch = []
    for lev in range(len(levels)):
        if direct and lev == len(levels) - 1:
            scratch.append(pltpu.VMEM((counts[lev],) + full[lev:], jnp.float32))
        else:
            scratch.append(pltpu.VMEM(full[lev:], jnp.float32))
    for lev in range(len(levels) - 1):
        scratch.append(pltpu.VMEM(full[lev + 1:], jnp.float32))
    for lev in range(len(levels) - 1):
        scratch.append(pltpu.VMEM(full[lev + 1:], jnp.float32))
    for _ in range(4):
        for _, n, _ in levels:
            scratch.append(pltpu.SemaphoreType.DMA((n,)))
    scratch.append(pltpu.SemaphoreType.DMA((1,)))
    out = pl.pallas_call(
        functools.partial(_allreduce_kernel, tuple(levels), direct),
        out_shape=jax.ShapeDtypeStruct(full, jnp.float32),
        in_specs=[pl.BlockSpec(memory_space=pltpu.VMEM)],
        out_specs=pl.BlockSpec(memory_space=pltpu.VMEM),
        scratch_shapes=scratch,
        compiler_params=pltpu.CompilerParams(collective_id=collective_id, has_side_effects=True),
        cost_estimate=pl.CostEstimate(flops=total * 2, bytes_accessed=total * 4 * 4, transcendentals=0),
    )(xr)
    return out.reshape(shape)


def _update_kernel(x_ref, mom_ref, master_ref, mom_out, master_out,
                   rows_buf, send1, recv1, local_sem):
    n, rows, cols = x_ref.shape
    me = lax.axis_index("tp")
    barrier = pltpu.get_barrier_semaphore()
    for off in range(1, n):
        j = lax.rem(me + off, n)
        pl.semaphore_signal(barrier, inc=1, device_id=_peer(("tp", n, 1), j),
                            device_id_type=pl.DeviceIdType.MESH)
    pl.semaphore_wait(barrier, n - 1)

    def to_rows(j, src):
        return pltpu.make_async_remote_copy(
            src_ref=src, dst_ref=rows_buf.at[:, pl.ds(pl.multiple_of(me * cols, cols), cols)],
            send_sem=send1.at[j], recv_sem=recv1.at[me],
            device_id=_peer(("tp", n, 1), j), device_id_type=pl.DeviceIdType.MESH)

    copies = []
    for off in range(1, n):
        j = lax.rem(me + off, n)
        cp = to_rows(j, x_ref.at[j])
        cp.start()
        copies.append((j, cp))
    own = pltpu.make_async_copy(
        x_ref.at[me], rows_buf.at[:, pl.ds(pl.multiple_of(me * cols, cols), cols)], local_sem.at[0])
    own.start()
    own.wait()
    for j, cp in copies:
        pltpu.make_async_remote_copy(
            src_ref=x_ref.at[j], dst_ref=rows_buf.at[:, pl.ds(pl.multiple_of(j * cols, cols), cols)],
            send_sem=send1.at[j], recv_sem=recv1.at[j],
            device_id=_peer(("tp", n, 1), j), device_id_type=pl.DeviceIdType.MESH).wait_recv()
    for j, cp in copies:
        cp.wait_send()

    new_mom = MOMENTUM_DECAY * mom_ref[...] + rows_buf[...]
    new_master = master_ref[...] - LEARNING_RATE * new_mom
    mom_out[...] = new_mom
    master_out[...] = new_master


def _columns_kernel(x_ref, cols_out, send, recv, local_sem):
    n, rows, cols = cols_out.shape
    me = lax.axis_index("tp")
    barrier = pltpu.get_barrier_semaphore()
    for off in range(1, n):
        j = lax.rem(me + off, n)
        pl.semaphore_signal(barrier, inc=1, device_id=_peer(("tp", n, 1), j),
                            device_id_type=pl.DeviceIdType.MESH)
    pl.semaphore_wait(barrier, n - 1)

    def block(j):
        return x_ref.at[:, pl.ds(pl.multiple_of(j * cols, cols), cols)]

    copies = []
    for off in range(1, n):
        j = lax.rem(me + off, n)
        cp = pltpu.make_async_remote_copy(
            src_ref=block(j), dst_ref=cols_out.at[me],
            send_sem=send.at[j], recv_sem=recv.at[me],
            device_id=_peer(("tp", n, 1), j), device_id_type=pl.DeviceIdType.MESH)
        cp.start()
        copies.append((j, cp))
    own = pltpu.make_async_copy(block(me), cols_out.at[me], local_sem.at[0])
    own.start()
    own.wait()
    for j, cp in copies:
        pltpu.make_async_remote_copy(
            src_ref=block(j), dst_ref=cols_out.at[j],
            send_sem=send.at[j], recv_sem=recv.at[j],
            device_id=_peer(("tp", n, 1), j), device_id_type=pl.DeviceIdType.MESH).wait_recv()
    for j, cp in copies:
        cp.wait_send()


def by_columns(x, n, collective_id):
    rows, width = x.shape
    cols = width // n
    vmem = pl.BlockSpec(memory_space=pltpu.VMEM)
    return pl.pallas_call(
        _columns_kernel,
        out_shape=jax.ShapeDtypeStruct((n, rows, cols), x.dtype),
        in_specs=[vmem],
        out_specs=vmem,
        scratch_shapes=[
            pltpu.SemaphoreType.DMA((n,)),
            pltpu.SemaphoreType.DMA((n,)),
            pltpu.SemaphoreType.DMA((1,)),
        ],
        compiler_params=pltpu.CompilerParams(collective_id=collective_id, has_side_effects=True),
        cost_estimate=pl.CostEstimate(flops=0, bytes_accessed=2 * x.size * x.dtype.itemsize,
                                      transcendentals=0),
    )(x)


def flat_update(own_block, momentum, master, n, collective_id):
    block_rows, cols = own_block.shape
    rows = block_rows // n
    x = own_block.reshape(n, rows, cols)
    f32 = jnp.float32
    vmem = pl.BlockSpec(memory_space=pltpu.VMEM)
    return pl.pallas_call(
        _update_kernel,
        out_shape=(
            jax.ShapeDtypeStruct(momentum.shape, f32),
            jax.ShapeDtypeStruct(master.shape, f32),
        ),
        in_specs=[vmem, vmem, vmem],
        out_specs=(vmem, vmem),
        scratch_shapes=[
            pltpu.VMEM((rows, n * cols), f32),
            pltpu.SemaphoreType.DMA((n,)),
            pltpu.SemaphoreType.DMA((n,)),
            pltpu.SemaphoreType.DMA((1,)),
        ],
        compiler_params=pltpu.CompilerParams(collective_id=collective_id, has_side_effects=True),
        cost_estimate=pl.CostEstimate(flops=4 * momentum.size, bytes_accessed=5 * 4 * momentum.size,
                                      transcendentals=0),
    )(x, momentum, master)


def split_levels(name, size, inner):
    if size % inner or size == inner:
        return ((name, size, 1),)
    if inner == 2:
        return ((name, inner, 1), (name, size // inner, inner))
    return ((name, size // inner, inner), (name, inner, 1))


def orthonormal_by_gram(factor):
    hi = lax.Precision.HIGHEST
    gram_now = local_gram(factor)
    rank = factor.shape[1]
    eye = jnp.eye(rank, dtype=factor.dtype)
    sum_squares = jnp.trace(gram_now, axis1=1, axis2=2)[:, None, None]
    factor_scale = lax.rsqrt(sum_squares + NORM_EPSILON)
    gram_now = gram_now * (factor_scale * factor_scale)
    mixing = None
    for iteration in range(NS_STEPS):
        step = 1.5 * eye - 0.5 * gram_now
        mixing = step if mixing is None else jnp.einsum("krs,kst->krt", step, mixing, precision=hi)
        if iteration < NS_STEPS - 1:
            gram_now = jnp.einsum(
                "krs,kst,kut->kru", step, gram_now, step, precision=hi)
    return jnp.einsum("krs,ksd->krd", mixing * factor_scale, factor, precision=hi)


def local_gram(factor):
    return jnp.einsum("krd,ksd->krs", factor, factor, precision=lax.Precision.HIGHEST)


def orthonormal(factor, gram_of):
    gram_now = gram_of(factor)
    sum_squares = jnp.trace(gram_now, axis1=1, axis2=2)[:, None, None]
    factor_scale = lax.rsqrt(sum_squares + NORM_EPSILON)
    ortho_basis = factor * factor_scale
    gram_now = gram_now * (factor_scale * factor_scale)
    for iteration in range(NS_STEPS):
        if iteration > 0:
            gram_now = gram_of(ortho_basis)
        ortho_basis = 1.5 * ortho_basis - 0.5 * jnp.einsum(
            "krs,ksd->krd", gram_now, ortho_basis, precision=lax.Precision.HIGHEST
        )
    return ortho_basis


def local(grads, error, query, momentum, master):
    corrected = grads[0].astype(jnp.float32) + error[0]
    current = query
    replicas = lax.axis_size("rep")
    tensor = lax.axis_size("tp")
    kept = master - LEARNING_RATE * (MOMENTUM_DECAY * momentum)
    kept_cols = by_columns(kept, tensor, 3)
    kept_cols = kept_cols.reshape(-1, kept_cols.shape[-1])
    kept_all = lax.all_gather(kept_cols, "rep", axis=0, tiled=True)
    rep_only = (("rep", replicas, 1),)
    both = split_levels("tp", lax.axis_size("tp"), 2) + split_levels("rep", replicas, 4)
    for power_pass in range(ROUNDS):
        partial_factor = jnp.einsum(
            "kdf,krf->krd", corrected, current, precision=lax.Precision.HIGHEST
        )
        summed = allreduce(partial_factor, both, 0, direct=True)
        ortho_basis = orthonormal_by_gram(summed)
        partial_query = jnp.einsum(
            "kdf,krd->krf", corrected, ortho_basis, precision=lax.Precision.HIGHEST
        )
        current = allreduce(partial_query, rep_only, 1) / replicas
    approx = jnp.einsum("krd,krf->kdf", ortho_basis, current, precision=lax.Precision.HIGHEST)
    new_error = (corrected - approx)[None]
    matrices, model_width, shard_cols = approx.shape
    weights = (kept_all.reshape(approx.shape) - LEARNING_RATE * approx).astype(jnp.bfloat16)
    block_rows = matrices * model_width // replicas
    span = min(matrices, -(-block_rows // model_width) + 1)
    first_row = lax.axis_index("rep") * block_rows
    first_mat = jnp.minimum(first_row // model_width, matrices - span)
    pair = jnp.einsum(
        "krd,krf->kdf",
        lax.dynamic_slice_in_dim(ortho_basis, first_mat, span, 0),
        lax.dynamic_slice_in_dim(current, first_mat, span, 0),
        precision=lax.Precision.HIGHEST,
    ).reshape(span * model_width, shard_cols)
    own_block = lax.dynamic_slice_in_dim(
        pair, first_row - first_mat * model_width, block_rows, 0
    )
    new_momentum, new_master = flat_update(own_block, momentum, master, tensor, 2)
    return (new_error, current, new_momentum, new_master, weights)


def solution(mesh):
    placed = (
        P("rep", None, None, "tp"),
        P("rep", None, None, "tp"),
        P(None, None, "tp"),
        P(("rep", "tp"), None),
        P(("rep", "tp"), None),
    )
    return jax.shard_map(
        local,
        mesh=mesh,
        in_specs=placed,
        out_specs=(
            P("rep", None, None, "tp"),
            P(None, None, "tp"),
            P(("rep", "tp"), None),
            P(("rep", "tp"), None),
            P(None, None, "tp"),
        ),
        check_vma=False,
    )
```

```python
import functools

import jax
import jax.numpy as jnp
from jax import lax
from jax.experimental import pallas as pl
from jax.experimental.pallas import tpu as pltpu
from jax.sharding import PartitionSpec as P

ROUNDS = 2
NS_STEPS = 5


NORM_EPSILON = 1e-06
MOMENTUM_DECAY = 0.9
LEARNING_RATE = 0.5

MESH_AXES = ("rep", "tp")
LANES = 128


def _coord(level):
    name, n, stride = level
    return lax.rem(lax.div(lax.axis_index(name), stride), n)


def _peer(level, j):
    name, n, stride = level
    base = lax.axis_index(name) + (j - _coord(level)) * stride
    return tuple(base if axis == name else lax.axis_index(axis) for axis in MESH_AXES)


def _allreduce_kernel(levels, direct, x_ref, o_ref, *scratch):
    n_lev = len(levels)
    it = iter(scratch)
    recv = [next(it) for _ in range(n_lev)]
    sums = [next(it) for _ in range(n_lev - 1)]
    gath = [next(it) for _ in range(n_lev - 1)] + [None]
    rs_send = [next(it) for _ in range(n_lev)]
    rs_recv = [next(it) for _ in range(n_lev)]
    ag_send = [next(it) for _ in range(n_lev)]
    ag_recv = [next(it) for _ in range(n_lev)]
    local_sem = next(it)

    me = [_coord(level) for level in levels]

    barrier = pltpu.get_barrier_semaphore()
    total_peers = 0
    for lev, (name, n, _) in enumerate(levels):
        for off in range(1, n):
            j = lax.rem(me[lev] + off, n)
            pl.semaphore_signal(barrier, inc=1, device_id=_peer(levels[lev], j),
                                device_id_type=pl.DeviceIdType.MESH)
        total_peers += n - 1
    pl.semaphore_wait(barrier, total_peers)

    gath_bufs = [o_ref] + gath[: n_lev - 1]

    src = x_ref
    for lev, (name, n, _) in enumerate(levels):
        m = me[lev]
        last_direct = direct and lev == n_lev - 1

        def piece(j, src=src, last_direct=last_direct):
            return src if last_direct else src.at[j]

        copies = []
        for off in range(1, n):
            j = lax.rem(m + off, n)
            cp = pltpu.make_async_remote_copy(
                src_ref=piece(j), dst_ref=recv[lev].at[m],
                send_sem=rs_send[lev].at[off], recv_sem=rs_recv[lev].at[m],
                device_id=_peer(levels[lev], j), device_id_type=pl.DeviceIdType.MESH)
            cp.start()
            copies.append((j, off, cp))
        own = pltpu.make_async_copy(piece(m), recv[lev].at[m], local_sem.at[0])
        own.start()
        own.wait()
        for j, off, cp in copies:
            pltpu.make_async_remote_copy(
                src_ref=piece(j), dst_ref=recv[lev].at[j],
                send_sem=rs_send[lev].at[off], recv_sem=rs_recv[lev].at[j],
                device_id=_peer(levels[lev], j), device_id_type=pl.DeviceIdType.MESH).wait_recv()
        for j, off, cp in copies:
            cp.wait_send()
        r = recv[lev]
        if lev < n_lev - 1:
            dst = sums[lev]
        elif last_direct:
            dst = gath_bufs[lev]
        else:
            dst = gath_bufs[lev].at[m]
        if len(r.shape) > 3:
            lead = r.shape[1:-2]
            count = 1
            for d in lead:
                count *= d

            def body(i, carry, r=r, dst=dst, n=n, lead=lead):
                idx = []
                rest = i
                for d in reversed(lead):
                    idx.append(lax.rem(rest, d))
                    rest = lax.div(rest, d)
                idx = tuple(reversed(idx))
                acc = r[(0,) + idx]
                for j in range(1, n):
                    acc = acc + r[(j,) + idx]
                dst[idx] = acc
                return carry
            lax.fori_loop(0, count, body, 0)
        else:
            acc = r[0]
            for j in range(1, n):
                acc = acc + r[j]
            dst[...] = acc
        if lev < n_lev - 1:
            src = sums[lev]

    for lev in reversed(range(n_lev - 1 if direct else n_lev)):
        name, n, _ = levels[lev]
        m = me[lev]
        buf = gath_bufs[lev]
        if lev == n_lev - 1:
            piece = buf.at[m]
        else:
            piece = gath_bufs[lev + 1]
            own = pltpu.make_async_copy(piece, buf.at[m], local_sem.at[0])
            own.start()
            own.wait()
        copies = []
        for off in range(1, n):
            j = lax.rem(m + off, n)
            cp = pltpu.make_async_remote_copy(
                src_ref=piece, dst_ref=buf.at[m],
                send_sem=ag_send[lev].at[off], recv_sem=ag_recv[lev].at[m],
                device_id=_peer(levels[lev], j), device_id_type=pl.DeviceIdType.MESH)
            cp.start()
            copies.append((j, off, cp))
        for j, off, cp in copies:
            pltpu.make_async_remote_copy(
                src_ref=piece, dst_ref=buf.at[j],
                send_sem=ag_send[lev].at[off], recv_sem=ag_recv[lev].at[j],
                device_id=_peer(levels[lev], j), device_id_type=pl.DeviceIdType.MESH).wait_recv()
        for j, off, cp in copies:
            cp.wait_send()


def allreduce(x, levels, collective_id, direct=False):
    shape = x.shape
    total = x.size
    counts = [n for _, n, _ in levels]
    per = total
    for n in counts:
        per //= n
    rows = per // LANES
    full = tuple(counts) + (rows, LANES)
    xr = x.reshape(full)
    scratch = []
    for lev in range(len(levels)):
        if direct and lev == len(levels) - 1:
            scratch.append(pltpu.VMEM((counts[lev],) + full[lev:], jnp.float32))
        else:
            scratch.append(pltpu.VMEM(full[lev:], jnp.float32))
    for lev in range(len(levels) - 1):
        scratch.append(pltpu.VMEM(full[lev + 1:], jnp.float32))
    for lev in range(len(levels) - 1):
        scratch.append(pltpu.VMEM(full[lev + 1:], jnp.float32))
    for _ in range(4):
        for _, n, _ in levels:
            scratch.append(pltpu.SemaphoreType.DMA((n,)))
    scratch.append(pltpu.SemaphoreType.DMA((1,)))
    out = pl.pallas_call(
        functools.partial(_allreduce_kernel, tuple(levels), direct),
        out_shape=jax.ShapeDtypeStruct(full, jnp.float32),
        in_specs=[pl.BlockSpec(memory_space=pltpu.VMEM)],
        out_specs=pl.BlockSpec(memory_space=pltpu.VMEM),
        scratch_shapes=scratch,
        compiler_params=pltpu.CompilerParams(collective_id=collective_id, has_side_effects=True),
        cost_estimate=pl.CostEstimate(flops=total * 2, bytes_accessed=total * 4 * 4, transcendentals=0),
    )(xr)
    return out.reshape(shape)


def _update_kernel(x_ref, mom_ref, master_ref, mom_out, master_out,
                   rows_buf, send1, recv1, local_sem):
    n, rows, cols = x_ref.shape
    me = lax.axis_index("tp")
    barrier = pltpu.get_barrier_semaphore()
    for off in range(1, n):
        j = lax.rem(me + off, n)
        pl.semaphore_signal(barrier, inc=1, device_id=_peer(("tp", n, 1), j),
                            device_id_type=pl.DeviceIdType.MESH)
    pl.semaphore_wait(barrier, n - 1)

    def to_rows(j, src):
        return pltpu.make_async_remote_copy(
            src_ref=src, dst_ref=rows_buf.at[:, pl.ds(pl.multiple_of(me * cols, cols), cols)],
            send_sem=send1.at[j], recv_sem=recv1.at[me],
            device_id=_peer(("tp", n, 1), j), device_id_type=pl.DeviceIdType.MESH)

    copies = []
    for off in range(1, n):
        j = lax.rem(me + off, n)
        cp = to_rows(j, x_ref.at[j])
        cp.start()
        copies.append((j, cp))
    own = pltpu.make_async_copy(
        x_ref.at[me], rows_buf.at[:, pl.ds(pl.multiple_of(me * cols, cols), cols)], local_sem.at[0])
    own.start()
    own.wait()
    for j, cp in copies:
        pltpu.make_async_remote_copy(
            src_ref=x_ref.at[j], dst_ref=rows_buf.at[:, pl.ds(pl.multiple_of(j * cols, cols), cols)],
            send_sem=send1.at[j], recv_sem=recv1.at[j],
            device_id=_peer(("tp", n, 1), j), device_id_type=pl.DeviceIdType.MESH).wait_recv()
    for j, cp in copies:
        cp.wait_send()

    new_mom = MOMENTUM_DECAY * mom_ref[...] + rows_buf[...]
    new_master = master_ref[...] - LEARNING_RATE * new_mom
    mom_out[...] = new_mom
    master_out[...] = new_master


def _columns_kernel(x_ref, cols_out, send, recv, local_sem):
    n, rows, cols = cols_out.shape
    me = lax.axis_index("tp")
    barrier = pltpu.get_barrier_semaphore()
    for off in range(1, n):
        j = lax.rem(me + off, n)
        pl.semaphore_signal(barrier, inc=1, device_id=_peer(("tp", n, 1), j),
                            device_id_type=pl.DeviceIdType.MESH)
    pl.semaphore_wait(barrier, n - 1)

    def block(j):
        return x_ref.at[:, pl.ds(pl.multiple_of(j * cols, cols), cols)]

    copies = []
    for off in range(1, n):
        j = lax.rem(me + off, n)
        cp = pltpu.make_async_remote_copy(
            src_ref=block(j), dst_ref=cols_out.at[me],
            send_sem=send.at[j], recv_sem=recv.at[me],
            device_id=_peer(("tp", n, 1), j), device_id_type=pl.DeviceIdType.MESH)
        cp.start()
        copies.append((j, cp))
    own = pltpu.make_async_copy(block(me), cols_out.at[me], local_sem.at[0])
    own.start()
    own.wait()
    for j, cp in copies:
        pltpu.make_async_remote_copy(
            src_ref=block(j), dst_ref=cols_out.at[j],
            send_sem=send.at[j], recv_sem=recv.at[j],
            device_id=_peer(("tp", n, 1), j), device_id_type=pl.DeviceIdType.MESH).wait_recv()
    for j, cp in copies:
        cp.wait_send()


def by_columns(x, n, collective_id):
    rows, width = x.shape
    cols = width // n
    vmem = pl.BlockSpec(memory_space=pltpu.VMEM)
    return pl.pallas_call(
        _columns_kernel,
        out_shape=jax.ShapeDtypeStruct((n, rows, cols), x.dtype),
        in_specs=[vmem],
        out_specs=vmem,
        scratch_shapes=[
            pltpu.SemaphoreType.DMA((n,)),
            pltpu.SemaphoreType.DMA((n,)),
            pltpu.SemaphoreType.DMA((1,)),
        ],
        compiler_params=pltpu.CompilerParams(collective_id=collective_id, has_side_effects=True),
        cost_estimate=pl.CostEstimate(flops=0, bytes_accessed=2 * x.size * x.dtype.itemsize,
                                      transcendentals=0),
    )(x)


def flat_update(own_block, momentum, master, n, collective_id):
    block_rows, cols = own_block.shape
    rows = block_rows // n
    x = own_block.reshape(n, rows, cols)
    f32 = jnp.float32
    vmem = pl.BlockSpec(memory_space=pltpu.VMEM)
    return pl.pallas_call(
        _update_kernel,
        out_shape=(
            jax.ShapeDtypeStruct(momentum.shape, f32),
            jax.ShapeDtypeStruct(master.shape, f32),
        ),
        in_specs=[vmem, vmem, vmem],
        out_specs=(vmem, vmem),
        scratch_shapes=[
            pltpu.VMEM((rows, n * cols), f32),
            pltpu.SemaphoreType.DMA((n,)),
            pltpu.SemaphoreType.DMA((n,)),
            pltpu.SemaphoreType.DMA((1,)),
        ],
        compiler_params=pltpu.CompilerParams(collective_id=collective_id, has_side_effects=True),
        cost_estimate=pl.CostEstimate(flops=4 * momentum.size, bytes_accessed=5 * 4 * momentum.size,
                                      transcendentals=0),
    )(x, momentum, master)


def split_levels(name, size, inner):
    if size % inner or size == inner:
        return ((name, size, 1),)
    if inner == 2:
        return ((name, inner, 1), (name, size // inner, inner))
    return ((name, size // inner, inner), (name, inner, 1))


def orthonormal_by_gram(factor):
    hi = lax.Precision.HIGHEST
    gram_now = local_gram(factor)
    rank = factor.shape[1]
    eye = jnp.eye(rank, dtype=factor.dtype)
    sum_squares = jnp.trace(gram_now, axis1=1, axis2=2)[:, None, None]
    factor_scale = lax.rsqrt(sum_squares + NORM_EPSILON)
    gram_now = gram_now * (factor_scale * factor_scale)
    mixing = None
    for iteration in range(NS_STEPS):
        step = 1.5 * eye - 0.5 * gram_now
        mixing = step if mixing is None else jnp.einsum("krs,kst->krt", step, mixing, precision=hi)
        if iteration < NS_STEPS - 1:
            gram_now = jnp.einsum(
                "krs,kst,kut->kru", step, gram_now, step, precision=hi)
    return jnp.einsum("krs,ksd->krd", mixing * factor_scale, factor, precision=hi)


def local_gram(factor):
    return jnp.einsum("krd,ksd->krs", factor, factor, precision=lax.Precision.HIGHEST)


def orthonormal(factor, gram_of):
    gram_now = gram_of(factor)
    sum_squares = jnp.trace(gram_now, axis1=1, axis2=2)[:, None, None]
    factor_scale = lax.rsqrt(sum_squares + NORM_EPSILON)
    ortho_basis = factor * factor_scale
    gram_now = gram_now * (factor_scale * factor_scale)
    for iteration in range(NS_STEPS):
        if iteration > 0:
            gram_now = gram_of(ortho_basis)
        ortho_basis = 1.5 * ortho_basis - 0.5 * jnp.einsum(
            "krs,ksd->krd", gram_now, ortho_basis, precision=lax.Precision.HIGHEST
        )
    return ortho_basis


def local(grads, error, query, momentum, master):
    corrected = grads[0].astype(jnp.float32) + error[0]
    current = query
    replicas = lax.axis_size("rep")
    tensor = lax.axis_size("tp")
    kept = master - LEARNING_RATE * (MOMENTUM_DECAY * momentum)
    kept_cols = by_columns(kept, tensor, 3)
    kept_cols = kept_cols.reshape(-1, kept_cols.shape[-1])
    kept_all = lax.all_gather(kept_cols, "rep", axis=0, tiled=True)
    rep_only = split_levels("rep", replicas, 4)
    both = split_levels("tp", lax.axis_size("tp"), 2) + split_levels("rep", replicas, 4)
    for power_pass in range(ROUNDS):
        partial_factor = jnp.einsum(
            "kdf,krf->krd", corrected, current, precision=lax.Precision.HIGHEST
        )
        summed = allreduce(partial_factor, both, 0, direct=True)
        ortho_basis = orthonormal_by_gram(summed)
        partial_query = jnp.einsum(
            "kdf,krd->krf", corrected, ortho_basis, precision=lax.Precision.HIGHEST
        )
        current = allreduce(partial_query, rep_only, 1, direct=len(rep_only) > 1) / replicas
    approx = jnp.einsum("krd,krf->kdf", ortho_basis, current, precision=lax.Precision.HIGHEST)
    new_error = (corrected - approx)[None]
    matrices, model_width, shard_cols = approx.shape
    weights = (kept_all.reshape(approx.shape) - LEARNING_RATE * approx).astype(jnp.bfloat16)
    block_rows = matrices * model_width // replicas
    span = min(matrices, -(-block_rows // model_width) + 1)
    first_row = lax.axis_index("rep") * block_rows
    first_mat = jnp.minimum(first_row // model_width, matrices - span)
    pair = jnp.einsum(
        "krd,krf->kdf",
        lax.dynamic_slice_in_dim(ortho_basis, first_mat, span, 0),
        lax.dynamic_slice_in_dim(current, first_mat, span, 0),
        precision=lax.Precision.HIGHEST,
    ).reshape(span * model_width, shard_cols)
    own_block = lax.dynamic_slice_in_dim(
        pair, first_row - first_mat * model_width, block_rows, 0
    )
    new_momentum, new_master = flat_update(own_block, momentum, master, tensor, 2)
    return (new_error, current, new_momentum, new_master, weights)


def solution(mesh):
    placed = (
        P("rep", None, None, "tp"),
        P("rep", None, None, "tp"),
        P(None, None, "tp"),
        P(("rep", "tp"), None),
        P(("rep", "tp"), None),
    )
    return jax.shard_map(
        local,
        mesh=mesh,
        in_specs=placed,
        out_specs=(
            P("rep", None, None, "tp"),
            P(None, None, "tp"),
            P(("rep", "tp"), None),
            P(("rep", "tp"), None),
            P(None, None, "tp"),
        ),
        check_vma=False,
    )
```

```python
import functools

import jax
import jax.numpy as jnp
from jax import lax
from jax.experimental import pallas as pl
from jax.experimental.pallas import tpu as pltpu
from jax.sharding import PartitionSpec as P

ROUNDS = 2
NS_STEPS = 5


NORM_EPSILON = 1e-06
MOMENTUM_DECAY = 0.9
LEARNING_RATE = 0.5

MESH_AXES = ("rep", "tp")
LANES = 128


def _coord(level):
    name, n, stride = level
    return lax.rem(lax.div(lax.axis_index(name), stride), n)


def _peer(level, j):
    name, n, stride = level
    base = lax.axis_index(name) + (j - _coord(level)) * stride
    return tuple(base if axis == name else lax.axis_index(axis) for axis in MESH_AXES)


def _allreduce_kernel(levels, direct, x_ref, o_ref, *scratch):
    n_lev = len(levels)
    it = iter(scratch)
    recv = [next(it) for _ in range(n_lev)]
    sums = [next(it) for _ in range(n_lev - 1)]
    gath = [next(it) for _ in range(n_lev - 1)] + [None]
    rs_send = [next(it) for _ in range(n_lev)]
    rs_recv = [next(it) for _ in range(n_lev)]
    ag_send = [next(it) for _ in range(n_lev)]
    ag_recv = [next(it) for _ in range(n_lev)]
    local_sem = next(it)

    me = [_coord(level) for level in levels]

    barrier = pltpu.get_barrier_semaphore()
    total_peers = 0
    for lev, (name, n, _) in enumerate(levels):
        for off in range(1, n):
            j = lax.rem(me[lev] + off, n)
            pl.semaphore_signal(barrier, inc=1, device_id=_peer(levels[lev], j),
                                device_id_type=pl.DeviceIdType.MESH)
        total_peers += n - 1
    pl.semaphore_wait(barrier, total_peers)

    gath_bufs = [o_ref] + gath[: n_lev - 1]

    src = x_ref
    for lev, (name, n, _) in enumerate(levels):
        m = me[lev]
        last_direct = direct and lev == n_lev - 1

        def piece(j, src=src, last_direct=last_direct):
            return src if last_direct else src.at[j]

        copies = []
        for off in range(1, n):
            j = lax.rem(m + off, n)
            cp = pltpu.make_async_remote_copy(
                src_ref=piece(j), dst_ref=recv[lev].at[m],
                send_sem=rs_send[lev].at[off], recv_sem=rs_recv[lev].at[m],
                device_id=_peer(levels[lev], j), device_id_type=pl.DeviceIdType.MESH)
            cp.start()
            copies.append((j, off, cp))
        own = pltpu.make_async_copy(piece(m), recv[lev].at[m], local_sem.at[0])
        own.start()
        own.wait()
        for j, off, cp in copies:
            pltpu.make_async_remote_copy(
                src_ref=piece(j), dst_ref=recv[lev].at[j],
                send_sem=rs_send[lev].at[off], recv_sem=rs_recv[lev].at[j],
                device_id=_peer(levels[lev], j), device_id_type=pl.DeviceIdType.MESH).wait_recv()
        for j, off, cp in copies:
            cp.wait_send()
        r = recv[lev]
        if lev < n_lev - 1:
            dst = sums[lev]
        elif last_direct:
            dst = gath_bufs[lev]
        else:
            dst = gath_bufs[lev].at[m]
        if len(r.shape) > 3:
            lead = r.shape[1:-2]
            count = 1
            for d in lead:
                count *= d

            def body(i, carry, r=r, dst=dst, n=n, lead=lead):
                idx = []
                rest = i
                for d in reversed(lead):
                    idx.append(lax.rem(rest, d))
                    rest = lax.div(rest, d)
                idx = tuple(reversed(idx))
                acc = r[(0,) + idx]
                for j in range(1, n):
                    acc = acc + r[(j,) + idx]
                dst[idx] = acc
                return carry
            lax.fori_loop(0, count, body, 0)
        else:
            acc = r[0]
            for j in range(1, n):
                acc = acc + r[j]
            dst[...] = acc
        if lev < n_lev - 1:
            src = sums[lev]

    for lev in reversed(range(n_lev - 1 if direct else n_lev)):
        name, n, _ = levels[lev]
        m = me[lev]
        buf = gath_bufs[lev]
        if lev == n_lev - 1:
            piece = buf.at[m]
        else:
            piece = gath_bufs[lev + 1]
            own = pltpu.make_async_copy(piece, buf.at[m], local_sem.at[0])
            own.start()
            own.wait()
        copies = []
        for off in range(1, n):
            j = lax.rem(m + off, n)
            cp = pltpu.make_async_remote_copy(
                src_ref=piece, dst_ref=buf.at[m],
                send_sem=ag_send[lev].at[off], recv_sem=ag_recv[lev].at[m],
                device_id=_peer(levels[lev], j), device_id_type=pl.DeviceIdType.MESH)
            cp.start()
            copies.append((j, off, cp))
        for j, off, cp in copies:
            pltpu.make_async_remote_copy(
                src_ref=piece, dst_ref=buf.at[j],
                send_sem=ag_send[lev].at[off], recv_sem=ag_recv[lev].at[j],
                device_id=_peer(levels[lev], j), device_id_type=pl.DeviceIdType.MESH).wait_recv()
        for j, off, cp in copies:
            cp.wait_send()


def allreduce(x, levels, collective_id, direct=False):
    shape = x.shape
    total = x.size
    counts = [n for _, n, _ in levels]
    per = total
    for n in counts:
        per //= n
    rows = per // LANES
    full = tuple(counts) + (rows, LANES)
    xr = x.reshape(full)
    scratch = []
    for lev in range(len(levels)):
        if direct and lev == len(levels) - 1:
            scratch.append(pltpu.VMEM((counts[lev],) + full[lev:], jnp.float32))
        else:
            scratch.append(pltpu.VMEM(full[lev:], jnp.float32))
    for lev in range(len(levels) - 1):
        scratch.append(pltpu.VMEM(full[lev + 1:], jnp.float32))
    for lev in range(len(levels) - 1):
        scratch.append(pltpu.VMEM(full[lev + 1:], jnp.float32))
    for _ in range(4):
        for _, n, _ in levels:
            scratch.append(pltpu.SemaphoreType.DMA((n,)))
    scratch.append(pltpu.SemaphoreType.DMA((1,)))
    out = pl.pallas_call(
        functools.partial(_allreduce_kernel, tuple(levels), direct),
        out_shape=jax.ShapeDtypeStruct(full, jnp.float32),
        in_specs=[pl.BlockSpec(memory_space=pltpu.VMEM)],
        out_specs=pl.BlockSpec(memory_space=pltpu.VMEM),
        scratch_shapes=scratch,
        compiler_params=pltpu.CompilerParams(collective_id=collective_id, has_side_effects=True),
        cost_estimate=pl.CostEstimate(flops=total * 2, bytes_accessed=total * 4 * 4, transcendentals=0),
    )(xr)
    return out.reshape(shape)


def _update_kernel(x_ref, mom_ref, master_ref, mom_out, master_out,
                   rows_buf, send1, recv1, local_sem):
    n, rows, cols = x_ref.shape
    me = lax.axis_index("tp")
    barrier = pltpu.get_barrier_semaphore()
    for off in range(1, n):
        j = lax.rem(me + off, n)
        pl.semaphore_signal(barrier, inc=1, device_id=_peer(("tp", n, 1), j),
                            device_id_type=pl.DeviceIdType.MESH)
    pl.semaphore_wait(barrier, n - 1)

    def to_rows(j, src):
        return pltpu.make_async_remote_copy(
            src_ref=src, dst_ref=rows_buf.at[:, pl.ds(pl.multiple_of(me * cols, cols), cols)],
            send_sem=send1.at[j], recv_sem=recv1.at[me],
            device_id=_peer(("tp", n, 1), j), device_id_type=pl.DeviceIdType.MESH)

    copies = []
    for off in range(1, n):
        j = lax.rem(me + off, n)
        cp = to_rows(j, x_ref.at[j])
        cp.start()
        copies.append((j, cp))
    own = pltpu.make_async_copy(
        x_ref.at[me], rows_buf.at[:, pl.ds(pl.multiple_of(me * cols, cols), cols)], local_sem.at[0])
    own.start()
    own.wait()
    for j, cp in copies:
        pltpu.make_async_remote_copy(
            src_ref=x_ref.at[j], dst_ref=rows_buf.at[:, pl.ds(pl.multiple_of(j * cols, cols), cols)],
            send_sem=send1.at[j], recv_sem=recv1.at[j],
            device_id=_peer(("tp", n, 1), j), device_id_type=pl.DeviceIdType.MESH).wait_recv()
    for j, cp in copies:
        cp.wait_send()

    new_mom = MOMENTUM_DECAY * mom_ref[...] + rows_buf[...]
    new_master = master_ref[...] - LEARNING_RATE * new_mom
    mom_out[...] = new_mom
    master_out[...] = new_master


def _columns_kernel(x_ref, cols_out, send, recv, local_sem):
    n, rows, cols = cols_out.shape
    me = lax.axis_index("tp")
    barrier = pltpu.get_barrier_semaphore()
    for off in range(1, n):
        j = lax.rem(me + off, n)
        pl.semaphore_signal(barrier, inc=1, device_id=_peer(("tp", n, 1), j),
                            device_id_type=pl.DeviceIdType.MESH)
    pl.semaphore_wait(barrier, n - 1)

    def block(j):
        return x_ref.at[:, pl.ds(pl.multiple_of(j * cols, cols), cols)]

    copies = []
    for off in range(1, n):
        j = lax.rem(me + off, n)
        cp = pltpu.make_async_remote_copy(
            src_ref=block(j), dst_ref=cols_out.at[me],
            send_sem=send.at[j], recv_sem=recv.at[me],
            device_id=_peer(("tp", n, 1), j), device_id_type=pl.DeviceIdType.MESH)
        cp.start()
        copies.append((j, cp))
    own = pltpu.make_async_copy(block(me), cols_out.at[me], local_sem.at[0])
    own.start()
    own.wait()
    for j, cp in copies:
        pltpu.make_async_remote_copy(
            src_ref=block(j), dst_ref=cols_out.at[j],
            send_sem=send.at[j], recv_sem=recv.at[j],
            device_id=_peer(("tp", n, 1), j), device_id_type=pl.DeviceIdType.MESH).wait_recv()
    for j, cp in copies:
        cp.wait_send()


def by_columns(x, n, collective_id):
    rows, width = x.shape
    cols = width // n
    vmem = pl.BlockSpec(memory_space=pltpu.VMEM)
    return pl.pallas_call(
        _columns_kernel,
        out_shape=jax.ShapeDtypeStruct((n, rows, cols), x.dtype),
        in_specs=[vmem],
        out_specs=vmem,
        scratch_shapes=[
            pltpu.SemaphoreType.DMA((n,)),
            pltpu.SemaphoreType.DMA((n,)),
            pltpu.SemaphoreType.DMA((1,)),
        ],
        compiler_params=pltpu.CompilerParams(collective_id=collective_id, has_side_effects=True),
        cost_estimate=pl.CostEstimate(flops=0, bytes_accessed=2 * x.size * x.dtype.itemsize,
                                      transcendentals=0),
    )(x)


def flat_update(own_block, momentum, master, n, collective_id):
    block_rows, cols = own_block.shape
    rows = block_rows // n
    x = own_block.reshape(n, rows, cols)
    f32 = jnp.float32
    vmem = pl.BlockSpec(memory_space=pltpu.VMEM)
    return pl.pallas_call(
        _update_kernel,
        out_shape=(
            jax.ShapeDtypeStruct(momentum.shape, f32),
            jax.ShapeDtypeStruct(master.shape, f32),
        ),
        in_specs=[vmem, vmem, vmem],
        out_specs=(vmem, vmem),
        scratch_shapes=[
            pltpu.VMEM((rows, n * cols), f32),
            pltpu.SemaphoreType.DMA((n,)),
            pltpu.SemaphoreType.DMA((n,)),
            pltpu.SemaphoreType.DMA((1,)),
        ],
        compiler_params=pltpu.CompilerParams(collective_id=collective_id, has_side_effects=True),
        cost_estimate=pl.CostEstimate(flops=4 * momentum.size, bytes_accessed=5 * 4 * momentum.size,
                                      transcendentals=0),
    )(x, momentum, master)


def split_levels(name, size, inner):
    if size % inner or size == inner:
        return ((name, size, 1),)
    if inner == 2:
        return ((name, inner, 1), (name, size // inner, inner))
    return ((name, size // inner, inner), (name, inner, 1))


def orthonormal_by_gram(factor):
    hi = lax.Precision.HIGHEST
    gram_now = local_gram(factor)
    rank = factor.shape[1]
    eye = jnp.eye(rank, dtype=factor.dtype)
    sum_squares = jnp.trace(gram_now, axis1=1, axis2=2)[:, None, None]
    factor_scale = lax.rsqrt(sum_squares + NORM_EPSILON)
    gram_now = gram_now * (factor_scale * factor_scale)
    mixing = None
    for iteration in range(NS_STEPS):
        step = 1.5 * eye - 0.5 * gram_now
        mixing = step if mixing is None else jnp.einsum("krs,kst->krt", step, mixing, precision=hi)
        if iteration < NS_STEPS - 1:
            gram_now = jnp.einsum(
                "krs,kst,kut->kru", step, gram_now, step, precision=hi)
    return jnp.einsum("krs,ksd->krd", mixing * factor_scale, factor, precision=hi)


def local_gram(factor):
    return jnp.einsum("krd,ksd->krs", factor, factor, precision=lax.Precision.HIGHEST)


def orthonormal(factor, gram_of):
    gram_now = gram_of(factor)
    sum_squares = jnp.trace(gram_now, axis1=1, axis2=2)[:, None, None]
    factor_scale = lax.rsqrt(sum_squares + NORM_EPSILON)
    ortho_basis = factor * factor_scale
    gram_now = gram_now * (factor_scale * factor_scale)
    for iteration in range(NS_STEPS):
        if iteration > 0:
            gram_now = gram_of(ortho_basis)
        ortho_basis = 1.5 * ortho_basis - 0.5 * jnp.einsum(
            "krs,ksd->krd", gram_now, ortho_basis, precision=lax.Precision.HIGHEST
        )
    return ortho_basis


def local(grads, error, query, momentum, master):
    corrected = grads[0].astype(jnp.float32) + error[0]
    current = query
    replicas = lax.axis_size("rep")
    tensor = lax.axis_size("tp")
    kept = master - LEARNING_RATE * (MOMENTUM_DECAY * momentum)
    kept_cols = by_columns(kept, tensor, 3)
    kept_cols = kept_cols.reshape(-1, kept_cols.shape[-1])
    kept_all = lax.all_gather(kept_cols, "rep", axis=0, tiled=True)
    rep_only = (("rep", replicas, 1),)
    both = split_levels("tp", lax.axis_size("tp"), 2)[::-1] + split_levels("rep", replicas, 4)
    for power_pass in range(ROUNDS):
        partial_factor = jnp.einsum(
            "kdf,krf->krd", corrected, current, precision=lax.Precision.HIGHEST
        )
        summed = allreduce(partial_factor, both, 0, direct=True)
        ortho_basis = orthonormal_by_gram(summed)
        partial_query = jnp.einsum(
            "kdf,krd->krf", corrected, ortho_basis, precision=lax.Precision.HIGHEST
        )
        current = allreduce(partial_query, rep_only, 1) / replicas
    approx = jnp.einsum("krd,krf->kdf", ortho_basis, current, precision=lax.Precision.HIGHEST)
    new_error = (corrected - approx)[None]
    matrices, model_width, shard_cols = approx.shape
    weights = (kept_all.reshape(approx.shape) - LEARNING_RATE * approx).astype(jnp.bfloat16)
    block_rows = matrices * model_width // replicas
    span = min(matrices, -(-block_rows // model_width) + 1)
    first_row = lax.axis_index("rep") * block_rows
    first_mat = jnp.minimum(first_row // model_width, matrices - span)
    pair = jnp.einsum(
        "krd,krf->kdf",
        lax.dynamic_slice_in_dim(ortho_basis, first_mat, span, 0),
        lax.dynamic_slice_in_dim(current, first_mat, span, 0),
        precision=lax.Precision.HIGHEST,
    ).reshape(span * model_width, shard_cols)
    own_block = lax.dynamic_slice_in_dim(
        pair, first_row - first_mat * model_width, block_rows, 0
    )
    new_momentum, new_master = flat_update(own_block, momentum, master, tensor, 2)
    return (new_error, current, new_momentum, new_master, weights)


def solution(mesh):
    placed = (
        P("rep", None, None, "tp"),
        P("rep", None, None, "tp"),
        P(None, None, "tp"),
        P(("rep", "tp"), None),
        P(("rep", "tp"), None),
    )
    return jax.shard_map(
        local,
        mesh=mesh,
        in_specs=placed,
        out_specs=(
            P("rep", None, None, "tp"),
            P(None, None, "tp"),
            P(("rep", "tp"), None),
            P(("rep", "tp"), None),
            P(None, None, "tp"),
        ),
        check_vma=False,
    )
```

```python
import functools

import jax
import jax.numpy as jnp
from jax import lax
from jax.experimental import pallas as pl
from jax.experimental.pallas import tpu as pltpu
from jax.sharding import PartitionSpec as P

ROUNDS = 2
NS_STEPS = 5


NORM_EPSILON = 1e-06
MOMENTUM_DECAY = 0.9
LEARNING_RATE = 0.5

MESH_AXES = ("rep", "tp")
LANES = 128


def _coord(level):
    name, n, stride = level
    return lax.rem(lax.div(lax.axis_index(name), stride), n)


def _peer(level, j):
    name, n, stride = level
    base = lax.axis_index(name) + (j - _coord(level)) * stride
    return tuple(base if axis == name else lax.axis_index(axis) for axis in MESH_AXES)


def _allreduce_kernel(levels, direct, x_ref, o_ref, *scratch):
    n_lev = len(levels)
    it = iter(scratch)
    recv = [next(it) for _ in range(n_lev)]
    sums = [next(it) for _ in range(n_lev - 1)]
    gath = [next(it) for _ in range(n_lev - 1)] + [None]
    rs_send = [next(it) for _ in range(n_lev)]
    rs_recv = [next(it) for _ in range(n_lev)]
    ag_send = [next(it) for _ in range(n_lev)]
    ag_recv = [next(it) for _ in range(n_lev)]
    local_sem = next(it)

    me = [_coord(level) for level in levels]

    barrier = pltpu.get_barrier_semaphore()
    total_peers = 0
    for lev, (name, n, _) in enumerate(levels):
        for off in range(1, n):
            j = lax.rem(me[lev] + off, n)
            pl.semaphore_signal(barrier, inc=1, device_id=_peer(levels[lev], j),
                                device_id_type=pl.DeviceIdType.MESH)
        total_peers += n - 1
    pl.semaphore_wait(barrier, total_peers)

    gath_bufs = [o_ref] + gath[: n_lev - 1]

    src = x_ref
    for lev, (name, n, _) in enumerate(levels):
        m = me[lev]
        last_direct = direct and lev == n_lev - 1

        def piece(j, src=src, last_direct=last_direct):
            return src if last_direct else src.at[j]

        copies = []
        for off in range(1, n):
            j = lax.rem(m + off, n)
            cp = pltpu.make_async_remote_copy(
                src_ref=piece(j), dst_ref=recv[lev].at[m],
                send_sem=rs_send[lev].at[off], recv_sem=rs_recv[lev].at[m],
                device_id=_peer(levels[lev], j), device_id_type=pl.DeviceIdType.MESH)
            cp.start()
            copies.append((j, off, cp))
        if last_direct:
            own = pltpu.make_async_copy(piece(m), recv[lev].at[m], local_sem.at[0])
            own.start()
            own.wait()
        for j, off, cp in copies:
            pltpu.make_async_remote_copy(
                src_ref=piece(j), dst_ref=recv[lev].at[j],
                send_sem=rs_send[lev].at[off], recv_sem=rs_recv[lev].at[j],
                device_id=_peer(levels[lev], j), device_id_type=pl.DeviceIdType.MESH).wait_recv()
        for j, off, cp in copies:
            cp.wait_send()
        r = recv[lev]
        if lev < n_lev - 1:
            dst = sums[lev]
        elif last_direct:
            dst = gath_bufs[lev]
        else:
            dst = gath_bufs[lev].at[m]
        if len(r.shape) > 3:
            lead = r.shape[1:-2]
            count = 1
            for d in lead:
                count *= d

            def body(i, carry, r=r, dst=dst, n=n, lead=lead, src=src, m=m, last_direct=last_direct):
                idx = []
                rest = i
                for d in reversed(lead):
                    idx.append(lax.rem(rest, d))
                    rest = lax.div(rest, d)
                idx = tuple(reversed(idx))
                if last_direct:
                    acc = r[(0,) + idx]
                    for j in range(1, n):
                        acc = acc + r[(j,) + idx]
                else:
                    acc = src[(m,) + idx]
                    for off in range(1, n):
                        acc = acc + r[(lax.rem(m + off, n),) + idx]
                dst[idx] = acc
                return carry
            lax.fori_loop(0, count, body, 0)
        elif last_direct:
            acc = r[0]
            for j in range(1, n):
                acc = acc + r[j]
            dst[...] = acc
        else:
            acc = src[m]
            for off in range(1, n):
                acc = acc + r[lax.rem(m + off, n)]
            dst[...] = acc
        if lev < n_lev - 1:
            src = sums[lev]

    for lev in reversed(range(n_lev - 1 if direct else n_lev)):
        name, n, _ = levels[lev]
        m = me[lev]
        buf = gath_bufs[lev]
        if lev == n_lev - 1:
            piece = buf.at[m]
        else:
            piece = gath_bufs[lev + 1]
            own = pltpu.make_async_copy(piece, buf.at[m], local_sem.at[0])
            own.start()
            own.wait()
        copies = []
        for off in range(1, n):
            j = lax.rem(m + off, n)
            cp = pltpu.make_async_remote_copy(
                src_ref=piece, dst_ref=buf.at[m],
                send_sem=ag_send[lev].at[off], recv_sem=ag_recv[lev].at[m],
                device_id=_peer(levels[lev], j), device_id_type=pl.DeviceIdType.MESH)
            cp.start()
            copies.append((j, off, cp))
        for j, off, cp in copies:
            pltpu.make_async_remote_copy(
                src_ref=piece, dst_ref=buf.at[j],
                send_sem=ag_send[lev].at[off], recv_sem=ag_recv[lev].at[j],
                device_id=_peer(levels[lev], j), device_id_type=pl.DeviceIdType.MESH).wait_recv()
        for j, off, cp in copies:
            cp.wait_send()


def allreduce(x, levels, collective_id, direct=False):
    shape = x.shape
    total = x.size
    counts = [n for _, n, _ in levels]
    per = total
    for n in counts:
        per //= n
    rows = per // LANES
    full = tuple(counts) + (rows, LANES)
    xr = x.reshape(full)
    scratch = []
    for lev in range(len(levels)):
        if direct and lev == len(levels) - 1:
            scratch.append(pltpu.VMEM((counts[lev],) + full[lev:], jnp.float32))
        else:
            scratch.append(pltpu.VMEM(full[lev:], jnp.float32))
    for lev in range(len(levels) - 1):
        scratch.append(pltpu.VMEM(full[lev + 1:], jnp.float32))
    for lev in range(len(levels) - 1):
        scratch.append(pltpu.VMEM(full[lev + 1:], jnp.float32))
    for _ in range(4):
        for _, n, _ in levels:
            scratch.append(pltpu.SemaphoreType.DMA((n,)))
    scratch.append(pltpu.SemaphoreType.DMA((1,)))
    out = pl.pallas_call(
        functools.partial(_allreduce_kernel, tuple(levels), direct),
        out_shape=jax.ShapeDtypeStruct(full, jnp.float32),
        in_specs=[pl.BlockSpec(memory_space=pltpu.VMEM)],
        out_specs=pl.BlockSpec(memory_space=pltpu.VMEM),
        scratch_shapes=scratch,
        compiler_params=pltpu.CompilerParams(collective_id=collective_id, has_side_effects=True),
        cost_estimate=pl.CostEstimate(flops=total * 2, bytes_accessed=total * 4 * 4, transcendentals=0),
    )(xr)
    return out.reshape(shape)


def _update_kernel(x_ref, mom_ref, master_ref, mom_out, master_out,
                   rows_buf, send1, recv1, local_sem):
    n, rows, cols = x_ref.shape
    me = lax.axis_index("tp")
    barrier = pltpu.get_barrier_semaphore()
    for off in range(1, n):
        j = lax.rem(me + off, n)
        pl.semaphore_signal(barrier, inc=1, device_id=_peer(("tp", n, 1), j),
                            device_id_type=pl.DeviceIdType.MESH)
    pl.semaphore_wait(barrier, n - 1)

    def to_rows(j, src):
        return pltpu.make_async_remote_copy(
            src_ref=src, dst_ref=rows_buf.at[:, pl.ds(pl.multiple_of(me * cols, cols), cols)],
            send_sem=send1.at[j], recv_sem=recv1.at[me],
            device_id=_peer(("tp", n, 1), j), device_id_type=pl.DeviceIdType.MESH)

    copies = []
    for off in range(1, n):
        j = lax.rem(me + off, n)
        cp = to_rows(j, x_ref.at[j])
        cp.start()
        copies.append((j, cp))
    own = pltpu.make_async_copy(
        x_ref.at[me], rows_buf.at[:, pl.ds(pl.multiple_of(me * cols, cols), cols)], local_sem.at[0])
    own.start()
    own.wait()
    for j, cp in copies:
        pltpu.make_async_remote_copy(
            src_ref=x_ref.at[j], dst_ref=rows_buf.at[:, pl.ds(pl.multiple_of(j * cols, cols), cols)],
            send_sem=send1.at[j], recv_sem=recv1.at[j],
            device_id=_peer(("tp", n, 1), j), device_id_type=pl.DeviceIdType.MESH).wait_recv()
    for j, cp in copies:
        cp.wait_send()

    new_mom = MOMENTUM_DECAY * mom_ref[...] + rows_buf[...]
    new_master = master_ref[...] - LEARNING_RATE * new_mom
    mom_out[...] = new_mom
    master_out[...] = new_master


def _columns_kernel(x_ref, cols_out, send, recv, local_sem):
    n, rows, cols = cols_out.shape
    me = lax.axis_index("tp")
    barrier = pltpu.get_barrier_semaphore()
    for off in range(1, n):
        j = lax.rem(me + off, n)
        pl.semaphore_signal(barrier, inc=1, device_id=_peer(("tp", n, 1), j),
                            device_id_type=pl.DeviceIdType.MESH)
    pl.semaphore_wait(barrier, n - 1)

    def block(j):
        return x_ref.at[:, pl.ds(pl.multiple_of(j * cols, cols), cols)]

    copies = []
    for off in range(1, n):
        j = lax.rem(me + off, n)
        cp = pltpu.make_async_remote_copy(
            src_ref=block(j), dst_ref=cols_out.at[me],
            send_sem=send.at[j], recv_sem=recv.at[me],
            device_id=_peer(("tp", n, 1), j), device_id_type=pl.DeviceIdType.MESH)
        cp.start()
        copies.append((j, cp))
    own = pltpu.make_async_copy(block(me), cols_out.at[me], local_sem.at[0])
    own.start()
    own.wait()
    for j, cp in copies:
        pltpu.make_async_remote_copy(
            src_ref=block(j), dst_ref=cols_out.at[j],
            send_sem=send.at[j], recv_sem=recv.at[j],
            device_id=_peer(("tp", n, 1), j), device_id_type=pl.DeviceIdType.MESH).wait_recv()
    for j, cp in copies:
        cp.wait_send()


def by_columns(x, n, collective_id):
    rows, width = x.shape
    cols = width // n
    vmem = pl.BlockSpec(memory_space=pltpu.VMEM)
    return pl.pallas_call(
        _columns_kernel,
        out_shape=jax.ShapeDtypeStruct((n, rows, cols), x.dtype),
        in_specs=[vmem],
        out_specs=vmem,
        scratch_shapes=[
            pltpu.SemaphoreType.DMA((n,)),
            pltpu.SemaphoreType.DMA((n,)),
            pltpu.SemaphoreType.DMA((1,)),
        ],
        compiler_params=pltpu.CompilerParams(collective_id=collective_id, has_side_effects=True),
        cost_estimate=pl.CostEstimate(flops=0, bytes_accessed=2 * x.size * x.dtype.itemsize,
                                      transcendentals=0),
    )(x)


def flat_update(own_block, momentum, master, n, collective_id):
    block_rows, cols = own_block.shape
    rows = block_rows // n
    x = own_block.reshape(n, rows, cols)
    f32 = jnp.float32
    vmem = pl.BlockSpec(memory_space=pltpu.VMEM)
    return pl.pallas_call(
        _update_kernel,
        out_shape=(
            jax.ShapeDtypeStruct(momentum.shape, f32),
            jax.ShapeDtypeStruct(master.shape, f32),
        ),
        in_specs=[vmem, vmem, vmem],
        out_specs=(vmem, vmem),
        scratch_shapes=[
            pltpu.VMEM((rows, n * cols), f32),
            pltpu.SemaphoreType.DMA((n,)),
            pltpu.SemaphoreType.DMA((n,)),
            pltpu.SemaphoreType.DMA((1,)),
        ],
        compiler_params=pltpu.CompilerParams(collective_id=collective_id, has_side_effects=True),
        cost_estimate=pl.CostEstimate(flops=4 * momentum.size, bytes_accessed=5 * 4 * momentum.size,
                                      transcendentals=0),
    )(x, momentum, master)


def split_levels(name, size, inner):
    if size % inner or size == inner:
        return ((name, size, 1),)
    if inner == 2:
        return ((name, inner, 1), (name, size // inner, inner))
    return ((name, size // inner, inner), (name, inner, 1))


def orthonormal_by_gram(factor):
    hi = lax.Precision.HIGHEST
    gram_now = local_gram(factor)
    rank = factor.shape[1]
    eye = jnp.eye(rank, dtype=factor.dtype)
    sum_squares = jnp.trace(gram_now, axis1=1, axis2=2)[:, None, None]
    factor_scale = lax.rsqrt(sum_squares + NORM_EPSILON)
    gram_now = gram_now * (factor_scale * factor_scale)
    mixing = None
    for iteration in range(NS_STEPS):
        step = 1.5 * eye - 0.5 * gram_now
        mixing = step if mixing is None else jnp.einsum("krs,kst->krt", step, mixing, precision=hi)
        if iteration < NS_STEPS - 1:
            gram_now = jnp.einsum(
                "krs,kst,kut->kru", step, gram_now, step, precision=hi)
    return jnp.einsum("krs,ksd->krd", mixing * factor_scale, factor, precision=hi)


def local_gram(factor):
    return jnp.einsum("krd,ksd->krs", factor, factor, precision=lax.Precision.HIGHEST)


def orthonormal(factor, gram_of):
    gram_now = gram_of(factor)
    sum_squares = jnp.trace(gram_now, axis1=1, axis2=2)[:, None, None]
    factor_scale = lax.rsqrt(sum_squares + NORM_EPSILON)
    ortho_basis = factor * factor_scale
    gram_now = gram_now * (factor_scale * factor_scale)
    for iteration in range(NS_STEPS):
        if iteration > 0:
            gram_now = gram_of(ortho_basis)
        ortho_basis = 1.5 * ortho_basis - 0.5 * jnp.einsum(
            "krs,ksd->krd", gram_now, ortho_basis, precision=lax.Precision.HIGHEST
        )
    return ortho_basis


def local(grads, error, query, momentum, master):
    corrected = grads[0].astype(jnp.float32) + error[0]
    current = query
    replicas = lax.axis_size("rep")
    tensor = lax.axis_size("tp")
    kept = master - LEARNING_RATE * (MOMENTUM_DECAY * momentum)
    kept_cols = by_columns(kept, tensor, 3)
    kept_cols = kept_cols.reshape(-1, kept_cols.shape[-1])
    kept_all = lax.all_gather(kept_cols, "rep", axis=0, tiled=True)
    rep_only = (("rep", replicas, 1),)
    both = split_levels("tp", lax.axis_size("tp"), 2) + split_levels("rep", replicas, 4)
    for power_pass in range(ROUNDS):
        partial_factor = jnp.einsum(
            "kdf,krf->krd", corrected, current, precision=lax.Precision.HIGHEST
        )
        summed = allreduce(partial_factor, both, 0, direct=True)
        ortho_basis = orthonormal_by_gram(summed)
        partial_query = jnp.einsum(
            "kdf,krd->krf", corrected, ortho_basis, precision=lax.Precision.HIGHEST
        )
        current = allreduce(partial_query, rep_only, 1) / replicas
    approx = jnp.einsum("krd,krf->kdf", ortho_basis, current, precision=lax.Precision.HIGHEST)
    new_error = (corrected - approx)[None]
    matrices, model_width, shard_cols = approx.shape
    weights = (kept_all.reshape(approx.shape) - LEARNING_RATE * approx).astype(jnp.bfloat16)
    block_rows = matrices * model_width // replicas
    span = min(matrices, -(-block_rows // model_width) + 1)
    first_row = lax.axis_index("rep") * block_rows
    first_mat = jnp.minimum(first_row // model_width, matrices - span)
    pair = jnp.einsum(
        "krd,krf->kdf",
        lax.dynamic_slice_in_dim(ortho_basis, first_mat, span, 0),
        lax.dynamic_slice_in_dim(current, first_mat, span, 0),
        precision=lax.Precision.HIGHEST,
    ).reshape(span * model_width, shard_cols)
    own_block = lax.dynamic_slice_in_dim(
        pair, first_row - first_mat * model_width, block_rows, 0
    )
    new_momentum, new_master = flat_update(own_block, momentum, master, tensor, 2)
    return (new_error, current, new_momentum, new_master, weights)


def solution(mesh):
    placed = (
        P("rep", None, None, "tp"),
        P("rep", None, None, "tp"),
        P(None, None, "tp"),
        P(("rep", "tp"), None),
        P(("rep", "tp"), None),
    )
    return jax.shard_map(
        local,
        mesh=mesh,
        in_specs=placed,
        out_specs=(
            P("rep", None, None, "tp"),
            P(None, None, "tp"),
            P(("rep", "tp"), None),
            P(("rep", "tp"), None),
            P(None, None, "tp"),
        ),
        check_vma=False,
    )
```

```python
import functools

import jax
import jax.numpy as jnp
from jax import lax
from jax.experimental import pallas as pl
from jax.experimental.pallas import tpu as pltpu
from jax.sharding import PartitionSpec as P

ROUNDS = 2
NS_STEPS = 5


NORM_EPSILON = 1e-06
MOMENTUM_DECAY = 0.9
LEARNING_RATE = 0.5

MESH_AXES = ("rep", "tp")
LANES = 128


def _coord(level):
    name, n, stride = level
    return lax.rem(lax.div(lax.axis_index(name), stride), n)


def _peer(level, j):
    name, n, stride = level
    base = lax.axis_index(name) + (j - _coord(level)) * stride
    return tuple(base if axis == name else lax.axis_index(axis) for axis in MESH_AXES)


def _allreduce_kernel(levels, direct, x_ref, o_ref, *scratch):
    n_lev = len(levels)
    it = iter(scratch)
    recv = [next(it) for _ in range(n_lev)]
    sums = [next(it) for _ in range(n_lev - 1)]
    gath = [next(it) for _ in range(n_lev - 1)] + [None]
    rs_send = [next(it) for _ in range(n_lev)]
    rs_recv = [next(it) for _ in range(n_lev)]
    ag_send = [next(it) for _ in range(n_lev)]
    ag_recv = [next(it) for _ in range(n_lev)]
    local_sem = next(it)

    me = [_coord(level) for level in levels]

    barrier = pltpu.get_barrier_semaphore()
    total_peers = 0
    for lev, (name, n, _) in enumerate(levels):
        for off in range(1, n):
            j = lax.rem(me[lev] + off, n)
            pl.semaphore_signal(barrier, inc=1, device_id=_peer(levels[lev], j),
                                device_id_type=pl.DeviceIdType.MESH)
        total_peers += n - 1
    pl.semaphore_wait(barrier, total_peers)

    gath_bufs = [o_ref] + gath[: n_lev - 1]

    src = x_ref
    for lev, (name, n, _) in enumerate(levels):
        m = me[lev]
        last_direct = direct and lev == n_lev - 1

        def piece(j, src=src, last_direct=last_direct):
            return src if last_direct else src.at[j]

        copies = []
        for off in range(1, n):
            j = lax.rem(m + off, n)
            cp = pltpu.make_async_remote_copy(
                src_ref=piece(j), dst_ref=recv[lev].at[m],
                send_sem=rs_send[lev].at[off], recv_sem=rs_recv[lev].at[m],
                device_id=_peer(levels[lev], j), device_id_type=pl.DeviceIdType.MESH)
            cp.start()
            copies.append((j, off, cp))
        if last_direct:
            own = pltpu.make_async_copy(piece(m), recv[lev].at[m], local_sem.at[0])
            own.start()
            own.wait()
        for j, off, cp in copies:
            pltpu.make_async_remote_copy(
                src_ref=piece(j), dst_ref=recv[lev].at[j],
                send_sem=rs_send[lev].at[off], recv_sem=rs_recv[lev].at[j],
                device_id=_peer(levels[lev], j), device_id_type=pl.DeviceIdType.MESH).wait_recv()
        for j, off, cp in copies:
            cp.wait_send()
        r = recv[lev]
        if lev < n_lev - 1:
            dst = sums[lev]
        elif last_direct:
            dst = gath_bufs[lev]
        else:
            dst = gath_bufs[lev].at[m]
        if len(r.shape) > 3:
            lead = r.shape[1:-2]
            count = 1
            for d in lead:
                count *= d

            def body(i, carry, r=r, dst=dst, n=n, lead=lead, src=src, m=m, last_direct=last_direct):
                idx = []
                rest = i
                for d in reversed(lead):
                    idx.append(lax.rem(rest, d))
                    rest = lax.div(rest, d)
                idx = tuple(reversed(idx))
                if last_direct:
                    acc = r[(0,) + idx]
                    for j in range(1, n):
                        acc = acc + r[(j,) + idx]
                else:
                    acc = src[(m,) + idx]
                    for off in range(1, n):
                        acc = acc + r[(lax.rem(m + off, n),) + idx]
                dst[idx] = acc
                return carry
            lax.fori_loop(0, count, body, 0)
        elif last_direct:
            acc = r[0]
            for j in range(1, n):
                acc = acc + r[j]
            dst[...] = acc
        else:
            acc = src[m]
            for off in range(1, n):
                acc = acc + r[lax.rem(m + off, n)]
            dst[...] = acc
        if lev < n_lev - 1:
            src = sums[lev]

    for lev in reversed(range(n_lev - 1 if direct else n_lev)):
        name, n, _ = levels[lev]
        m = me[lev]
        buf = gath_bufs[lev]
        if lev == n_lev - 1:
            piece = buf.at[m]
        else:
            piece = gath_bufs[lev + 1]
            own = pltpu.make_async_copy(piece, buf.at[m], local_sem.at[0])
            own.start()
            own.wait()
        copies = []
        for off in range(1, n):
            j = lax.rem(m + off, n)
            cp = pltpu.make_async_remote_copy(
                src_ref=piece, dst_ref=buf.at[m],
                send_sem=ag_send[lev].at[off], recv_sem=ag_recv[lev].at[m],
                device_id=_peer(levels[lev], j), device_id_type=pl.DeviceIdType.MESH)
            cp.start()
            copies.append((j, off, cp))
        for j, off, cp in copies:
            pltpu.make_async_remote_copy(
                src_ref=piece, dst_ref=buf.at[j],
                send_sem=ag_send[lev].at[off], recv_sem=ag_recv[lev].at[j],
                device_id=_peer(levels[lev], j), device_id_type=pl.DeviceIdType.MESH).wait_recv()
        for j, off, cp in copies:
            cp.wait_send()


def allreduce(x, levels, collective_id, direct=False):
    shape = x.shape
    total = x.size
    counts = [n for _, n, _ in levels]
    per = total
    for n in counts:
        per //= n
    rows = per // LANES
    full = tuple(counts) + (rows, LANES)
    xr = x.reshape(full)
    scratch = []
    for lev in range(len(levels)):
        if direct and lev == len(levels) - 1:
            scratch.append(pltpu.VMEM((counts[lev],) + full[lev:], jnp.float32))
        else:
            scratch.append(pltpu.VMEM(full[lev:], jnp.float32))
    for lev in range(len(levels) - 1):
        scratch.append(pltpu.VMEM(full[lev + 1:], jnp.float32))
    for lev in range(len(levels) - 1):
        scratch.append(pltpu.VMEM(full[lev + 1:], jnp.float32))
    for _ in range(4):
        for _, n, _ in levels:
            scratch.append(pltpu.SemaphoreType.DMA((n,)))
    scratch.append(pltpu.SemaphoreType.DMA((1,)))
    out = pl.pallas_call(
        functools.partial(_allreduce_kernel, tuple(levels), direct),
        out_shape=jax.ShapeDtypeStruct(full, jnp.float32),
        in_specs=[pl.BlockSpec(memory_space=pltpu.VMEM)],
        out_specs=pl.BlockSpec(memory_space=pltpu.VMEM),
        scratch_shapes=scratch,
        compiler_params=pltpu.CompilerParams(collective_id=collective_id, has_side_effects=True),
        cost_estimate=pl.CostEstimate(flops=total * 2, bytes_accessed=total * 4 * 4, transcendentals=0),
    )(xr)
    return out.reshape(shape)


def _update_kernel(x_ref, mom_ref, master_ref, mom_out, master_out,
                   rows_buf, send1, recv1, local_sem):
    n, rows, cols = x_ref.shape
    me = lax.axis_index("tp")
    barrier = pltpu.get_barrier_semaphore()
    for off in range(1, n):
        j = lax.rem(me + off, n)
        pl.semaphore_signal(barrier, inc=1, device_id=_peer(("tp", n, 1), j),
                            device_id_type=pl.DeviceIdType.MESH)
    pl.semaphore_wait(barrier, n - 1)

    def to_rows(j, src):
        return pltpu.make_async_remote_copy(
            src_ref=src, dst_ref=rows_buf.at[:, pl.ds(pl.multiple_of(me * cols, cols), cols)],
            send_sem=send1.at[j], recv_sem=recv1.at[me],
            device_id=_peer(("tp", n, 1), j), device_id_type=pl.DeviceIdType.MESH)

    copies = []
    for off in range(1, n):
        j = lax.rem(me + off, n)
        cp = to_rows(j, x_ref.at[j])
        cp.start()
        copies.append((j, cp))
    own = pltpu.make_async_copy(
        x_ref.at[me], rows_buf.at[:, pl.ds(pl.multiple_of(me * cols, cols), cols)], local_sem.at[0])
    own.start()
    own.wait()
    for j, cp in copies:
        pltpu.make_async_remote_copy(
            src_ref=x_ref.at[j], dst_ref=rows_buf.at[:, pl.ds(pl.multiple_of(j * cols, cols), cols)],
            send_sem=send1.at[j], recv_sem=recv1.at[j],
            device_id=_peer(("tp", n, 1), j), device_id_type=pl.DeviceIdType.MESH).wait_recv()
    for j, cp in copies:
        cp.wait_send()

    new_mom = MOMENTUM_DECAY * mom_ref[...] + rows_buf[...]
    new_master = master_ref[...] - LEARNING_RATE * new_mom
    mom_out[...] = new_mom
    master_out[...] = new_master


def _columns_kernel(x_ref, cols_out, send, recv, local_sem):
    n, rows, cols = cols_out.shape
    me = lax.axis_index("tp")
    barrier = pltpu.get_barrier_semaphore()
    for off in range(1, n):
        j = lax.rem(me + off, n)
        pl.semaphore_signal(barrier, inc=1, device_id=_peer(("tp", n, 1), j),
                            device_id_type=pl.DeviceIdType.MESH)
    pl.semaphore_wait(barrier, n - 1)

    def block(j):
        return x_ref.at[:, pl.ds(pl.multiple_of(j * cols, cols), cols)]

    copies = []
    for off in range(1, n):
        j = lax.rem(me + off, n)
        cp = pltpu.make_async_remote_copy(
            src_ref=block(j), dst_ref=cols_out.at[me],
            send_sem=send.at[j], recv_sem=recv.at[me],
            device_id=_peer(("tp", n, 1), j), device_id_type=pl.DeviceIdType.MESH)
        cp.start()
        copies.append((j, cp))
    own = pltpu.make_async_copy(block(me), cols_out.at[me], local_sem.at[0])
    own.start()
    own.wait()
    for j, cp in copies:
        pltpu.make_async_remote_copy(
            src_ref=block(j), dst_ref=cols_out.at[j],
            send_sem=send.at[j], recv_sem=recv.at[j],
            device_id=_peer(("tp", n, 1), j), device_id_type=pl.DeviceIdType.MESH).wait_recv()
    for j, cp in copies:
        cp.wait_send()


def by_columns(x, n, collective_id):
    rows, width = x.shape
    cols = width // n
    vmem = pl.BlockSpec(memory_space=pltpu.VMEM)
    return pl.pallas_call(
        _columns_kernel,
        out_shape=jax.ShapeDtypeStruct((n, rows, cols), x.dtype),
        in_specs=[vmem],
        out_specs=vmem,
        scratch_shapes=[
            pltpu.SemaphoreType.DMA((n,)),
            pltpu.SemaphoreType.DMA((n,)),
            pltpu.SemaphoreType.DMA((1,)),
        ],
        compiler_params=pltpu.CompilerParams(collective_id=collective_id, has_side_effects=True),
        cost_estimate=pl.CostEstimate(flops=0, bytes_accessed=2 * x.size * x.dtype.itemsize,
                                      transcendentals=0),
    )(x)


def flat_update(own_block, momentum, master, n, collective_id):
    block_rows, cols = own_block.shape
    rows = block_rows // n
    x = own_block.reshape(n, rows, cols)
    f32 = jnp.float32
    vmem = pl.BlockSpec(memory_space=pltpu.VMEM)
    return pl.pallas_call(
        _update_kernel,
        out_shape=(
            jax.ShapeDtypeStruct(momentum.shape, f32),
            jax.ShapeDtypeStruct(master.shape, f32),
        ),
        in_specs=[vmem, vmem, vmem],
        out_specs=(vmem, vmem),
        scratch_shapes=[
            pltpu.VMEM((rows, n * cols), f32),
            pltpu.SemaphoreType.DMA((n,)),
            pltpu.SemaphoreType.DMA((n,)),
            pltpu.SemaphoreType.DMA((1,)),
        ],
        compiler_params=pltpu.CompilerParams(collective_id=collective_id, has_side_effects=True),
        cost_estimate=pl.CostEstimate(flops=4 * momentum.size, bytes_accessed=5 * 4 * momentum.size,
                                      transcendentals=0),
    )(x, momentum, master)


def split_levels(name, size, inner):
    if size % inner or size == inner:
        return ((name, size, 1),)
    if inner == 2:
        return ((name, inner, 1), (name, size // inner, inner))
    return ((name, size // inner, inner), (name, inner, 1))


def orthonormal_by_gram(factor):
    hi = lax.Precision.HIGHEST
    gram_now = local_gram(factor)
    rank = factor.shape[1]
    eye = jnp.eye(rank, dtype=factor.dtype)
    sum_squares = jnp.trace(gram_now, axis1=1, axis2=2)[:, None, None]
    factor_scale = lax.rsqrt(sum_squares + NORM_EPSILON)
    gram_now = gram_now * (factor_scale * factor_scale)
    mixing = None
    for iteration in range(NS_STEPS):
        step = 1.5 * eye - 0.5 * gram_now
        mixing = step if mixing is None else jnp.einsum("krs,kst->krt", step, mixing, precision=hi)
        if iteration < NS_STEPS - 1:
            gram_now = jnp.einsum(
                "krs,kst,kut->kru", step, gram_now, step, precision=hi)
    return jnp.einsum("krs,ksd->krd", mixing * factor_scale, factor, precision=hi)


def local_gram(factor):
    return jnp.einsum("krd,ksd->krs", factor, factor, precision=lax.Precision.HIGHEST)


def orthonormal(factor, gram_of):
    gram_now = gram_of(factor)
    sum_squares = jnp.trace(gram_now, axis1=1, axis2=2)[:, None, None]
    factor_scale = lax.rsqrt(sum_squares + NORM_EPSILON)
    ortho_basis = factor * factor_scale
    gram_now = gram_now * (factor_scale * factor_scale)
    for iteration in range(NS_STEPS):
        if iteration > 0:
            gram_now = gram_of(ortho_basis)
        ortho_basis = 1.5 * ortho_basis - 0.5 * jnp.einsum(
            "krs,ksd->krd", gram_now, ortho_basis, precision=lax.Precision.HIGHEST
        )
    return ortho_basis


def local(grads, error, query, momentum, master):
    corrected = grads[0].astype(jnp.float32) + error[0]
    current = query
    replicas = lax.axis_size("rep")
    tensor = lax.axis_size("tp")
    kept = master - LEARNING_RATE * (MOMENTUM_DECAY * momentum)
    kept_cols = by_columns(kept, tensor, 3)
    kept_cols = kept_cols.reshape(-1, kept_cols.shape[-1])
    kept_all = lax.all_gather(kept_cols, "rep", axis=0, tiled=True)
    rep_only = (("rep", replicas, 1),)
    both = split_levels("tp", lax.axis_size("tp"), 2) + split_levels("rep", replicas, 4)[::-1]
    for power_pass in range(ROUNDS):
        partial_factor = jnp.einsum(
            "kdf,krf->krd", corrected, current, precision=lax.Precision.HIGHEST
        )
        summed = allreduce(partial_factor, both, 0, direct=True)
        ortho_basis = orthonormal_by_gram(summed)
        partial_query = jnp.einsum(
            "kdf,krd->krf", corrected, ortho_basis, precision=lax.Precision.HIGHEST
        )
        current = allreduce(partial_query, rep_only, 1) / replicas
    approx = jnp.einsum("krd,krf->kdf", ortho_basis, current, precision=lax.Precision.HIGHEST)
    new_error = (corrected - approx)[None]
    matrices, model_width, shard_cols = approx.shape
    weights = (kept_all.reshape(approx.shape) - LEARNING_RATE * approx).astype(jnp.bfloat16)
    block_rows = matrices * model_width // replicas
    span = min(matrices, -(-block_rows // model_width) + 1)
    first_row = lax.axis_index("rep") * block_rows
    first_mat = jnp.minimum(first_row // model_width, matrices - span)
    pair = jnp.einsum(
        "krd,krf->kdf",
        lax.dynamic_slice_in_dim(ortho_basis, first_mat, span, 0),
        lax.dynamic_slice_in_dim(current, first_mat, span, 0),
        precision=lax.Precision.HIGHEST,
    ).reshape(span * model_width, shard_cols)
    own_block = lax.dynamic_slice_in_dim(
        pair, first_row - first_mat * model_width, block_rows, 0
    )
    new_momentum, new_master = flat_update(own_block, momentum, master, tensor, 2)
    return (new_error, current, new_momentum, new_master, weights)


def solution(mesh):
    placed = (
        P("rep", None, None, "tp"),
        P("rep", None, None, "tp"),
        P(None, None, "tp"),
        P(("rep", "tp"), None),
        P(("rep", "tp"), None),
    )
    return jax.shard_map(
        local,
        mesh=mesh,
        in_specs=placed,
        out_specs=(
            P("rep", None, None, "tp"),
            P(None, None, "tp"),
            P(("rep", "tp"), None),
            P(("rep", "tp"), None),
            P(None, None, "tp"),
        ),
        check_vma=False,
    )
```

```python
import functools

import jax
import jax.numpy as jnp
from jax import lax
from jax.experimental import pallas as pl
from jax.experimental.pallas import tpu as pltpu
from jax.sharding import PartitionSpec as P

ROUNDS = 2
NS_STEPS = 5


NORM_EPSILON = 1e-06
MOMENTUM_DECAY = 0.9
LEARNING_RATE = 0.5

MESH_AXES = ("rep", "tp")
LANES = 128


def _coord(level):
    name, n, stride = level
    return lax.rem(lax.div(lax.axis_index(name), stride), n)


def _peer(level, j):
    name, n, stride = level
    base = lax.axis_index(name) + (j - _coord(level)) * stride
    return tuple(base if axis == name else lax.axis_index(axis) for axis in MESH_AXES)


def _allreduce_kernel(levels, direct, x_ref, o_ref, *scratch):
    n_lev = len(levels)
    it = iter(scratch)
    recv = [next(it) for _ in range(n_lev)]
    sums = [next(it) for _ in range(n_lev - 1)]
    gath = [next(it) for _ in range(n_lev - 1)] + [None]
    rs_send = [next(it) for _ in range(n_lev)]
    rs_recv = [next(it) for _ in range(n_lev)]
    ag_send = [next(it) for _ in range(n_lev)]
    ag_recv = [next(it) for _ in range(n_lev)]
    local_sem = next(it)

    me = [_coord(level) for level in levels]

    barrier = pltpu.get_barrier_semaphore()
    total_peers = 0
    for lev, (name, n, _) in enumerate(levels):
        for off in range(1, n):
            j = lax.rem(me[lev] + off, n)
            pl.semaphore_signal(barrier, inc=1, device_id=_peer(levels[lev], j),
                                device_id_type=pl.DeviceIdType.MESH)
        total_peers += n - 1
    pl.semaphore_wait(barrier, total_peers)

    gath_bufs = [o_ref] + gath[: n_lev - 1]

    src = x_ref
    for lev, (name, n, _) in enumerate(levels):
        m = me[lev]
        last_direct = direct and lev == n_lev - 1

        def piece(j, src=src, last_direct=last_direct):
            return src if last_direct else src.at[j]

        copies = []
        for off in range(1, n):
            j = lax.rem(m + off, n)
            cp = pltpu.make_async_remote_copy(
                src_ref=piece(j), dst_ref=recv[lev].at[m],
                send_sem=rs_send[lev].at[off], recv_sem=rs_recv[lev].at[m],
                device_id=_peer(levels[lev], j), device_id_type=pl.DeviceIdType.MESH)
            cp.start()
            copies.append((j, off, cp))
        if last_direct:
            own = pltpu.make_async_copy(piece(m), recv[lev].at[m], local_sem.at[0])
            own.start()
            own.wait()
        for j, off, cp in copies:
            pltpu.make_async_remote_copy(
                src_ref=piece(j), dst_ref=recv[lev].at[j],
                send_sem=rs_send[lev].at[off], recv_sem=rs_recv[lev].at[j],
                device_id=_peer(levels[lev], j), device_id_type=pl.DeviceIdType.MESH).wait_recv()
        for j, off, cp in copies:
            cp.wait_send()
        r = recv[lev]
        if lev < n_lev - 1:
            dst = sums[lev]
        elif last_direct:
            dst = gath_bufs[lev]
        else:
            dst = gath_bufs[lev].at[m]
        if len(r.shape) > 3:
            lead = r.shape[1:-2]
            count = 1
            for d in lead:
                count *= d

            def body(i, carry, r=r, dst=dst, n=n, lead=lead, src=src, m=m, last_direct=last_direct):
                idx = []
                rest = i
                for d in reversed(lead):
                    idx.append(lax.rem(rest, d))
                    rest = lax.div(rest, d)
                idx = tuple(reversed(idx))
                if last_direct:
                    acc = r[(0,) + idx]
                    for j in range(1, n):
                        acc = acc + r[(j,) + idx]
                else:
                    acc = src[(m,) + idx]
                    for off in range(1, n):
                        acc = acc + r[(lax.rem(m + off, n),) + idx]
                dst[idx] = acc
                return carry
            lax.fori_loop(0, count, body, 0)
        elif last_direct:
            acc = r[0]
            for j in range(1, n):
                acc = acc + r[j]
            dst[...] = acc
        else:
            acc = src[m]
            for off in range(1, n):
                acc = acc + r[lax.rem(m + off, n)]
            dst[...] = acc
        if lev < n_lev - 1:
            src = sums[lev]

    for lev in reversed(range(n_lev - 1 if direct else n_lev)):
        name, n, _ = levels[lev]
        m = me[lev]
        buf = gath_bufs[lev]
        piece = buf.at[m] if lev == n_lev - 1 else gath_bufs[lev + 1]
        copies = []
        for off in range(1, n):
            j = lax.rem(m + off, n)
            cp = pltpu.make_async_remote_copy(
                src_ref=piece, dst_ref=buf.at[m],
                send_sem=ag_send[lev].at[off], recv_sem=ag_recv[lev].at[m],
                device_id=_peer(levels[lev], j), device_id_type=pl.DeviceIdType.MESH)
            cp.start()
            copies.append((j, off, cp))
        if lev < n_lev - 1:
            own = pltpu.make_async_copy(piece, buf.at[m], local_sem.at[0])
            own.start()
            own.wait()
        for j, off, cp in copies:
            pltpu.make_async_remote_copy(
                src_ref=piece, dst_ref=buf.at[j],
                send_sem=ag_send[lev].at[off], recv_sem=ag_recv[lev].at[j],
                device_id=_peer(levels[lev], j), device_id_type=pl.DeviceIdType.MESH).wait_recv()
        for j, off, cp in copies:
            cp.wait_send()


def allreduce(x, levels, collective_id, direct=False):
    shape = x.shape
    total = x.size
    counts = [n for _, n, _ in levels]
    per = total
    for n in counts:
        per //= n
    rows = per // LANES
    full = tuple(counts) + (rows, LANES)
    xr = x.reshape(full)
    scratch = []
    for lev in range(len(levels)):
        if direct and lev == len(levels) - 1:
            scratch.append(pltpu.VMEM((counts[lev],) + full[lev:], jnp.float32))
        else:
            scratch.append(pltpu.VMEM(full[lev:], jnp.float32))
    for lev in range(len(levels) - 1):
        scratch.append(pltpu.VMEM(full[lev + 1:], jnp.float32))
    for lev in range(len(levels) - 1):
        scratch.append(pltpu.VMEM(full[lev + 1:], jnp.float32))
    for _ in range(4):
        for _, n, _ in levels:
            scratch.append(pltpu.SemaphoreType.DMA((n,)))
    scratch.append(pltpu.SemaphoreType.DMA((1,)))
    out = pl.pallas_call(
        functools.partial(_allreduce_kernel, tuple(levels), direct),
        out_shape=jax.ShapeDtypeStruct(full, jnp.float32),
        in_specs=[pl.BlockSpec(memory_space=pltpu.VMEM)],
        out_specs=pl.BlockSpec(memory_space=pltpu.VMEM),
        scratch_shapes=scratch,
        compiler_params=pltpu.CompilerParams(collective_id=collective_id, has_side_effects=True),
        cost_estimate=pl.CostEstimate(flops=total * 2, bytes_accessed=total * 4 * 4, transcendentals=0),
    )(xr)
    return out.reshape(shape)


def _update_kernel(x_ref, mom_ref, master_ref, mom_out, master_out,
                   rows_buf, send1, recv1, local_sem):
    n, rows, cols = x_ref.shape
    me = lax.axis_index("tp")
    barrier = pltpu.get_barrier_semaphore()
    for off in range(1, n):
        j = lax.rem(me + off, n)
        pl.semaphore_signal(barrier, inc=1, device_id=_peer(("tp", n, 1), j),
                            device_id_type=pl.DeviceIdType.MESH)
    pl.semaphore_wait(barrier, n - 1)

    def to_rows(j, src):
        return pltpu.make_async_remote_copy(
            src_ref=src, dst_ref=rows_buf.at[:, pl.ds(pl.multiple_of(me * cols, cols), cols)],
            send_sem=send1.at[j], recv_sem=recv1.at[me],
            device_id=_peer(("tp", n, 1), j), device_id_type=pl.DeviceIdType.MESH)

    copies = []
    for off in range(1, n):
        j = lax.rem(me + off, n)
        cp = to_rows(j, x_ref.at[j])
        cp.start()
        copies.append((j, cp))
    own = pltpu.make_async_copy(
        x_ref.at[me], rows_buf.at[:, pl.ds(pl.multiple_of(me * cols, cols), cols)], local_sem.at[0])
    own.start()
    own.wait()
    for j, cp in copies:
        pltpu.make_async_remote_copy(
            src_ref=x_ref.at[j], dst_ref=rows_buf.at[:, pl.ds(pl.multiple_of(j * cols, cols), cols)],
            send_sem=send1.at[j], recv_sem=recv1.at[j],
            device_id=_peer(("tp", n, 1), j), device_id_type=pl.DeviceIdType.MESH).wait_recv()
    for j, cp in copies:
        cp.wait_send()

    new_mom = MOMENTUM_DECAY * mom_ref[...] + rows_buf[...]
    new_master = master_ref[...] - LEARNING_RATE * new_mom
    mom_out[...] = new_mom
    master_out[...] = new_master


def _columns_kernel(x_ref, cols_out, send, recv, local_sem):
    n, rows, cols = cols_out.shape
    me = lax.axis_index("tp")
    barrier = pltpu.get_barrier_semaphore()
    for off in range(1, n):
        j = lax.rem(me + off, n)
        pl.semaphore_signal(barrier, inc=1, device_id=_peer(("tp", n, 1), j),
                            device_id_type=pl.DeviceIdType.MESH)
    pl.semaphore_wait(barrier, n - 1)

    def block(j):
        return x_ref.at[:, pl.ds(pl.multiple_of(j * cols, cols), cols)]

    copies = []
    for off in range(1, n):
        j = lax.rem(me + off, n)
        cp = pltpu.make_async_remote_copy(
            src_ref=block(j), dst_ref=cols_out.at[me],
            send_sem=send.at[j], recv_sem=recv.at[me],
            device_id=_peer(("tp", n, 1), j), device_id_type=pl.DeviceIdType.MESH)
        cp.start()
        copies.append((j, cp))
    own = pltpu.make_async_copy(block(me), cols_out.at[me], local_sem.at[0])
    own.start()
    own.wait()
    for j, cp in copies:
        pltpu.make_async_remote_copy(
            src_ref=block(j), dst_ref=cols_out.at[j],
            send_sem=send.at[j], recv_sem=recv.at[j],
            device_id=_peer(("tp", n, 1), j), device_id_type=pl.DeviceIdType.MESH).wait_recv()
    for j, cp in copies:
        cp.wait_send()


def by_columns(x, n, collective_id):
    rows, width = x.shape
    cols = width // n
    vmem = pl.BlockSpec(memory_space=pltpu.VMEM)
    return pl.pallas_call(
        _columns_kernel,
        out_shape=jax.ShapeDtypeStruct((n, rows, cols), x.dtype),
        in_specs=[vmem],
        out_specs=vmem,
        scratch_shapes=[
            pltpu.SemaphoreType.DMA((n,)),
            pltpu.SemaphoreType.DMA((n,)),
            pltpu.SemaphoreType.DMA((1,)),
        ],
        compiler_params=pltpu.CompilerParams(collective_id=collective_id, has_side_effects=True),
        cost_estimate=pl.CostEstimate(flops=0, bytes_accessed=2 * x.size * x.dtype.itemsize,
                                      transcendentals=0),
    )(x)


def flat_update(own_block, momentum, master, n, collective_id):
    block_rows, cols = own_block.shape
    rows = block_rows // n
    x = own_block.reshape(n, rows, cols)
    f32 = jnp.float32
    vmem = pl.BlockSpec(memory_space=pltpu.VMEM)
    return pl.pallas_call(
        _update_kernel,
        out_shape=(
            jax.ShapeDtypeStruct(momentum.shape, f32),
            jax.ShapeDtypeStruct(master.shape, f32),
        ),
        in_specs=[vmem, vmem, vmem],
        out_specs=(vmem, vmem),
        scratch_shapes=[
            pltpu.VMEM((rows, n * cols), f32),
            pltpu.SemaphoreType.DMA((n,)),
            pltpu.SemaphoreType.DMA((n,)),
            pltpu.SemaphoreType.DMA((1,)),
        ],
        compiler_params=pltpu.CompilerParams(collective_id=collective_id, has_side_effects=True),
        cost_estimate=pl.CostEstimate(flops=4 * momentum.size, bytes_accessed=5 * 4 * momentum.size,
                                      transcendentals=0),
    )(x, momentum, master)


def split_levels(name, size, inner):
    if size % inner or size == inner:
        return ((name, size, 1),)
    if inner == 2:
        return ((name, inner, 1), (name, size // inner, inner))
    return ((name, size // inner, inner), (name, inner, 1))


def orthonormal_by_gram(factor):
    hi = lax.Precision.HIGHEST
    gram_now = local_gram(factor)
    rank = factor.shape[1]
    eye = jnp.eye(rank, dtype=factor.dtype)
    sum_squares = jnp.trace(gram_now, axis1=1, axis2=2)[:, None, None]
    factor_scale = lax.rsqrt(sum_squares + NORM_EPSILON)
    gram_now = gram_now * (factor_scale * factor_scale)
    mixing = None
    for iteration in range(NS_STEPS):
        step = 1.5 * eye - 0.5 * gram_now
        mixing = step if mixing is None else jnp.einsum("krs,kst->krt", step, mixing, precision=hi)
        if iteration < NS_STEPS - 1:
            gram_now = jnp.einsum(
                "krs,kst,kut->kru", step, gram_now, step, precision=hi)
    return jnp.einsum("krs,ksd->krd", mixing * factor_scale, factor, precision=hi)


def local_gram(factor):
    return jnp.einsum("krd,ksd->krs", factor, factor, precision=lax.Precision.HIGHEST)


def orthonormal(factor, gram_of):
    gram_now = gram_of(factor)
    sum_squares = jnp.trace(gram_now, axis1=1, axis2=2)[:, None, None]
    factor_scale = lax.rsqrt(sum_squares + NORM_EPSILON)
    ortho_basis = factor * factor_scale
    gram_now = gram_now * (factor_scale * factor_scale)
    for iteration in range(NS_STEPS):
        if iteration > 0:
            gram_now = gram_of(ortho_basis)
        ortho_basis = 1.5 * ortho_basis - 0.5 * jnp.einsum(
            "krs,ksd->krd", gram_now, ortho_basis, precision=lax.Precision.HIGHEST
        )
    return ortho_basis


def local(grads, error, query, momentum, master):
    corrected = grads[0].astype(jnp.float32) + error[0]
    current = query
    replicas = lax.axis_size("rep")
    tensor = lax.axis_size("tp")
    kept = master - LEARNING_RATE * (MOMENTUM_DECAY * momentum)
    kept_cols = by_columns(kept, tensor, 3)
    kept_cols = kept_cols.reshape(-1, kept_cols.shape[-1])
    kept_all = lax.all_gather(kept_cols, "rep", axis=0, tiled=True)
    rep_only = (("rep", replicas, 1),)
    both = split_levels("tp", lax.axis_size("tp"), 2) + split_levels("rep", replicas, 4)
    for power_pass in range(ROUNDS):
        partial_factor = jnp.einsum(
            "kdf,krf->krd", corrected, current, precision=lax.Precision.HIGHEST
        )
        summed = allreduce(partial_factor, both, 0, direct=True)
        ortho_basis = orthonormal_by_gram(summed)
        partial_query = jnp.einsum(
            "kdf,krd->krf", corrected, ortho_basis, precision=lax.Precision.HIGHEST
        )
        current = allreduce(partial_query, rep_only, 1) / replicas
    approx = jnp.einsum("krd,krf->kdf", ortho_basis, current, precision=lax.Precision.HIGHEST)
    new_error = (corrected - approx)[None]
    matrices, model_width, shard_cols = approx.shape
    weights = (kept_all.reshape(approx.shape) - LEARNING_RATE * approx).astype(jnp.bfloat16)
    block_rows = matrices * model_width // replicas
    span = min(matrices, -(-block_rows // model_width) + 1)
    first_row = lax.axis_index("rep") * block_rows
    first_mat = jnp.minimum(first_row // model_width, matrices - span)
    pair = jnp.einsum(
        "krd,krf->kdf",
        lax.dynamic_slice_in_dim(ortho_basis, first_mat, span, 0),
        lax.dynamic_slice_in_dim(current, first_mat, span, 0),
        precision=lax.Precision.HIGHEST,
    ).reshape(span * model_width, shard_cols)
    own_block = lax.dynamic_slice_in_dim(
        pair, first_row - first_mat * model_width, block_rows, 0
    )
    new_momentum, new_master = flat_update(own_block, momentum, master, tensor, 2)
    return (new_error, current, new_momentum, new_master, weights)


def solution(mesh):
    placed = (
        P("rep", None, None, "tp"),
        P("rep", None, None, "tp"),
        P(None, None, "tp"),
        P(("rep", "tp"), None),
        P(("rep", "tp"), None),
    )
    return jax.shard_map(
        local,
        mesh=mesh,
        in_specs=placed,
        out_specs=(
            P("rep", None, None, "tp"),
            P(None, None, "tp"),
            P(("rep", "tp"), None),
            P(("rep", "tp"), None),
            P(None, None, "tp"),
        ),
        check_vma=False,
    )
```
